32 devices in a mesh: ctx: 16 (over z, y, x), tp: 2 (over core).
Axes of the slice: x: 2, y: 2, z: 4, core: 2. Of those that a mesh axis runs over, the one named last changes fastest.
Arguments:
- queries: bfloat16 [4096, 2048], P('tp', 'ctx'), may hold values from -6 to 6
- keys_in: bfloat16 [4096, 2048], P('tp', 'ctx'), may hold values from -6 to 6
- values_in: bfloat16 [4096, 2048], P('tp', 'ctx'), may hold values from -6 to 6
- grad_out: bfloat16 [4096, 2048], P('tp', 'ctx'), may hold values from -6 to 6
- residue: float32 [64, 16], replicated, may hold values from -0.07 to 0.07
- decay_rate: float32 [64, 16], replicated, may hold values from 9.765625e-05 to 0.0333333333
Outputs:
- grad_queries: bfloat16 [4096, 2048], P('tp', 'ctx')
- grad_keys: bfloat16 [4096, 2048], P('tp', 'ctx')
- grad_values: bfloat16 [4096, 2048], P('tp', 'ctx')
- grad_residue: float32 [64, 16], replicated
- grad_decay: float32 [64, 16], replicated
The draws below stay inside these ranges and needn't reach their ends.
All inputs are finite; a program needn't handle non-finite values.
Results may differ from the reference program's by a relative error of at most 0.0085.
Values may be sent and summed in bfloat16 or wider, within the bound.
No kernel may reach another device: no remote copies, remote signals or barrier semaphores. Data moves between devices by JAX's collectives and lax.ppermute only.
A program may use at most 128 MiB of HBM per device.

```python
import math
import jax
import jax.numpy as jnp
from jax import lax

D = 4096
GROUPS = 64
MODES = 16
TOKENS = 2048


def decay_values(key):
    base = jax.random.fold_in(key, 11)
    first, second, third = jax.random.split(base, 3)
    slower = jax.random.uniform(first, (GROUPS, MODES), jnp.float32, 0.2, 2.0) / TOKENS
    quicker = jax.random.uniform(second, (GROUPS, MODES), jnp.float32, 1.0 / 50.0, 1.0 / 30.0)
    share = 0.5
    chosen = jax.random.uniform(third, (GROUPS, MODES), jnp.float32) < share
    return jnp.where(chosen, slower, quicker)


def draw_decay_rate(key, part):
    return decay_values(key)


def draw_residue(key, part):
    rates = decay_values(key)
    spread_key = jax.random.fold_in(key, 23)
    spread = jax.random.uniform(spread_key, (GROUPS, MODES), jnp.float32, -1.0, 1.0)
    return spread * jnp.sqrt(1.0 - jnp.exp(-2.0 * rates)) / math.sqrt(MODES)


def steps_of(stream_key, dims, cuts, smallest, high):
    def one(dim, parts):
        steps = jax.random.uniform(jax.random.fold_in(jax.random.fold_in(stream_key, 6), dim), (parts,), jnp.float32, smallest / len(cuts), high / len(cuts))
        return jnp.repeat(jnp.exp(steps), dims[dim] // parts).reshape((-1,) + (1,) * (len(dims) - dim - 1))

    level = one(*cuts[0])
    for cut in cuts[1:]:
        level = level * one(*cut)
    return level


def scatter_about(own_key, extent, scale, bound, cuts=(), held_as=jnp.bfloat16):
    loudness = steps_of(own_key, extent, cuts, -0.22, 0.18) if cuts else 1.0
    array = jax.random.normal(own_key, extent, jnp.float32) * scale * loudness
    return jnp.minimum(jnp.maximum(array, -bound), bound).astype(held_as)


def setup_inputs(seed: int = 0) -> dict:
    splits = jax.random.split(jax.random.key(seed), 7)
    queries = scatter_about(splits[0], (D, TOKENS), 1.0, 6.0, ((0, 2), (1, 16)))
    keys_in = scatter_about(splits[1], (D, TOKENS), 1.0, 6.0, ((0, 2), (1, 16)))
    values_in = scatter_about(splits[2], (D, TOKENS), 1.0, 6.0, ((0, 2), (1, 16)))
    grad_out = scatter_about(splits[3], (D, TOKENS), 1.0, 6.0, ((0, 2), (1, 16)))
    residue = draw_residue(jax.random.fold_in(splits[6], 71), 0)
    decay_rate = draw_decay_rate(jax.random.fold_in(splits[6], 71), 0)
    return {"queries": queries, "keys_in": keys_in, "values_in": values_in, "grad_out": grad_out, "residue": residue, "decay_rate": decay_rate}


def reference(queries, keys_in, values_in, grad_out, residue, decay_rate):
    block = min(256, D)
    count = D // block
    highest = lax.Precision.HIGHEST
    positions = jnp.arange(TOKENS).astype(jnp.float32)
    length_fft = 2 * TOKENS

    def one_block(packed):
        index, query_b, key_b, value_b, grad_b = packed
        channel_ids = index * block + jnp.arange(block, dtype=jnp.int32)
        onehot = ((channel_ids % GROUPS)[:, None] == jnp.arange(GROUPS, dtype=jnp.int32)[None, :]).astype(jnp.float32)
        res_chan = jnp.dot(onehot, residue, precision=highest)
        dec_chan = jnp.dot(onehot, decay_rate, precision=highest)
        basis = jnp.exp(-dec_chan[:, :, None] * positions[None, None, :])
        filt = jnp.einsum("cm,cmt->ct", res_chan, basis, precision=highest)
        gated = (key_b.astype(jnp.float32) * value_b.astype(jnp.float32)).astype(jnp.bfloat16)
        conv_grad = (grad_b.astype(jnp.float32) * query_b.astype(jnp.float32)).astype(jnp.bfloat16)
        spec_gated = jnp.fft.rfft(gated.astype(jnp.float32), n=length_fft, axis=1)
        spec_filt = jnp.fft.rfft(filt, n=length_fft, axis=1)
        spec_cot = jnp.fft.rfft(conv_grad.astype(jnp.float32), n=length_fft, axis=1)
        conv = jnp.fft.irfft(spec_gated * spec_filt, n=length_fft, axis=1)[:, :TOKENS].astype(jnp.bfloat16)
        input_grad = jnp.fft.irfft(jnp.conj(spec_filt) * spec_cot, n=length_fft, axis=1)[:, :TOKENS].astype(jnp.bfloat16)
        filter_grad = jnp.fft.irfft(jnp.conj(spec_gated) * spec_cot, n=length_fft, axis=1)[:, :TOKENS]
        grad_q = (grad_b.astype(jnp.float32) * conv.astype(jnp.float32)).astype(jnp.bfloat16)
        grad_k = (input_grad.astype(jnp.float32) * value_b.astype(jnp.float32)).astype(jnp.bfloat16)
        grad_v = (input_grad.astype(jnp.float32) * key_b.astype(jnp.float32)).astype(jnp.bfloat16)
        res_terms = jnp.einsum("ct,cmt->cm", filter_grad, basis, precision=highest)
        dec_terms = -res_chan * dec_chan * jnp.einsum("ct,cmt->cm", filter_grad * positions[None, :], basis, precision=highest)
        return (grad_q, grad_k, grad_v,
                jnp.dot(onehot.T, res_terms, precision=highest),
                jnp.dot(onehot.T, dec_terms, precision=highest))

    packed = (jnp.arange(count, dtype=jnp.int32),
              queries.reshape(count, block, TOKENS), keys_in.reshape(count, block, TOKENS),
              values_in.reshape(count, block, TOKENS), grad_out.reshape(count, block, TOKENS))
    grad_q, grad_k, grad_v, res_sum, dec_sum = lax.map(one_block, packed)
    return (grad_q.reshape(D, TOKENS), grad_k.reshape(D, TOKENS), grad_v.reshape(D, TOKENS),
            jnp.sum(res_sum, axis=0) / TOKENS, jnp.sum(dec_sum, axis=0) / TOKENS)
```

```python
import functools
import math

import jax
import jax.numpy as jnp
from jax import lax
from jax.experimental import pallas as pl
from jax.experimental.pallas import tpu as pltpu
from jax.sharding import PartitionSpec as P

F32 = jnp.float32
BF16 = jnp.bfloat16
PLANE = 4
NT = (((1,), (1,)), ((), ()))
NN = (((1,), (0,)), ((), ()))
TN = (((0,), (0,)), ((), ()))


def dot(a, b, dims):
    return lax.dot_general(a, b, dims, preferred_element_type=F32)


def product(a, b):
    return (a.astype(F32) * b.astype(F32)).astype(BF16)


def column(block, row):
    modes = block.shape[1]
    eye = lax.broadcasted_iota(jnp.int32, (modes, modes), 0) == lax.broadcasted_iota(
        jnp.int32, (modes, modes), 1
    )
    wide = jnp.broadcast_to(block[row : row + 1, :], (modes, modes))
    return jnp.sum(jnp.where(eye, wide, 0.0), axis=1, keepdims=True)


def lane_iota(shape):
    return lax.broadcasted_iota(jnp.int32, shape, len(shape) - 1)


def states_kernel(place, k_ref, v_ref, g_ref, q_ref, dec_ref, gx_ref, cx_ref, *rest):
    outs, gs, cs = rest[:PLANE], rest[PLANE], rest[PLANE + 1]
    step = pl.program_id(0)
    rows, groups, length = k_ref.shape
    modes = dec_ref.shape[1]
    flat = rows * groups
    gs[...] = product(k_ref[...], v_ref[...]).astype(F32).reshape(flat, length)
    cs[...] = product(g_ref[...], q_ref[...]).astype(F32).reshape(flat, length)
    dec = dec_ref[...]
    ahead = lane_iota((modes, length)).astype(F32)
    behind = float(length) - ahead
    zero = jnp.zeros((modes, length), BF16)
    results = []
    for pair in range(groups // 2):
        left, right = [], []
        for side in range(2):
            group = 2 * pair + side
            rate = column(dec, group)
            fwd = jnp.exp(-rate * behind)
            bwd = jnp.exp(-rate * ahead)
            x = gs[pl.ds(group, rows, stride=groups), :].astype(BF16)
            c = cs[pl.ds(group, rows, stride=groups), :].astype(BF16)
            gx_ref[group] = x
            cx_ref[group] = c
            wx = [zero] * 8
            wx[side] = fwd.astype(BF16)
            wx[4 + side] = (behind * fwd).astype(BF16)
            wc = [zero] * 8
            wc[2 + side] = bwd.astype(BF16)
            wc[6 + side] = (ahead * bwd).astype(BF16)
            left += [x, c]
            right += [jnp.concatenate(wx, axis=0), jnp.concatenate(wc, axis=0)]
        results.append(
            dot(jnp.concatenate(left, axis=1), jnp.concatenate(right, axis=1), NT).astype(BF16)
        )
    for index in range(PLANE):

        @pl.when(step == index)
        def _():
            for pair in range(groups // 2):
                outs[index][pair] = results[pair]


def local_kernel(gx_ref, cx_ref, dec_ref, res_ref, conv_ref, ig_ref, sums_ref):
    groups, rows, length = gx_ref.shape
    modes = dec_ref.shape[1]
    dec, res = dec_ref[...], res_ref[...]
    ahead = lane_iota((modes, length)).astype(F32)
    later = lane_iota((length, length)) >= lax.broadcasted_iota(jnp.int32, (length, length), 0)
    column_of = lane_iota((length, length)) + lax.broadcasted_iota(jnp.int32, (length, length), 0)
    paired = column_of < length
    mirror = jnp.where(column_of == length - 1, 1.0, 0.0).astype(BF16)
    reverse = dot(cx_ref[...].reshape(groups * rows, length), mirror, NN).astype(BF16)
    sub = lax.broadcasted_iota(jnp.int32, (modes, length), 0)
    lane = lane_iota((modes, length))
    lag = float(length - 1) - ahead
    for pair in range(groups // 2):
        total = jnp.zeros((modes, length), F32)
        for side in range(2):
            group = 2 * pair + side
            rate = column(dec, group)
            basis = jnp.exp(-rate * ahead)
            taps = jnp.sum(column(res, group) * basis, axis=0, keepdims=True)
            toep = pltpu.roll(
                jnp.broadcast_to(taps, (length, length)), 0, 1, stride=1, stride_axis=0
            )
            toep = jnp.where(later, toep, 0.0).astype(BF16)
            x, c = gx_ref[group], cx_ref[group]
            conv_ref[0, pl.ds(group, rows, stride=groups), :] = dot(x, toep, NN)
            ig_ref[0, pl.ds(group, rows, stride=groups), :] = dot(c, toep, NT)
            mirrored = reverse[group * rows : (group + 1) * rows]
            prods = jnp.where(paired, dot(x, mirrored, TN), 0.0)
            prods = pltpu.roll(prods, 0, 1, stride=1, stride_axis=0)
            corr = jnp.sum(prods, axis=0, keepdims=True) * jnp.exp(-rate * lag)
            plain = jnp.sum(corr, axis=1, keepdims=True)
            moment = jnp.sum(corr * lag, axis=1, keepdims=True)
            total += jnp.where(lane == sub + side * modes, plain, 0.0)
            total += jnp.where(lane == sub + (2 + side) * modes, moment, 0.0)
        sums_ref[pair : pair + 1, :] = jnp.sum(total, axis=0, keepdims=True)


def split_pair(x, half):
    head = x.astype(BF16).astype(F32)
    tail = (x - head).astype(BF16).astype(F32)
    low = lane_iota(x.shape) < half
    return jnp.where(low, head, pltpu.roll(jnp.where(low, tail, 0.0), half, x.ndim - 1)).astype(BF16)


def join_pair(x, half):
    x = x.astype(F32)
    low = lane_iota(x.shape) < half
    return jnp.where(low, x + pltpu.roll(x, half, x.ndim - 1), 0.0)


def in_order(arrays, place):
    arrays, bit = list(arrays), 1
    while bit < len(arrays):
        swap = (place & bit) != 0
        new = list(arrays)
        for i in range(len(arrays)):
            new[i] = jnp.where(swap, arrays[i ^ bit], arrays[i])
        arrays, bit = new, 2 * bit
    return arrays


def advance(state, decay, gap, half, axis):
    lane = lane_iota(state.shape)
    shifted = pltpu.roll(state, half, axis)
    return decay * (state + jnp.where(lane >= half, gap * shifted, 0.0))


def pair_terms(state, x, modes):
    lanes = x.shape[-1]
    axis = x.ndim - 1
    plain = jnp.sum(state * pltpu.roll(x, lanes - 2 * modes, axis), axis=1)
    first = jnp.sum(state * pltpu.roll(x, lanes - 6 * modes, axis), axis=1)
    second = jnp.sum(state * pltpu.roll(x, 2 * modes, axis), axis=1)
    lane = lane_iota(plain.shape)
    second = pltpu.roll(second, lanes - 2 * modes, 1)
    first = pltpu.roll(first, 2 * modes, 1)
    return jnp.where(
        lane < 2 * modes, plain, jnp.where(lane < 4 * modes, first + second, 0.0)
    )


def scan_blocks(blocks, start, rate, gap, modes):
    half = 4 * modes
    axis = blocks[0].ndim - 1
    lane = lane_iota(blocks[0].shape)
    forward = (lane % half) < 2 * modes
    decay = jnp.exp(-rate * gap)
    state, states = start, []
    for i in range(len(blocks)):
        states.append(state)
        block = jnp.where(forward, blocks[i], blocks[len(blocks) - 1 - i])
        state = advance(state, decay, gap, half, axis) + block
    return states, state


def all_pair_terms(states, blocks, modes):
    lane = lane_iota(blocks[0].shape)
    total = None
    for i in range(len(blocks)):
        term = pair_terms(states[i], blocks[i], modes)
        total = term if total is None else total + term
    return total


def plane_kernel(length, place, rate_ref, *refs):
    *msgs, sums_ref, out_ref, acc = refs
    pairs, rows, lanes = msgs[0].shape
    modes = lanes // 8
    blocks = in_order([m[...].astype(F32) for m in msgs], place[0])
    rate = rate_ref[...].reshape(pairs, 1, lanes)
    states, last = scan_blocks(blocks, jnp.zeros_like(blocks[0]), rate, float(length), modes)
    out_ref[: pairs * rows] = last.astype(BF16).reshape(pairs * rows, lanes)
    acc[...] = sums_ref[...]
    acc[pl.ds(pl.multiple_of(place[0] * pairs, pairs), pairs), :] += all_pair_terms(
        states, blocks, modes
    )
    out_ref[pairs * rows :] = split_pair(acc[...], lanes // 2)


def line_kernel(length, place, rate_ref, *refs):
    count = (len(refs) - 2 * PLANE - 1)
    msgs, lines = refs[:PLANE], refs[PLANE : PLANE + count]
    outs, acc = refs[PLANE + count : -1], refs[-1]
    pairs, rows, lanes = msgs[0].shape
    modes = lanes // 8
    flat = pairs * rows
    rate = rate_ref[...].reshape(pairs, 1, lanes)
    planes = in_order(
        [r[:flat].astype(F32).reshape(pairs, rows, lanes) for r in lines], place[1]
    )
    gap = float(PLANE * length)
    states, _ = scan_blocks(planes, jnp.zeros_like(planes[0]), rate, gap, modes)
    lane = lane_iota(planes[0].shape)
    forward = (lane % (4 * modes)) < 2 * modes
    incoming = jnp.zeros_like(planes[0])
    for i in range(count):
        here = jnp.where(forward, i, count - 1 - i) == place[1]
        incoming = incoming + jnp.where(here, states[i], 0.0)
    total = join_pair(lines[0][flat:], lanes // 2)
    for r in lines[1:]:
        total = total + join_pair(r[flat:], lanes // 2)
    acc[...] = total
    acc[pl.ds(pl.multiple_of(place[0] * pairs, pairs), pairs), :] += all_pair_terms(
        states, planes, modes
    )
    sums = split_pair(acc[...], lanes // 2)
    blocks = in_order([m[...].astype(F32) for m in msgs], place[0])
    states, _ = scan_blocks(blocks, incoming, rate, float(length), modes)
    found = [
        jnp.where(forward, states[i], states[PLANE - 1 - i]) for i in range(PLANE)
    ]
    found = in_order(found, place[0])
    low = lane[: pairs // 2] < 4 * modes
    for i in range(PLANE):
        packed = jnp.where(
            low, found[i][: pairs // 2], pltpu.roll(found[i][pairs // 2 :], 4 * modes, 2)
        )
        outs[i][: flat // 2] = packed.astype(BF16).reshape(flat // 2, lanes)
        outs[i][flat // 2 :] = sums


def outputs_kernel(
    place, k_ref, v_ref, g_ref, conv_ref, ig_ref, dec_ref, res_ref, *refs
):
    incoming, outs, cs, gs = refs[:PLANE], refs[PLANE : PLANE + 3], refs[-2], refs[-1]
    step = pl.program_id(0)
    rows, groups, length = k_ref.shape
    modes = dec_ref.shape[1]
    pairs = groups // 2
    flat = pairs * rows // 2
    dec, res = dec_ref[...], res_ref[...]
    ahead = lane_iota((modes, length)).astype(F32)
    behind = float(length) - ahead
    state = incoming[0][:flat]
    for i in range(1, PLANE):
        state = jnp.where(step == i, incoming[i][:flat], state)
    zero = jnp.zeros((modes, length), BF16)
    for group in range(groups):
        pair, side = group // 2, group % 2
        rate, weight = column(dec, group), column(res, group)
        base = (4 if pair >= pairs // 2 else 0) + side
        left, right = [zero] * 8, [zero] * 8
        left[base] = (weight * jnp.exp(-rate * ahead)).astype(BF16)
        right[base + 2] = (weight * jnp.exp(-rate * behind)).astype(BF16)
        quad = pair % (pairs // 2)
        s = state[quad * rows : (quad + 1) * rows]
        both = dot(
            s,
            jnp.concatenate(
                [jnp.concatenate(left, axis=0), jnp.concatenate(right, axis=0)], axis=1
            ),
            NN,
        )
        cs[pl.ds(group, rows, stride=groups), :] = both[:, :length]
        gs[pl.ds(group, rows, stride=groups), :] = both[:, length:]
    shape = (rows, groups, length)
    conv = (cs[...] + conv_ref[0]).astype(BF16).reshape(shape)
    ig = (gs[...] + ig_ref[0]).astype(BF16).reshape(shape)
    outs[0][...] = product(g_ref[...], conv)
    outs[1][...] = product(ig, v_ref[...])
    outs[2][...] = product(ig, k_ref[...])


def per_device(queries, keys_in, values_in, grad_out, residue, decay_rate):
    chans, length = queries.shape
    groups, modes = residue.shape
    count = lax.axis_size("ctx")
    tp = lax.axis_size("tp")
    depth = count // PLANE
    rows = chans // groups
    part = groups // PLANE
    pairs = part // 2
    lanes = 8 * modes
    me = lax.axis_index("ctx").astype(jnp.int32)
    place = jnp.stack([me % PLANE, me // PLANE])

    def cube(x):
        return x.reshape(rows, groups, length)

    query, key, value, grad = cube(queries), cube(keys_in), cube(values_in), cube(grad_out)
    rates = jnp.tile(decay_rate.reshape(groups // 2, 2 * modes), (1, 4))

    turn = pl.BlockSpec((rows, part, length), lambda i, s: (0, s[0] ^ i, 0))
    small = pl.BlockSpec((part, modes), lambda i, s: (s[0] ^ i, 0))
    deep = pl.BlockSpec((part, rows, length), lambda i, s: (s[0] ^ i, 0, 0))
    whole = pl.BlockSpec((pairs, rows, lanes), lambda i, s: (0, 0, 0))
    gx, cx, *own = pl.pallas_call(
        states_kernel,
        grid_spec=pltpu.PrefetchScalarGridSpec(
            num_scalar_prefetch=1,
            grid=(PLANE,),
            in_specs=[turn] * 4 + [small],
            out_specs=[deep] * 2 + [whole] * PLANE,
            scratch_shapes=[pltpu.VMEM((rows * part, length), F32)] * 2,
        ),
        out_shape=[jax.ShapeDtypeStruct((groups, rows, length), BF16)] * 2
        + [jax.ShapeDtypeStruct((pairs, rows, lanes), BF16)] * PLANE,
        cost_estimate=pl.CostEstimate(flops=10**9, bytes_accessed=3 * 10**6, transcendentals=0),
        name="states",
    )(place, key, value, grad, query, decay_rate)

    def swap(x, bits):
        return lax.ppermute(x, "ctx", [(i, i ^ bits) for i in range(count)])

    near = [own[0]] + [swap(own[i], i) for i in range(1, PLANE)]

    tall = pl.BlockSpec((part, rows, length), lambda i: (i, 0, 0))
    table = pl.BlockSpec((part, modes), lambda i: (i, 0))
    slab = pl.BlockSpec((1, rows * part, length), lambda i: (i, 0, 0))
    conv, ig, sums = pl.pallas_call(
        local_kernel,
        grid=(PLANE,),
        in_specs=[tall] * 2 + [table] * 2,
        out_specs=[slab] * 2 + [pl.BlockSpec((pairs, lanes), lambda i: (i, 0))],
        out_shape=[jax.ShapeDtypeStruct((PLANE, rows * part, length), F32)] * 2
        + [jax.ShapeDtypeStruct((groups // 2, lanes), F32)],
        cost_estimate=pl.CostEstimate(flops=10**9, bytes_accessed=4 * 10**6, transcendentals=0),
        name="local",
    )(gx, cx, decay_rate, residue)

    flat = pairs * rows
    here = pl.BlockSpec((pairs, lanes), lambda i, s: (s[0], 0))

    def full(*shape):
        return pl.BlockSpec(shape, lambda i, s: (0,) * len(shape))

    plane = pl.pallas_call(
        functools.partial(plane_kernel, length),
        grid_spec=pltpu.PrefetchScalarGridSpec(
            num_scalar_prefetch=1,
            grid=(1,),
            in_specs=[here] + [full(pairs, rows, lanes)] * PLANE + [full(groups // 2, lanes)],
            out_specs=full(flat + groups // 2, lanes),
            scratch_shapes=[pltpu.VMEM((groups // 2, lanes), F32)],
        ),
        out_shape=jax.ShapeDtypeStruct((flat + groups // 2, lanes), BF16),
        name="plane",
    )(place, rates, *near, sums)

    line = [plane] + [swap(plane, PLANE * i) for i in range(1, depth)]
    back = pl.pallas_call(
        functools.partial(line_kernel, length),
        grid_spec=pltpu.PrefetchScalarGridSpec(
            num_scalar_prefetch=1,
            grid=(1,),
            in_specs=[here]
            + [full(pairs, rows, lanes)] * PLANE
            + [full(flat + groups // 2, lanes)] * depth,
            out_specs=[full(flat // 2 + groups // 2, lanes)] * PLANE,
            scratch_shapes=[pltpu.VMEM((groups // 2, lanes), F32)],
        ),
        out_shape=[jax.ShapeDtypeStruct((flat // 2 + groups // 2, lanes), BF16)] * PLANE,
        name="line",
    )(place, rates, *near, *line)
    back = [back[0]] + [swap(back[i], i) for i in range(1, PLANE)]

    total = sum(
        b[flat // 2 :, : lanes // 2].astype(F32) + b[flat // 2 :, lanes // 2 :].astype(F32)
        for b in back
    )
    bit = 1
    while bit < tp:
        total = total + lax.ppermute(total, "tp", [(i, i ^ bit) for i in range(tp)])
        bit *= 2

    turned = pl.BlockSpec((1, rows * part, length), lambda i, s: (s[0] ^ i, 0, 0))
    outs = pl.pallas_call(
        outputs_kernel,
        grid_spec=pltpu.PrefetchScalarGridSpec(
            num_scalar_prefetch=1,
            grid=(PLANE,),
            in_specs=[turn] * 3
            + [turned] * 2
            + [small] * 2
            + [full(flat // 2 + groups // 2, lanes)] * PLANE,
            out_specs=[turn] * 3,
            scratch_shapes=[pltpu.VMEM((rows * part, length), F32)] * 2,
        ),
        out_shape=[jax.ShapeDtypeStruct((rows, groups, length), BF16)] * 3,
        cost_estimate=pl.CostEstimate(flops=10**9, bytes_accessed=5 * 10**6, transcendentals=0),
        name="outputs",
    )(place, key, value, grad, conv, ig, decay_rate, residue, *back)
    tokens = count * length
    plain = total[:, : 2 * modes].reshape(groups, modes)
    moment = total[:, 2 * modes :].reshape(groups, modes)
    return (
        outs[0].reshape(chans, length),
        outs[1].reshape(chans, length),
        outs[2].reshape(chans, length),
        plain / tokens,
        -(residue * decay_rate) * moment / tokens,
    )


def solution(mesh):
    in_specs = (P("tp", "ctx"), P("tp", "ctx"), P("tp", "ctx"), P("tp", "ctx"), P(), P())
    out_specs = (P("tp", "ctx"), P("tp", "ctx"), P("tp", "ctx"), P(), P())
    return jax.shard_map(
        per_device, mesh=mesh, in_specs=in_specs, out_specs=out_specs, check_vma=False
    )
```

```python
import functools
import math

import jax
import jax.numpy as jnp
from jax import lax
from jax.experimental import pallas as pl
from jax.experimental.pallas import tpu as pltpu
from jax.sharding import PartitionSpec as P

F32 = jnp.float32
BF16 = jnp.bfloat16
PLANE = 4
NT = (((1,), (1,)), ((), ()))
NN = (((1,), (0,)), ((), ()))
TN = (((0,), (0,)), ((), ()))


def dot(a, b, dims):
    return lax.dot_general(a, b, dims, preferred_element_type=F32)


def product(a, b):
    return (a.astype(F32) * b.astype(F32)).astype(BF16)


def column(table, group):
    return jnp.sum(jnp.where(lane_iota(table.shape) == group, table, 0.0), axis=1, keepdims=True)


def mirror_of(length):
    total = lane_iota((length, length)) + lax.broadcasted_iota(jnp.int32, (length, length), 0)
    return jnp.where(total == length - 1, 1.0, 0.0).astype(BF16)


def places():
    me = lax.axis_index("ctx")
    return lax.rem(me, PLANE), lax.div(me, PLANE)


def lane_iota(shape):
    return lax.broadcasted_iota(jnp.int32, shape, len(shape) - 1)


def states_kernel(k_hbm, v_hbm, g_hbm, q_hbm, dec_ref, gx_ref, cx_ref, rate_ref, *rest):
    outs, (bufs, sems, wx_ref, wc_ref, gs, cs) = rest[:PLANE], rest[PLANE:]
    place, _ = places()
    _, rows, part, length = bufs.shape[1:]
    modes, groups = dec_ref.shape
    pairs = part // 2
    flat = rows * part
    sources = (k_hbm, v_hbm, g_hbm, q_hbm)

    def copy(which, quarter):
        return pltpu.make_async_copy(
            sources[which].at[:, pl.ds(quarter * part, part), :],
            bufs.at[which, quarter],
            sems.at[which, quarter],
        )

    for quarter in range(PLANE):
        for which in range(4):
            copy(which, quarter).start()
    dec = dec_ref[...]
    ahead = lane_iota((modes, length)).astype(F32)
    behind = float(length) - ahead
    wide = (modes, 8 * modes)
    target = lane_iota(wide) % (2 * modes) - lax.broadcasted_iota(jnp.int32, wide, 0)

    def weights(index, _):
        rates = jnp.zeros(wide, F32)
        for side in range(2):
            group = 2 * index + side
            rate = column(dec, group)
            fwd = jnp.exp(-rate * behind)
            bwd = jnp.exp(-rate * (behind - 1.0))
            wx_ref[group, 0] = fwd.astype(BF16)
            wx_ref[group, 1] = (behind * fwd).astype(BF16)
            wc_ref[group, 0] = bwd.astype(BF16)
            wc_ref[group, 1] = ((behind - 1.0) * bwd).astype(BF16)
            rates += jnp.where(target == side * modes, rate, 0.0)
        rate_ref[pl.ds(index, 1), :] = jnp.sum(rates, axis=0, keepdims=True)
        return 0

    lax.fori_loop(0, groups // 2, weights, 0, unroll=8)
    mirror = mirror_of(length)
    zero = jnp.zeros((modes, length), BF16)

    def quarter_step(quarter, _):
        for which in range(4):
            copy(which, quarter).wait()
        gs[...] = product(bufs[0, quarter], bufs[1, quarter]).astype(F32).reshape(flat, length)
        cs[...] = dot(
            product(bufs[2, quarter], bufs[3, quarter]).reshape(flat, length), mirror, NN
        )
        results = []
        for pair in range(pairs):
            left, right = [], []
            for side in range(2):
                local = 2 * pair + side
                group = quarter * part + local
                x = gs[pl.ds(local, rows, stride=part), :].astype(BF16)
                c = cs[pl.ds(local, rows, stride=part), :].astype(BF16)
                gx_ref[group] = x
                cx_ref[group] = c
                wx, wc = [zero] * 8, [zero] * 8
                wx[side], wx[4 + side] = wx_ref[group, 0], wx_ref[group, 1]
                wc[2 + side], wc[6 + side] = wc_ref[group, 0], wc_ref[group, 1]
                left += [x, c]
                right += [jnp.concatenate(wx, axis=0), jnp.concatenate(wc, axis=0)]
            results.append(
                dot(jnp.concatenate(left, axis=1), jnp.concatenate(right, axis=1), NT).astype(BF16)
            )
        for index in range(PLANE):

            @pl.when((place ^ quarter) == index)
            def _():
                for pair in range(pairs):
                    outs[index][pair] = results[pair]

        return 0

    lax.fori_loop(0, PLANE, quarter_step, 0)


def sums_kernel(gx_ref, cx_ref, dec_ref, sums_ref, corr_ref):
    groups, rows, length = gx_ref.shape
    modes = dec_ref.shape[0]
    part = groups // PLANE
    paired = (
        lane_iota((length, length)) + lax.broadcasted_iota(jnp.int32, (length, length), 0) < length
    )

    def correlate(quarter, _):
        for local in range(part):
            group = quarter * part + local
            prods = jnp.where(paired, dot(gx_ref[group], cx_ref[group], TN), 0.0)
            prods = pltpu.roll(prods, 0, 1, stride=1, stride_axis=0)
            corr_ref[pl.ds(group, 1), :] = jnp.sum(prods, axis=0, keepdims=True)
        return 0

    lax.fori_loop(0, PLANE, correlate, 0)
    dec = dec_ref[...]
    lag = float(length - 1) - lane_iota((modes, length)).astype(F32)
    lane = lane_iota((modes, sums_ref.shape[1]))

    def contract(quarter, carry):
        plain, moment = carry
        for local in range(part):
            group = quarter * part + local
            terms = jnp.exp(-column(dec, group) * lag) * corr_ref[pl.ds(group, 1), :]
            plain = jnp.where(lane == group, jnp.sum(terms, axis=1, keepdims=True), plain)
            moment = jnp.where(lane == group, jnp.sum(terms * lag, axis=1, keepdims=True), moment)
        return plain, moment

    zero = jnp.zeros(lane.shape, F32)
    plain, moment = lax.fori_loop(0, PLANE, contract, (zero, zero))
    sums_ref[:modes] = plain
    sums_ref[modes:] = moment


def local_kernel(gx_ref, cx_ref, dec_ref, res_ref, conv_ref, ig_ref, wl_ref, wr_ref, toep_ref):
    groups, rows, length = gx_ref.shape
    modes = dec_ref.shape[0]
    part = groups // PLANE
    dec, res = dec_ref[...], res_ref[...]
    ahead = lane_iota((modes, length)).astype(F32)
    later = lane_iota((length, length)) >= lax.broadcasted_iota(jnp.int32, (length, length), 0)

    def quarter_step(quarter, _):
        for local in range(part):
            group = quarter * part + local
            rate = column(dec, group)
            taps = column(res, group) * jnp.exp(-rate * ahead)
            wl_ref[group] = taps.astype(BF16)
            wr_ref[group] = (taps * jnp.exp(-rate)).astype(BF16)
            taps = jnp.sum(taps, axis=0, keepdims=True)
            toep = pltpu.roll(
                jnp.broadcast_to(taps, (length, length)), 0, 1, stride=1, stride_axis=0
            )
            toep_ref[local] = jnp.where(later, toep, 0.0).astype(BF16)
        for local in range(part):
            group = quarter * part + local
            both = dot(
                jnp.concatenate([gx_ref[group], cx_ref[group]], axis=0), toep_ref[local], NN
            )
            conv_ref[quarter, pl.ds(local, rows, stride=part), :] = both[:rows]
            ig_ref[quarter, pl.ds(local, rows, stride=part), :] = both[rows:]
        return 0

    lax.fori_loop(0, PLANE, quarter_step, 0)


def split_pair(x, half):
    head = x.astype(BF16).astype(F32)
    tail = (x - head).astype(BF16).astype(F32)
    low = lane_iota(x.shape) < half
    return jnp.where(low, head, pltpu.roll(jnp.where(low, tail, 0.0), half, x.ndim - 1)).astype(BF16)


def join_pair(x, half):
    x = x.astype(F32)
    low = lane_iota(x.shape) < half
    return jnp.where(low, x + pltpu.roll(x, half, x.ndim - 1), 0.0)


def in_order(arrays, place):
    arrays, bit = list(arrays), 1
    while bit < len(arrays):
        swap = (place & bit) != 0
        new = list(arrays)
        for i in range(len(arrays)):
            new[i] = jnp.where(swap, arrays[i ^ bit], arrays[i])
        arrays, bit = new, 2 * bit
    return arrays


def advance(state, decay, gap, half, axis):
    lane = lane_iota(state.shape)
    shifted = pltpu.roll(state, half, axis)
    return decay * (state + jnp.where(lane >= half, gap * shifted, 0.0))


def pair_terms(state, x, modes):
    lanes = x.shape[-1]
    axis = x.ndim - 1
    plain = jnp.sum(state * pltpu.roll(x, lanes - 2 * modes, axis), axis=1)
    first = jnp.sum(state * pltpu.roll(x, lanes - 6 * modes, axis), axis=1)
    second = jnp.sum(state * pltpu.roll(x, 2 * modes, axis), axis=1)
    lane = lane_iota(plain.shape)
    second = pltpu.roll(second, lanes - 2 * modes, 1)
    first = pltpu.roll(first, 2 * modes, 1)
    return jnp.where(
        lane < 2 * modes, plain, jnp.where(lane < 4 * modes, first + second, 0.0)
    )


def scan_blocks(blocks, start, rate, gap, modes):
    half = 4 * modes
    axis = blocks[0].ndim - 1
    lane = lane_iota(blocks[0].shape)
    forward = (lane % half) < 2 * modes
    decay = jnp.exp(-rate * gap)
    state, states = start, []
    for i in range(len(blocks)):
        states.append(state)
        block = jnp.where(forward, blocks[i], blocks[len(blocks) - 1 - i])
        state = advance(state, decay, gap, half, axis) + block
    return states, state


def all_pair_terms(states, blocks, modes):
    lane = lane_iota(blocks[0].shape)
    total = None
    for i in range(len(blocks)):
        term = pair_terms(states[i], blocks[i], modes)
        total = term if total is None else total + term
    return total


def spread(terms, place, acc, modes):
    pairs = terms.shape[0]
    shape = (pairs, acc.shape[1])
    group = lane_iota(shape) - 2 * pairs * place
    row = lax.broadcasted_iota(jnp.int32, shape, 0)
    for side in range(2):
        chosen = jnp.where(group == 2 * row + side, 1.0, 0.0)
        turned = lax.dot_general(
            terms, chosen, TN, precision=lax.Precision.HIGHEST, preferred_element_type=F32
        )
        acc[:modes] += turned[side * modes : (side + 1) * modes]
        acc[modes:] += turned[(2 + side) * modes : (3 + side) * modes]


def plane_kernel(length, rate_ref, *refs):
    *msgs, sums_ref, out_ref, acc = refs
    place, _ = places()
    pairs, rows, lanes = msgs[0].shape
    modes = lanes // 8
    flat = pairs * rows
    blocks = in_order([m[...].astype(F32) for m in msgs], place)
    rate = rate_ref[pl.ds(pl.multiple_of(place * pairs, pairs), pairs), :].reshape(pairs, 1, lanes)
    states, last = scan_blocks(blocks, jnp.zeros_like(blocks[0]), rate, float(length), modes)
    out_ref[:flat] = last.astype(BF16).reshape(flat, lanes)
    acc[...] = sums_ref[...]
    spread(all_pair_terms(states, blocks, modes), place, acc, modes)
    out_ref[flat:] = split_pair(acc[...], lanes // 2)


def line_kernel(length, rate_ref, *refs):
    count = len(refs) - 2 * PLANE - 1
    msgs, lines = refs[:PLANE], refs[PLANE : PLANE + count]
    outs, acc = refs[PLANE + count : -1], refs[-1]
    place, level = places()
    pairs, rows, lanes = msgs[0].shape
    modes = lanes // 8
    flat = pairs * rows
    rate = rate_ref[pl.ds(pl.multiple_of(place * pairs, pairs), pairs), :].reshape(pairs, 1, lanes)
    planes = in_order([r[:flat].astype(F32).reshape(pairs, rows, lanes) for r in lines], level)
    gap = float(PLANE * length)
    states, _ = scan_blocks(planes, jnp.zeros_like(planes[0]), rate, gap, modes)
    lane = lane_iota(planes[0].shape)
    forward = (lane % (4 * modes)) < 2 * modes
    incoming = jnp.zeros_like(planes[0])
    for i in range(count):
        here = jnp.where(forward, i, count - 1 - i) == level
        incoming = incoming + jnp.where(here, states[i], 0.0)
    total = join_pair(lines[0][flat:], lanes // 2)
    for r in lines[1:]:
        total = total + join_pair(r[flat:], lanes // 2)
    acc[...] = total
    spread(all_pair_terms(states, planes, modes), place, acc, modes)
    sums = split_pair(acc[...], lanes // 2)
    blocks = in_order([m[...].astype(F32) for m in msgs], place)
    states, _ = scan_blocks(blocks, incoming, rate, float(length), modes)
    found = [jnp.where(forward, states[i], states[PLANE - 1 - i]) for i in range(PLANE)]
    found = in_order(found, place)
    low = lane[: pairs // 2] < 4 * modes
    for i in range(PLANE):
        packed = jnp.where(
            low, found[i][: pairs // 2], pltpu.roll(found[i][pairs // 2 :], 4 * modes, 2)
        )
        outs[i][: flat // 2] = packed.astype(BF16).reshape(flat // 2, lanes)
        outs[i][flat // 2 :] = sums


def outputs_kernel(k_hbm, v_hbm, g_hbm, conv_ref, ig_ref, wl_ref, wr_ref, *refs):
    incoming, results = refs[:PLANE], refs[PLANE : PLANE + 3]
    bufs, sems, outs, out_sems, cs, gs = refs[PLANE + 3 :]
    place, _ = places()
    _, rows, part, length = bufs.shape[1:]
    modes = wl_ref.shape[1]
    pairs = part // 2
    flat = pairs * rows // 2
    sources = (k_hbm, v_hbm, g_hbm)

    def copy(which, quarter):
        return pltpu.make_async_copy(
            sources[which].at[:, pl.ds(quarter * part, part), :],
            bufs.at[which, quarter],
            sems.at[which, quarter],
        )

    def store(which, quarter):
        return pltpu.make_async_copy(
            outs.at[which, quarter],
            results[which].at[:, pl.ds(quarter * part, part), :],
            out_sems.at[which, quarter],
        )

    for quarter in range(PLANE):
        for which in range(3):
            copy(which, quarter).start()
    mirror = mirror_of(length)
    zero = jnp.zeros((modes, length), BF16)

    def quarter_step(quarter, _):
        index = place ^ quarter
        state = incoming[0][:flat]
        for i in range(1, PLANE):
            state = jnp.where(index == i, incoming[i][:flat], state)
        for local in range(part):
            group = quarter * part + local
            pair, side = local // 2, local % 2
            base = (4 if pair >= pairs // 2 else 0) + side
            left, right = [zero] * 8, [zero] * 8
            left[base], right[base + 2] = wl_ref[group], wr_ref[group]
            quad = pair % (pairs // 2)
            both = dot(
                state[quad * rows : (quad + 1) * rows],
                jnp.concatenate(
                    [jnp.concatenate(left, axis=0), jnp.concatenate(right, axis=0)], axis=1
                ),
                NN,
            )
            cs[pl.ds(local, rows, stride=part), :] = both[:, :length]
            gs[pl.ds(local, rows, stride=part), :] = both[:, length:]
        shape = (rows, part, length)
        for which in range(3):
            copy(which, quarter).wait()
        conv = (cs[...] + conv_ref[quarter]).astype(BF16).reshape(shape)
        ig = (gs[...] + ig_ref[quarter]).astype(BF16)
        ig = dot(ig, mirror, NN).reshape(shape)
        outs[0, quarter] = product(bufs[2, quarter], conv)
        outs[1, quarter] = product(ig, bufs[1, quarter])
        outs[2, quarter] = product(ig, bufs[0, quarter])
        for which in range(3):
            store(which, quarter).start()
        return 0

    lax.fori_loop(0, PLANE, quarter_step, 0)
    for quarter in range(PLANE):
        for which in range(3):
            store(which, quarter).wait()


def per_device(queries, keys_in, values_in, grad_out, residue, decay_rate):
    chans, length = queries.shape
    groups, modes = residue.shape
    count = lax.axis_size("ctx")
    tp = lax.axis_size("tp")
    depth = count // PLANE
    rows = chans // groups
    part = groups // PLANE
    pairs = part // 2
    lanes = 8 * modes

    def cube(x):
        return x.reshape(rows, groups, length)

    query, key, value, grad = cube(queries), cube(keys_in), cube(values_in), cube(grad_out)
    decay, resid = decay_rate.T, residue.T
    vmem = pl.BlockSpec(memory_space=pltpu.VMEM)
    anywhere = pl.BlockSpec(memory_space=pl.ANY)

    def shaped(shape, dtype):
        return jax.ShapeDtypeStruct(shape, dtype)

    def call(kernel, name, in_specs, out_specs, out_shape, scratch, flops, size):
        return pl.pallas_call(
            kernel,
            in_specs=in_specs,
            out_specs=out_specs,
            out_shape=out_shape,
            scratch_shapes=scratch,
            cost_estimate=pl.CostEstimate(flops=flops, bytes_accessed=size, transcendentals=0),
            compiler_params=pltpu.CompilerParams(vmem_limit_bytes=16 * 2**20),
            name=name,
        )

    grouped = shaped((groups, rows, length), BF16)
    block = shaped((pairs, rows, lanes), BF16)
    plane_f32 = pltpu.VMEM((rows * part, length), F32)
    weight = pltpu.VMEM((groups, 2, modes, length), BF16)
    gx, cx, rates, *own = call(
        states_kernel,
        "states",
        [anywhere] * 4 + [vmem],
        [vmem] * (3 + PLANE),
        [grouped] * 2 + [shaped((groups // 2, lanes), F32)] + [block] * PLANE,
        [
            pltpu.VMEM((4, PLANE, rows, part, length), BF16),
            pltpu.SemaphoreType.DMA((4, PLANE)),
            weight,
            weight,
            plane_f32,
            plane_f32,
        ],
        10**9,
        4 * 10**6,
    )(key, value, grad, query, decay)

    def swap(x, bits):
        return lax.ppermute(x, "ctx", [(i, i ^ bits) for i in range(count)])

    near = [own[0]] + [swap(own[i], i) for i in range(1, PLANE)]
    sums = call(
        sums_kernel,
        "sums",
        [vmem] * 3,
        vmem,
        shaped((2 * modes, lanes), F32),
        [pltpu.VMEM((groups, length), F32)],
        10**9,
        4 * 10**6,
    )(gx, cx, decay)
    flat = pairs * rows
    plane = call(
        functools.partial(plane_kernel, length),
        "plane",
        [vmem] * (2 + PLANE),
        vmem,
        shaped((flat + 2 * modes, lanes), BF16),
        [pltpu.VMEM((2 * modes, lanes), F32)],
        10**7,
        10**6,
    )(rates, *near, sums)
    line = [plane] + [swap(plane, PLANE * i) for i in range(1, depth)]
    natural = shaped((PLANE, rows * part, length), F32)
    table = shaped((groups, modes, length), BF16)
    conv, ig, wl, wr = call(
        local_kernel,
        "local",
        [vmem] * 4,
        [vmem] * 4,
        [natural] * 2 + [table] * 2,
        [pltpu.VMEM((part, length, length), BF16)],
        10**9,
        4 * 10**6,
    )(gx, cx, decay, resid)
    back = call(
        functools.partial(line_kernel, length),
        "line",
        [vmem] * (1 + PLANE + depth),
        [vmem] * PLANE,
        [shaped((flat // 2 + 2 * modes, lanes), BF16)] * PLANE,
        [pltpu.VMEM((2 * modes, lanes), F32)],
        10**7,
        10**6,
    )(rates, *near, *line)
    back = [back[0]] + [swap(back[i], i) for i in range(1, PLANE)]

    total = sum(
        b[flat // 2 :, : lanes // 2].astype(F32) + b[flat // 2 :, lanes // 2 :].astype(F32)
        for b in back
    )
    bit = 1
    while bit < tp:
        total = total + lax.ppermute(total, "tp", [(i, i ^ bit) for i in range(tp)])
        bit *= 2

    outs = call(
        outputs_kernel,
        "outputs",
        [anywhere] * 3 + [vmem] * (4 + PLANE),
        [anywhere] * 3,
        [shaped((rows, groups, length), BF16)] * 3,
        [
            pltpu.VMEM((3, PLANE, rows, part, length), BF16),
            pltpu.SemaphoreType.DMA((3, PLANE)),
            pltpu.VMEM((3, PLANE, rows, part, length), BF16),
            pltpu.SemaphoreType.DMA((3, PLANE)),
            plane_f32,
            plane_f32,
        ],
        10**9,
        5 * 10**6,
    )(key, value, grad, conv, ig, wl, wr, *back)
    tokens = count * length
    plain, moment = total[:modes, :groups], total[modes:, :groups]
    return (
        outs[0].reshape(chans, length),
        outs[1].reshape(chans, length),
        outs[2].reshape(chans, length),
        (plain / tokens).T,
        (-(resid * decay) * moment / tokens).T,
    )


def solution(mesh):
    in_specs = (P("tp", "ctx"), P("tp", "ctx"), P("tp", "ctx"), P("tp", "ctx"), P(), P())
    out_specs = (P("tp", "ctx"), P("tp", "ctx"), P("tp", "ctx"), P(), P())
    return jax.shard_map(
        per_device, mesh=mesh, in_specs=in_specs, out_specs=out_specs, check_vma=False
    )
```

```python
import functools
import math

import jax
import jax.numpy as jnp
from jax import lax
from jax.experimental import pallas as pl
from jax.experimental.pallas import tpu as pltpu
from jax.sharding import PartitionSpec as P

F32 = jnp.float32
BF16 = jnp.bfloat16
PLANE = 4
NT = (((1,), (1,)), ((), ()))
NN = (((1,), (0,)), ((), ()))
TN = (((0,), (0,)), ((), ()))


def dot(a, b, dims):
    return lax.dot_general(a, b, dims, preferred_element_type=F32)


def product(a, b):
    return (a.astype(F32) * b.astype(F32)).astype(BF16)


def column(table, group):
    return jnp.sum(jnp.where(lane_iota(table.shape) == group, table, 0.0), axis=1, keepdims=True)


def mirror_of(length):
    total = lane_iota((length, length)) + lax.broadcasted_iota(jnp.int32, (length, length), 0)
    return jnp.where(total == length - 1, 1.0, 0.0).astype(BF16)


def places():
    me = lax.axis_index("ctx")
    return lax.rem(me, PLANE), lax.div(me, PLANE)


def lane_iota(shape):
    return lax.broadcasted_iota(jnp.int32, shape, len(shape) - 1)


def states_kernel(dec_hbm, k_hbm, v_hbm, g_hbm, q_hbm, gx_ref, cx_ref, rate_ref, *rest):
    outs, (dec_ref, dec_sem, bufs, sems, wx_ref, wc_ref, gs, cs) = rest[:PLANE], rest[PLANE:]
    place, _ = places()
    _, rows, part, length = bufs.shape[1:]
    modes, groups = dec_ref.shape
    pairs = part // 2
    flat = rows * part
    sources = (k_hbm, v_hbm, g_hbm, q_hbm)

    def copy(which, quarter):
        return pltpu.make_async_copy(
            sources[which].at[:, pl.ds(quarter * part, part), :],
            bufs.at[which, quarter],
            sems.at[which, quarter],
        )

    rates_in = pltpu.make_async_copy(dec_hbm, dec_ref, dec_sem)
    rates_in.start()
    for quarter in range(PLANE):
        for which in range(4):
            copy(which, quarter).start()
    rates_in.wait()
    dec = dec_ref[...]
    ahead = lane_iota((modes, length)).astype(F32)
    behind = float(length) - ahead
    wide = (modes, 8 * modes)
    target = lane_iota(wide) % (2 * modes) - lax.broadcasted_iota(jnp.int32, wide, 0)

    def weights(index, _):
        rates = jnp.zeros(wide, F32)
        for side in range(2):
            group = 2 * index + side
            rate = column(dec, group)
            fwd = jnp.exp(-rate * behind)
            bwd = jnp.exp(-rate * (behind - 1.0))
            wx_ref[group, 0] = fwd.astype(BF16)
            wx_ref[group, 1] = (behind * fwd).astype(BF16)
            wc_ref[group, 0] = bwd.astype(BF16)
            wc_ref[group, 1] = ((behind - 1.0) * bwd).astype(BF16)
            rates += jnp.where(target == side * modes, rate, 0.0)
        rate_ref[pl.ds(index, 1), :] = jnp.sum(rates, axis=0, keepdims=True)
        return 0

    lax.fori_loop(0, groups // 2, weights, 0, unroll=8)
    mirror = mirror_of(length)
    zero = jnp.zeros((modes, length), BF16)

    def quarter_step(quarter, _):
        for which in range(4):
            copy(which, quarter).wait()
        gs[...] = product(bufs[0, quarter], bufs[1, quarter]).astype(F32).reshape(flat, length)
        cs[...] = dot(
            product(bufs[2, quarter], bufs[3, quarter]).reshape(flat, length), mirror, NN
        )
        results = []
        for pair in range(pairs):
            left, right = [], []
            for side in range(2):
                local = 2 * pair + side
                group = quarter * part + local
                x = gs[pl.ds(local, rows, stride=part), :].astype(BF16)
                c = cs[pl.ds(local, rows, stride=part), :].astype(BF16)
                gx_ref[group] = x
                cx_ref[group] = c
                wx, wc = [zero] * 8, [zero] * 8
                wx[side], wx[4 + side] = wx_ref[group, 0], wx_ref[group, 1]
                wc[2 + side], wc[6 + side] = wc_ref[group, 0], wc_ref[group, 1]
                left += [x, c]
                right += [jnp.concatenate(wx, axis=0), jnp.concatenate(wc, axis=0)]
            results.append(
                dot(jnp.concatenate(left, axis=1), jnp.concatenate(right, axis=1), NT).astype(BF16)
            )
        for index in range(PLANE):

            @pl.when((place ^ quarter) == index)
            def _():
                for pair in range(pairs):
                    outs[index][pair] = results[pair]

        return 0

    lax.fori_loop(0, PLANE, quarter_step, 0)


def sums_kernel(gx_ref, cx_ref, dec_ref, sums_ref, corr_ref):
    groups, rows, length = gx_ref.shape
    modes = dec_ref.shape[0]
    part = groups // PLANE
    paired = (
        lane_iota((length, length)) + lax.broadcasted_iota(jnp.int32, (length, length), 0) < length
    )

    def correlate(quarter, _):
        for local in range(part):
            group = quarter * part + local
            prods = jnp.where(paired, dot(gx_ref[group], cx_ref[group], TN), 0.0)
            prods = pltpu.roll(prods, 0, 1, stride=1, stride_axis=0)
            corr_ref[pl.ds(group, 1), :] = jnp.sum(prods, axis=0, keepdims=True)
        return 0

    lax.fori_loop(0, PLANE, correlate, 0)
    dec = dec_ref[...]
    lag = float(length - 1) - lane_iota((modes, length)).astype(F32)
    lane = lane_iota((modes, sums_ref.shape[1]))

    def contract(quarter, carry):
        plain, moment = carry
        for local in range(part):
            group = quarter * part + local
            terms = jnp.exp(-column(dec, group) * lag) * corr_ref[pl.ds(group, 1), :]
            plain = jnp.where(lane == group, jnp.sum(terms, axis=1, keepdims=True), plain)
            moment = jnp.where(lane == group, jnp.sum(terms * lag, axis=1, keepdims=True), moment)
        return plain, moment

    zero = jnp.zeros(lane.shape, F32)
    plain, moment = lax.fori_loop(0, PLANE, contract, (zero, zero))
    sums_ref[:modes] = plain
    sums_ref[modes:] = moment


def local_kernel(gx_ref, cx_ref, dec_ref, res_ref, after_ref, conv_ref, ig_ref, wl_ref, wr_ref, toep_ref):
    groups, rows, length = gx_ref.shape
    modes = dec_ref.shape[0]
    part = groups // PLANE
    dec, res = dec_ref[...], res_ref[...]
    ahead = lane_iota((modes, length)).astype(F32)
    later = lane_iota((length, length)) >= lax.broadcasted_iota(jnp.int32, (length, length), 0)

    def quarter_step(quarter, _):
        for local in range(part):
            group = quarter * part + local
            rate = column(dec, group)
            taps = column(res, group) * jnp.exp(-rate * ahead)
            wl_ref[group] = taps.astype(BF16)
            wr_ref[group] = (taps * jnp.exp(-rate)).astype(BF16)
            taps = jnp.sum(taps, axis=0, keepdims=True)
            toep = pltpu.roll(
                jnp.broadcast_to(taps, (length, length)), 0, 1, stride=1, stride_axis=0
            )
            toep_ref[local] = jnp.where(later, toep, 0.0).astype(BF16)
        for local in range(part):
            group = quarter * part + local
            both = dot(
                jnp.concatenate([gx_ref[group], cx_ref[group]], axis=0), toep_ref[local], NN
            )
            conv_ref[quarter, pl.ds(local, rows, stride=part), :] = both[:rows]
            ig_ref[quarter, pl.ds(local, rows, stride=part), :] = both[rows:]
        return 0

    lax.fori_loop(0, PLANE, quarter_step, 0)


def split_pair(x, half):
    head = x.astype(BF16).astype(F32)
    tail = (x - head).astype(BF16).astype(F32)
    low = lane_iota(x.shape) < half
    return jnp.where(low, head, pltpu.roll(jnp.where(low, tail, 0.0), half, x.ndim - 1)).astype(BF16)


def join_pair(x, half):
    x = x.astype(F32)
    low = lane_iota(x.shape) < half
    return jnp.where(low, x + pltpu.roll(x, half, x.ndim - 1), 0.0)


def in_order(arrays, place):
    arrays, bit = list(arrays), 1
    while bit < len(arrays):
        swap = (place & bit) != 0
        new = list(arrays)
        for i in range(len(arrays)):
            new[i] = jnp.where(swap, arrays[i ^ bit], arrays[i])
        arrays, bit = new, 2 * bit
    return arrays


def advance(state, decay, gap, half, axis):
    lane = lane_iota(state.shape)
    shifted = pltpu.roll(state, half, axis)
    return decay * (state + jnp.where(lane >= half, gap * shifted, 0.0))


def pair_terms(state, x, modes):
    lanes = x.shape[-1]
    axis = x.ndim - 1
    plain = jnp.sum(state * pltpu.roll(x, lanes - 2 * modes, axis), axis=1)
    first = jnp.sum(state * pltpu.roll(x, lanes - 6 * modes, axis), axis=1)
    second = jnp.sum(state * pltpu.roll(x, 2 * modes, axis), axis=1)
    lane = lane_iota(plain.shape)
    second = pltpu.roll(second, lanes - 2 * modes, 1)
    first = pltpu.roll(first, 2 * modes, 1)
    return jnp.where(
        lane < 2 * modes, plain, jnp.where(lane < 4 * modes, first + second, 0.0)
    )


def scan_blocks(blocks, start, rate, gap, modes):
    half = 4 * modes
    axis = blocks[0].ndim - 1
    lane = lane_iota(blocks[0].shape)
    forward = (lane % half) < 2 * modes
    decay = jnp.exp(-rate * gap)
    state, states = start, []
    for i in range(len(blocks)):
        states.append(state)
        block = jnp.where(forward, blocks[i], blocks[len(blocks) - 1 - i])
        state = advance(state, decay, gap, half, axis) + block
    return states, state


def all_pair_terms(states, blocks, modes):
    lane = lane_iota(blocks[0].shape)
    total = None
    for i in range(len(blocks)):
        term = pair_terms(states[i], blocks[i], modes)
        total = term if total is None else total + term
    return total


def spread(terms, place, acc, modes):
    pairs = terms.shape[0]
    shape = (pairs, acc.shape[1])
    group = lane_iota(shape) - 2 * pairs * place
    row = lax.broadcasted_iota(jnp.int32, shape, 0)
    for side in range(2):
        chosen = jnp.where(group == 2 * row + side, 1.0, 0.0)
        turned = lax.dot_general(
            terms, chosen, TN, precision=lax.Precision.HIGHEST, preferred_element_type=F32
        )
        acc[:modes] += turned[side * modes : (side + 1) * modes]
        acc[modes:] += turned[(2 + side) * modes : (3 + side) * modes]


def plane_kernel(length, rate_ref, *refs):
    *msgs, sums_ref, out_ref, acc = refs
    place, _ = places()
    pairs, rows, lanes = msgs[0].shape
    modes = lanes // 8
    flat = pairs * rows
    blocks = in_order([m[...].astype(F32) for m in msgs], place)
    rate = rate_ref[pl.ds(pl.multiple_of(place * pairs, pairs), pairs), :].reshape(pairs, 1, lanes)
    states, last = scan_blocks(blocks, jnp.zeros_like(blocks[0]), rate, float(length), modes)
    out_ref[:flat] = last.astype(BF16).reshape(flat, lanes)
    acc[...] = sums_ref[...]
    spread(all_pair_terms(states, blocks, modes), place, acc, modes)
    out_ref[flat:] = split_pair(acc[...], lanes // 2)


def line_kernel(length, rate_ref, after_ref, *refs):
    count = len(refs) - 2 * PLANE - 1
    msgs, lines = refs[:PLANE], refs[PLANE : PLANE + count]
    outs, acc = refs[PLANE + count : -1], refs[-1]
    place, level = places()
    pairs, rows, lanes = msgs[0].shape
    modes = lanes // 8
    flat = pairs * rows
    rate = rate_ref[pl.ds(pl.multiple_of(place * pairs, pairs), pairs), :].reshape(pairs, 1, lanes)
    planes = in_order([r[:flat].astype(F32).reshape(pairs, rows, lanes) for r in lines], level)
    gap = float(PLANE * length)
    states, _ = scan_blocks(planes, jnp.zeros_like(planes[0]), rate, gap, modes)
    lane = lane_iota(planes[0].shape)
    forward = (lane % (4 * modes)) < 2 * modes
    incoming = jnp.zeros_like(planes[0])
    for i in range(count):
        here = jnp.where(forward, i, count - 1 - i) == level
        incoming = incoming + jnp.where(here, states[i], 0.0)
    total = join_pair(lines[0][flat:], lanes // 2)
    for r in lines[1:]:
        total = total + join_pair(r[flat:], lanes // 2)
    acc[...] = total
    spread(all_pair_terms(states, planes, modes), place, acc, modes)
    sums = split_pair(acc[...], lanes // 2)
    blocks = in_order([m[...].astype(F32) for m in msgs], place)
    states, _ = scan_blocks(blocks, incoming, rate, float(length), modes)
    found = [jnp.where(forward, states[i], states[PLANE - 1 - i]) for i in range(PLANE)]
    found = in_order(found, place)
    low = lane[: pairs // 2] < 4 * modes
    for i in range(PLANE):
        packed = jnp.where(
            low, found[i][: pairs // 2], pltpu.roll(found[i][pairs // 2 :], 4 * modes, 2)
        )
        outs[i][: flat // 2] = packed.astype(BF16).reshape(flat // 2, lanes)
        outs[i][flat // 2 :] = sums


def outputs_kernel(k_ref, v_ref, g_ref, conv_ref, ig_ref, wl_ref, wr_ref, *refs):
    incoming, results = refs[:PLANE], refs[PLANE : PLANE + 3]
    outs, out_sems, cs, gs = refs[PLANE + 3 :]
    place, _ = places()
    _, rows, part, length = outs.shape[1:]
    modes = wl_ref.shape[1]
    pairs = part // 2
    flat = pairs * rows // 2
    def store(which, quarter):
        return pltpu.make_async_copy(
            outs.at[which, quarter],
            results[which].at[:, pl.ds(quarter * part, part), :],
            out_sems.at[which, quarter],
        )

    mirror = mirror_of(length)
    zero = jnp.zeros((modes, length), BF16)

    def quarter_step(quarter, _):
        index = place ^ quarter
        state = incoming[0][:flat]
        for i in range(1, PLANE):
            state = jnp.where(index == i, incoming[i][:flat], state)
        for local in range(part):
            group = quarter * part + local
            pair, side = local // 2, local % 2
            base = (4 if pair >= pairs // 2 else 0) + side
            left, right = [zero] * 8, [zero] * 8
            left[base], right[base + 2] = wl_ref[group], wr_ref[group]
            quad = pair % (pairs // 2)
            both = dot(
                state[quad * rows : (quad + 1) * rows],
                jnp.concatenate(
                    [jnp.concatenate(left, axis=0), jnp.concatenate(right, axis=0)], axis=1
                ),
                NN,
            )
            cs[pl.ds(local, rows, stride=part), :] = both[:, :length]
            gs[pl.ds(local, rows, stride=part), :] = both[:, length:]
        shape = (rows, part, length)
        own = pl.ds(pl.multiple_of(quarter * part, part), part)
        conv = (cs[...] + conv_ref[quarter]).astype(BF16).reshape(shape)
        ig = (gs[...] + ig_ref[quarter]).astype(BF16)
        ig = dot(ig, mirror, NN).reshape(shape)
        outs[0, quarter] = product(g_ref[:, own, :], conv)
        outs[1, quarter] = product(ig, v_ref[:, own, :])
        outs[2, quarter] = product(ig, k_ref[:, own, :])
        for which in range(3):
            store(which, quarter).start()
        return 0

    lax.fori_loop(0, PLANE, quarter_step, 0)
    for quarter in range(PLANE):
        for which in range(3):
            store(which, quarter).wait()


def per_device(queries, keys_in, values_in, grad_out, residue, decay_rate):
    chans, length = queries.shape
    groups, modes = residue.shape
    count = lax.axis_size("ctx")
    tp = lax.axis_size("tp")
    depth = count // PLANE
    rows = chans // groups
    part = groups // PLANE
    pairs = part // 2
    lanes = 8 * modes

    def cube(x):
        return x.reshape(rows, groups, length)

    query, key, value, grad = cube(queries), cube(keys_in), cube(values_in), cube(grad_out)
    decay, resid = decay_rate.T, residue.T
    vmem = pl.BlockSpec(memory_space=pltpu.VMEM)
    anywhere = pl.BlockSpec(memory_space=pltpu.HBM)

    def shaped(shape, dtype):
        return jax.ShapeDtypeStruct(shape, dtype)

    def call(kernel, name, in_specs, out_specs, out_shape, scratch, flops, size):
        return pl.pallas_call(
            kernel,
            in_specs=in_specs,
            out_specs=out_specs,
            out_shape=out_shape,
            scratch_shapes=scratch,
            cost_estimate=pl.CostEstimate(flops=flops, bytes_accessed=size, transcendentals=0),
            compiler_params=pltpu.CompilerParams(vmem_limit_bytes=16 * 2**20),
            name=name,
        )

    grouped = shaped((groups, rows, length), BF16)
    block = shaped((pairs, rows, lanes), BF16)
    plane_f32 = pltpu.VMEM((rows * part, length), F32)
    weight = pltpu.VMEM((groups, 2, modes, length), BF16)
    gx, cx, rates, *own = call(
        states_kernel,
        "states",
        [anywhere] * 5,
        [vmem] * (3 + PLANE),
        [grouped] * 2 + [shaped((groups // 2, lanes), F32)] + [block] * PLANE,
        [
            pltpu.VMEM((modes, groups), F32),
            pltpu.SemaphoreType.DMA,
            pltpu.VMEM((4, PLANE, rows, part, length), BF16),
            pltpu.SemaphoreType.DMA((4, PLANE)),
            weight,
            weight,
            plane_f32,
            plane_f32,
        ],
        10**9,
        4 * 10**6,
    )(*(pltpu.with_memory_space_constraint(x, pltpu.HBM) for x in (decay, key, value, grad, query)))

    def swap(x, bits):
        return lax.ppermute(x, "ctx", [(i, i ^ bits) for i in range(count)])

    near = [own[0]] + [swap(own[i], i) for i in range(1, PLANE)]
    sums = call(
        sums_kernel,
        "sums",
        [vmem] * 3,
        vmem,
        shaped((2 * modes, lanes), F32),
        [pltpu.VMEM((groups, length), F32)],
        10**9,
        4 * 10**6,
    )(gx, cx, decay)
    flat = pairs * rows
    plane = call(
        functools.partial(plane_kernel, length),
        "plane",
        [vmem] * (2 + PLANE),
        vmem,
        shaped((flat + 2 * modes, lanes), BF16),
        [pltpu.VMEM((2 * modes, lanes), F32)],
        10**7,
        10**6,
    )(rates, *near, sums)
    line = [plane] + [swap(plane, PLANE * i) for i in range(1, depth)]
    natural = shaped((PLANE, rows * part, length), F32)
    table = shaped((groups, modes, length), BF16)
    conv, ig, wl, wr = call(
        local_kernel,
        "local",
        [vmem] * 5,
        [vmem] * 4,
        [natural] * 2 + [table] * 2,
        [pltpu.VMEM((part, length, length), BF16)],
        10**9,
        4 * 10**6,
    )(gx, cx, decay, resid, plane)
    back = call(
        functools.partial(line_kernel, length),
        "line",
        [vmem] * (2 + PLANE + depth),
        [vmem] * PLANE,
        [shaped((flat // 2 + 2 * modes, lanes), BF16)] * PLANE,
        [pltpu.VMEM((2 * modes, lanes), F32)],
        10**7,
        10**6,
    )(rates, wl, *near, *line)
    back = [back[0]] + [swap(back[i], i) for i in range(1, PLANE)]

    total = sum(
        b[flat // 2 :, : lanes // 2].astype(F32) + b[flat // 2 :, lanes // 2 :].astype(F32)
        for b in back
    )
    bit = 1
    while bit < tp:
        total = total + lax.ppermute(total, "tp", [(i, i ^ bit) for i in range(tp)])
        bit *= 2

    outs = call(
        outputs_kernel,
        "outputs",
        [vmem] * (7 + PLANE),
        [anywhere] * 3,
        [shaped((rows, groups, length), BF16)] * 3,
        [
            pltpu.VMEM((3, PLANE, rows, part, length), BF16),
            pltpu.SemaphoreType.DMA((3, PLANE)),
            plane_f32,
            plane_f32,
        ],
        10**9,
        5 * 10**6,
    )(key, value, grad, conv, ig, wl, wr, *back)
    tokens = count * length
    plain, moment = total[:modes, :groups], total[modes:, :groups]
    return (
        outs[0].reshape(chans, length),
        outs[1].reshape(chans, length),
        outs[2].reshape(chans, length),
        (plain / tokens).T,
        (-(resid * decay) * moment / tokens).T,
    )


def solution(mesh):
    in_specs = (P("tp", "ctx"), P("tp", "ctx"), P("tp", "ctx"), P("tp", "ctx"), P(), P())
    out_specs = (P("tp", "ctx"), P("tp", "ctx"), P("tp", "ctx"), P(), P())
    return jax.shard_map(
        per_device, mesh=mesh, in_specs=in_specs, out_specs=out_specs, check_vma=False
    )
```

```python
import functools
import math

import jax
import jax.numpy as jnp
from jax import lax
from jax.experimental import pallas as pl
from jax.experimental.pallas import tpu as pltpu
from jax.sharding import PartitionSpec as P

F32 = jnp.float32
BF16 = jnp.bfloat16
PLANE = 4
NT = (((1,), (1,)), ((), ()))
NN = (((1,), (0,)), ((), ()))
TN = (((0,), (0,)), ((), ()))


def dot(a, b, dims):
    return lax.dot_general(a, b, dims, preferred_element_type=F32)


def product(a, b):
    return (a.astype(F32) * b.astype(F32)).astype(BF16)


def column(table, group):
    return jnp.sum(jnp.where(lane_iota(table.shape) == group, table, 0.0), axis=1, keepdims=True)


def mirror_of(length):
    total = lane_iota((length, length)) + lax.broadcasted_iota(jnp.int32, (length, length), 0)
    return jnp.where(total == length - 1, 1.0, 0.0).astype(BF16)


def places():
    me = lax.axis_index("ctx")
    return lax.rem(me, PLANE), lax.div(me, PLANE)


def lane_iota(shape):
    return lax.broadcasted_iota(jnp.int32, shape, len(shape) - 1)


def states_kernel(dec_hbm, k_hbm, v_hbm, g_hbm, q_hbm, xc_ref, rate_ref, *rest):
    outs, rest = rest[:PLANE], rest[PLANE:]
    dec_ref, dec_sem, bufs, sems, w_ref, gs, cs, st_ref = rest
    place, _ = places()
    _, rows, part, length = bufs.shape[1:]
    modes, groups = dec_ref.shape
    quads = part // 4
    flat = rows * part
    sources = (k_hbm, v_hbm, g_hbm, q_hbm)

    def copy(which, quarter):
        return pltpu.make_async_copy(
            sources[which].at[:, pl.ds(quarter * part, part), :],
            bufs.at[which, quarter],
            sems.at[which, quarter],
        )

    rates_in = pltpu.make_async_copy(dec_hbm, dec_ref, dec_sem)
    rates_in.start()
    for quarter in range(PLANE):
        for which in range(4):
            copy(which, quarter).start()
    rates_in.wait()
    dec = dec_ref[...]
    behind = float(length) - lane_iota((modes, length)).astype(F32)
    wide = (modes, 8 * modes)
    target = lane_iota(wide) % (4 * modes) - lax.broadcasted_iota(jnp.int32, wide, 0)

    def weights(index, _):
        rates = jnp.zeros(wide, F32)
        for side in range(4):
            group = 4 * index + side
            rate = column(dec, group)
            basis = jnp.exp(-rate * behind)
            w_ref[group, 0] = basis.astype(BF16)
            w_ref[group, 1] = (behind * basis).astype(BF16)
            rates = jnp.where(target == side * modes, rate, rates)
        rate_ref[pl.ds(index, 1), :] = jnp.sum(rates, axis=0, keepdims=True)
        return 0

    lax.fori_loop(0, groups // 4, weights, 0, unroll=4)
    mirror = mirror_of(length)
    zero = jnp.zeros((modes, length), BF16)

    def load(quarter):
        for which in range(4):
            copy(which, quarter).wait()
        slot = quarter % 2
        x = product(bufs[0, quarter], bufs[1, quarter]).astype(F32)
        c = product(bufs[2, quarter], bufs[3, quarter]).reshape(flat, length)
        c = dot(c, mirror, NN).reshape(x.shape)
        for part8 in range(part // 8):
            gs[slot, part8] = x[:, 8 * part8 : 8 * part8 + 8].reshape(8 * rows, length)
            cs[slot, part8] = c[:, 8 * part8 : 8 * part8 + 8].reshape(8 * rows, length)

    def reduce(quarter):
        slot = quarter % 2
        for quad in range(quads):
            left, right = [], []
            for side in range(4):
                local = 4 * quad + side
                group = quarter * part + local
                both = jnp.concatenate(
                    [
                        gs[slot, local // 8, pl.ds(local % 8, rows, stride=8), :],
                        cs[slot, local // 8, pl.ds(local % 8, rows, stride=8), :],
                    ],
                    axis=0,
                ).astype(BF16)
                xc_ref[group] = both
                w = [zero] * 8
                w[side], w[4 + side] = w_ref[group, 0], w_ref[group, 1]
                left.append(both)
                right.append(jnp.concatenate(w, axis=0))
            st_ref[quarter, quad] = dot(
                jnp.concatenate(left, axis=1), jnp.concatenate(right, axis=1), NT
            ).astype(BF16)

    for quarter in range(PLANE + 1):
        if quarter < PLANE:
            load(quarter)
        if quarter > 0:
            reduce(quarter - 1)
    for quad in range(quads):
        for index, x in enumerate(in_order([st_ref[i, quad] for i in range(PLANE)], place)):
            outs[index][quad] = x


def sums_kernel(xc_ref, dec_ref, sums_ref, corr_ref):
    groups, rows, length = xc_ref.shape
    rows = rows // 2
    modes = dec_ref.shape[0]
    part = groups // PLANE
    paired = (
        lane_iota((length, length)) + lax.broadcasted_iota(jnp.int32, (length, length), 0) < length
    )

    def correlate(quarter, _):
        for local in range(part):
            group = quarter * part + local
            prods = jnp.where(paired, dot(xc_ref[group, :rows], xc_ref[group, rows:], TN), 0.0)
            prods = pltpu.roll(prods, 0, 1, stride=1, stride_axis=0)
            corr_ref[pl.ds(group, 1), :] = jnp.sum(prods, axis=0, keepdims=True)
        return 0

    lax.fori_loop(0, PLANE, correlate, 0)
    dec = dec_ref[...]
    lag = float(length - 1) - lane_iota((modes, length)).astype(F32)
    lane = lane_iota((modes, sums_ref.shape[1]))

    def contract(quarter, carry):
        plain, moment = carry
        for local in range(part):
            group = quarter * part + local
            terms = jnp.exp(-column(dec, group) * lag) * corr_ref[pl.ds(group, 1), :]
            plain = jnp.where(lane == group, jnp.sum(terms, axis=1, keepdims=True), plain)
            moment = jnp.where(lane == group, jnp.sum(terms * lag, axis=1, keepdims=True), moment)
        return plain, moment

    zero = jnp.zeros(lane.shape, F32)
    plain, moment = lax.fori_loop(0, PLANE, contract, (zero, zero))
    sums_ref[:modes] = plain
    sums_ref[modes:] = moment


def local_kernel(xc_ref, dec_ref, res_ref, after_ref, out_ref, taps_ref, toep_ref):
    groups, _, length = xc_ref.shape
    modes = dec_ref.shape[0]
    part = groups // PLANE
    dec, res = dec_ref[...], res_ref[...]
    ahead = lane_iota((modes, length)).astype(F32)
    later = lane_iota((length, length)) >= lax.broadcasted_iota(jnp.int32, (length, length), 0)

    def quarter_step(quarter, _):
        for local in range(part):
            group = quarter * part + local
            rate = column(dec, group)
            taps = column(res, group) * jnp.exp(-rate * ahead)
            taps_ref[group] = taps.astype(BF16)
            taps = jnp.sum(taps, axis=0, keepdims=True)
            toep = pltpu.roll(
                jnp.broadcast_to(taps, (length, length)), 0, 1, stride=1, stride_axis=0
            )
            toep_ref[local] = jnp.where(later, toep, 0.0).astype(BF16)
        for local in range(part):
            group = quarter * part + local
            out_ref[group] = dot(xc_ref[group], toep_ref[local], NN)
        return 0

    lax.fori_loop(0, PLANE, quarter_step, 0)


def split_pair(x, half):
    head = x.astype(BF16).astype(F32)
    tail = (x - head).astype(BF16).astype(F32)
    low = lane_iota(x.shape) < half
    return jnp.where(low, head, pltpu.roll(jnp.where(low, tail, 0.0), half, x.ndim - 1)).astype(BF16)


def join_pair(x, half):
    x = x.astype(F32)
    low = lane_iota(x.shape) < half
    return jnp.where(low, x + pltpu.roll(x, half, x.ndim - 1), 0.0)


def in_order(arrays, place):
    arrays, bit = list(arrays), 1
    while bit < len(arrays):
        swap = (place & bit) != 0
        new = list(arrays)
        for i in range(len(arrays)):
            new[i] = jnp.where(swap, arrays[i ^ bit], arrays[i])
        arrays, bit = new, 2 * bit
    return arrays


def advance(state, decay, gap):
    half = state.shape[2] // 2
    shifted = pltpu.roll(state, half, 2)
    return decay * (state + jnp.where(lane_iota(state.shape) >= half, gap * shifted, 0.0))


def scan_blocks(heads, tails, start, rate, gap):
    decay = jnp.exp(-rate * gap)
    state, before = start[0], []
    for head in heads:
        before.append(state)
        state = advance(state, decay, gap) + head
    other, after = start[1], []
    for tail in tails[::-1]:
        after.insert(0, other)
        other = advance(other, decay, gap) + tail
    return before, after, state, other


def pair_terms(before, tails, rate):
    half = rate.shape[2] // 2
    plain, moment = 0.0, 0.0
    for state, tail in zip(before, tails, strict=True):
        plain = plain + state * tail
        moment = moment + state * pltpu.roll(tail, half, 2)
    plain, moment = jnp.sum(plain, axis=1), jnp.sum(moment, axis=1)
    moment = moment + pltpu.roll(moment, half, 1) - pltpu.roll(plain, half, 1)
    return jnp.where(lane_iota(plain.shape) < half, plain, moment) * jnp.exp(rate[:, 0])


def spread(terms, place, acc, modes):
    quads = terms.shape[0]
    shape = (quads, acc.shape[1])
    group = lane_iota(shape) - 4 * quads * place
    row = lax.broadcasted_iota(jnp.int32, shape, 0)
    for side in range(4):
        chosen = jnp.where(group == 4 * row + side, 1.0, 0.0)
        turned = lax.dot_general(
            terms, chosen, TN, precision=lax.Precision.HIGHEST, preferred_element_type=F32
        )
        acc[:modes] += turned[side * modes : (side + 1) * modes]
        acc[modes:] += turned[(4 + side) * modes : (5 + side) * modes]


def own_rates(rate_ref, place, quads):
    rate = rate_ref[pl.ds(place * quads, quads), :]
    return rate.reshape(quads, 1, rate.shape[1])


def halves(blocks, rows):
    return [b[:, :rows] for b in blocks], [b[:, rows:] for b in blocks]


def plane_kernel(length, rate_ref, *refs):
    *msgs, sums_ref, out_ref, acc = refs
    place, _ = places()
    quads, rows, lanes = msgs[0].shape
    rows, flat = rows // 2, quads * rows
    modes = lanes // 8
    heads, tails = halves(in_order([m[...].astype(F32) for m in msgs], place), rows)
    rate = own_rates(rate_ref, place, quads)
    nothing = jnp.zeros_like(heads[0])
    before, _, head, tail = scan_blocks(heads, tails, (nothing, nothing), rate, float(length))
    both = jnp.concatenate([head, tail], axis=1)
    out_ref[:flat] = both.astype(BF16).reshape(flat, lanes)
    acc[...] = sums_ref[...]
    spread(pair_terms(before, tails, rate), place, acc, modes)
    out_ref[flat:] = split_pair(acc[...], lanes // 2)


def line_kernel(length, rate_ref, after_ref, *refs):
    count = len(refs) - 2 * PLANE - 1
    msgs, lines = refs[:PLANE], refs[PLANE : PLANE + count]
    outs, acc = refs[PLANE + count : -1], refs[-1]
    place, level = places()
    quads, rows, lanes = msgs[0].shape
    shape = (quads, rows, lanes)
    rows, flat = rows // 2, quads * rows
    modes = lanes // 8
    rate = own_rates(rate_ref, place, quads)
    heads, tails = halves(
        in_order([r[:flat].astype(F32).reshape(shape) for r in lines], level), rows
    )
    nothing = jnp.zeros_like(heads[0])
    before, after, _, _ = scan_blocks(
        heads, tails, (nothing, nothing), rate, float(PLANE * length)
    )
    total = join_pair(lines[0][flat:], lanes // 2)
    for r in lines[1:]:
        total = total + join_pair(r[flat:], lanes // 2)
    acc[...] = total
    spread(pair_terms(before, tails, rate), place, acc, modes)
    sums = split_pair(acc[...], lanes // 2)
    start = [nothing, nothing]
    for i in range(count):
        start[0] = jnp.where(level == i, before[i], start[0])
        start[1] = jnp.where(level == i, after[i], start[1])
    heads, tails = halves(in_order([m[...].astype(F32) for m in msgs], place), rows)
    before, after, _, _ = scan_blocks(heads, tails, start, rate, float(length))
    found = [jnp.concatenate(pair, axis=1) for pair in zip(before, after, strict=True)]
    found = in_order(found, place)
    low = lane_iota((quads // 2,) + shape[1:]) < lanes // 2
    for i in range(PLANE):
        packed = jnp.where(low, found[i][: quads // 2], pltpu.roll(found[i][quads // 2 :], lanes // 2, 2))
        outs[i][: flat // 2] = packed.astype(BF16).reshape(flat // 2, lanes)
        outs[i][flat // 2 :] = sums


def outputs_kernel(k_ref, v_ref, g_ref, near_ref, taps_ref, *refs):
    incoming, results = refs[:PLANE], refs[PLANE : PLANE + 3]
    outs, out_sems, cs, gs = refs[PLANE + 3 :]
    place, _ = places()
    _, rows, part, length = outs.shape[1:]
    modes = taps_ref.shape[1]
    quads = part // 4
    flat = quads * rows

    def store(which, quarter):
        return pltpu.make_async_copy(
            outs.at[which, quarter],
            results[which].at[:, pl.ds(quarter * part, part), :],
            out_sems.at[which, quarter],
        )

    mirror = mirror_of(length)
    zero = jnp.zeros((modes, length), BF16)

    def expand(quarter):
        slot = quarter % 2
        index = place ^ quarter
        state = incoming[0][:flat]
        for i in range(1, PLANE):
            state = jnp.where(index == i, incoming[i][:flat], state)
        for local in range(part):
            quad, side = local // 4, local % 4
            base = side + (4 if quad >= quads // 2 else 0)
            first = (quad % (quads // 2)) * 2 * rows
            taps = jnp.concatenate(
                [zero] * base + [taps_ref[quarter * part + local]] + [zero] * (7 - base), axis=0
            )
            both = dot(state[first : first + 2 * rows], taps, NN)
            both = both + near_ref[quarter * part + local]
            cs[slot, local // 8, pl.ds(local % 8, rows, stride=8), :] = both[:rows]
            gs[slot, local // 8, pl.ds(local % 8, rows, stride=8), :] = both[rows:]

    def finish(quarter):
        slot = quarter % 2
        shape = (rows, part, length)
        own = pl.ds(quarter * part, part)
        conv, ig = (
            jnp.concatenate(
                [ref[slot, i].reshape(rows, 8, length) for i in range(part // 8)], axis=1
            ).astype(BF16)
            for ref in (cs, gs)
        )
        ig = dot(ig.reshape(rows * part, length), mirror, NN).reshape(shape)
        outs[0, quarter] = product(g_ref[:, own, :], conv)
        outs[1, quarter] = product(ig, v_ref[:, own, :])
        outs[2, quarter] = product(ig, k_ref[:, own, :])
        for which in range(3):
            store(which, quarter).start()

    for quarter in range(PLANE + 1):
        if quarter < PLANE:
            expand(quarter)
        if quarter > 0:
            finish(quarter - 1)
    for quarter in range(PLANE):
        for which in range(3):
            store(which, quarter).wait()


def per_device(queries, keys_in, values_in, grad_out, residue, decay_rate):
    chans, length = queries.shape
    groups, modes = residue.shape
    count = lax.axis_size("ctx")
    tp = lax.axis_size("tp")
    depth = count // PLANE
    rows = chans // groups
    part = groups // PLANE
    quads = part // 4
    lanes = 8 * modes

    def cube(x):
        return x.reshape(rows, groups, length)

    query, key, value, grad = cube(queries), cube(keys_in), cube(values_in), cube(grad_out)
    decay, resid = decay_rate.T, residue.T
    vmem = pl.BlockSpec(memory_space=pltpu.VMEM)
    anywhere = pl.BlockSpec(memory_space=pltpu.HBM)

    def shaped(shape, dtype):
        return jax.ShapeDtypeStruct(shape, dtype)

    def call(kernel, name, in_specs, out_specs, out_shape, scratch, flops, size):
        return pl.pallas_call(
            kernel,
            in_specs=in_specs,
            out_specs=out_specs,
            out_shape=out_shape,
            scratch_shapes=scratch,
            cost_estimate=pl.CostEstimate(flops=flops, bytes_accessed=size, transcendentals=0),
            compiler_params=pltpu.CompilerParams(vmem_limit_bytes=16 * 2**20),
            name=name,
        )

    grouped = shaped((groups, 2 * rows, length), BF16)
    block = shaped((quads, 2 * rows, lanes), BF16)
    xc, rates, *own = call(
        states_kernel,
        "states",
        [anywhere] * 5,
        [vmem] * (2 + PLANE),
        [grouped, shaped((groups // 4, lanes), F32)] + [block] * PLANE,
        [
            pltpu.VMEM((modes, groups), F32),
            pltpu.SemaphoreType.DMA,
            pltpu.VMEM((4, PLANE, rows, part, length), BF16),
            pltpu.SemaphoreType.DMA((4, PLANE)),
            pltpu.VMEM((groups, 2, modes, length), BF16),
            pltpu.VMEM((2, part // 8, rows * 8, length), F32),
            pltpu.VMEM((2, part // 8, rows * 8, length), F32),
            pltpu.VMEM((PLANE, quads, 2 * rows, lanes), BF16),
        ],
        10**9,
        4 * 10**6,
    )(*(pltpu.with_memory_space_constraint(x, pltpu.HBM) for x in (decay, key, value, grad, query)))

    def swap(x, bits):
        return lax.ppermute(x, "ctx", [(i, i ^ bits) for i in range(count)])

    near = [own[0]] + [swap(own[i], i) for i in range(1, PLANE)]
    sums = call(
        sums_kernel,
        "sums",
        [vmem] * 2,
        vmem,
        shaped((2 * modes, lanes), F32),
        [pltpu.VMEM((groups, length), F32)],
        10**9,
        4 * 10**6,
    )(xc, decay)
    flat = quads * 2 * rows
    plane = call(
        functools.partial(plane_kernel, length),
        "plane",
        [vmem] * (2 + PLANE),
        vmem,
        shaped((flat + 2 * modes, lanes), BF16),
        [pltpu.VMEM((2 * modes, lanes), F32)],
        10**7,
        10**6,
    )(rates, *near, sums)
    line = [plane] + [swap(plane, PLANE * i) for i in range(1, depth)]
    table = shaped((groups, modes, length), BF16)
    near_part, taps = call(
        local_kernel,
        "local",
        [vmem] * 4,
        [vmem] * 2,
        [shaped((groups, 2 * rows, length), F32), table],
        [pltpu.VMEM((part, length, length), BF16)],
        10**9,
        4 * 10**6,
    )(xc, decay, resid, plane)
    back = call(
        functools.partial(line_kernel, length),
        "line",
        [vmem] * (2 + PLANE + depth),
        [vmem] * PLANE,
        [shaped((flat // 2 + 2 * modes, lanes), BF16)] * PLANE,
        [pltpu.VMEM((2 * modes, lanes), F32)],
        10**7,
        10**6,
    )(rates, taps, *near, *line)
    back = [back[0]] + [swap(back[i], i) for i in range(1, PLANE)]

    total = sum(
        b[flat // 2 :, : lanes // 2].astype(F32) + b[flat // 2 :, lanes // 2 :].astype(F32)
        for b in back
    )
    bit = 1
    while bit < tp:
        total = total + lax.ppermute(total, "tp", [(i, i ^ bit) for i in range(tp)])
        bit *= 2

    outs = call(
        outputs_kernel,
        "outputs",
        [vmem] * (5 + PLANE),
        [anywhere] * 3,
        [shaped((rows, groups, length), BF16)] * 3,
        [
            pltpu.VMEM((3, PLANE, rows, part, length), BF16),
            pltpu.SemaphoreType.DMA((3, PLANE)),
            pltpu.VMEM((2, part // 8, rows * 8, length), F32),
            pltpu.VMEM((2, part // 8, rows * 8, length), F32),
        ],
        10**9,
        5 * 10**6,
    )(key, value, grad, near_part, taps, *back)
    tokens = count * length
    plain, moment = total[:modes, :groups], total[modes:, :groups]
    return (
        outs[0].reshape(chans, length),
        outs[1].reshape(chans, length),
        outs[2].reshape(chans, length),
        (plain / tokens).T,
        (-(resid * decay) * moment / tokens).T,
    )


def solution(mesh):
    in_specs = (P("tp", "ctx"), P("tp", "ctx"), P("tp", "ctx"), P("tp", "ctx"), P(), P())
    out_specs = (P("tp", "ctx"), P("tp", "ctx"), P("tp", "ctx"), P(), P())
    return jax.shard_map(
        per_device, mesh=mesh, in_specs=in_specs, out_specs=out_specs, check_vma=False
    )
```

```python
import functools
import math

import jax
import jax.numpy as jnp
from jax import lax
from jax.experimental import pallas as pl
from jax.experimental.pallas import tpu as pltpu
from jax.sharding import PartitionSpec as P

F32 = jnp.float32
BF16 = jnp.bfloat16
PLANE = 4
NT = (((1,), (1,)), ((), ()))
NN = (((1,), (0,)), ((), ()))
TN = (((0,), (0,)), ((), ()))


def dot(a, b, dims):
    return lax.dot_general(a, b, dims, preferred_element_type=F32)


def product(a, b):
    return (a.astype(F32) * b.astype(F32)).astype(BF16)


def column(table, group):
    return jnp.sum(jnp.where(lane_iota(table.shape) == group, table, 0.0), axis=1, keepdims=True)


def mirror_of(length):
    total = lane_iota((length, length)) + lax.broadcasted_iota(jnp.int32, (length, length), 0)
    return jnp.where(total == length - 1, 1.0, 0.0).astype(BF16)


def places():
    me = lax.axis_index("ctx")
    return lax.rem(me, PLANE), lax.div(me, PLANE)


def lane_iota(shape):
    return lax.broadcasted_iota(jnp.int32, shape, len(shape) - 1)


class Reducer:
    def __init__(self, sources, bufs, sems, w_ref, gs, cs):
        self.sources, self.bufs, self.sems, self.w_ref, self.gs, self.cs = (
            sources, bufs, sems, w_ref, gs, cs
        )
        _, self.rows, self.part, self.length = bufs.shape[1:]
        self.mirror = mirror_of(self.length)

    def copies(self, slot, quarter):
        return [
            pltpu.make_async_copy(
                source.at[:, pl.ds(pl.multiple_of(quarter * self.part, self.part), self.part), :],
                self.bufs.at[which, slot],
                self.sems.at[which, slot],
            )
            for which, source in enumerate(self.sources)
        ]

    def load(self, slot, quarter):
        for copy in self.copies(slot, quarter):
            copy.wait()
        bufs, flat = self.bufs, self.rows * self.part
        x = product(bufs[0, slot], bufs[1, slot]).astype(F32)
        c = product(bufs[2, slot], bufs[3, slot]).reshape(flat, self.length)
        c = dot(c, self.mirror, NN).reshape(x.shape)
        for eight in range(self.part // 8):
            span = slice(8 * eight, 8 * eight + 8)
            self.gs[slot, eight] = x[:, span].reshape(8 * self.rows, self.length)
            self.cs[slot, eight] = c[:, span].reshape(8 * self.rows, self.length)

    def reduce(self, slot, quarter, xc_ref, out_ref):
        zero = jnp.zeros(self.w_ref.shape[2:], BF16)
        for quad in range(self.part // 4):
            left, right = [], []
            for side in range(4):
                local = 4 * quad + side
                group = quarter * self.part + local
                where = pl.ds(local % 8, self.rows, stride=8)
                both = jnp.concatenate(
                    [ref[slot, local // 8, where, :] for ref in (self.gs, self.cs)], axis=0
                ).astype(BF16)
                xc_ref[local] = both
                w = [zero] * 8
                w[side], w[4 + side] = self.w_ref[group, 0], self.w_ref[group, 1]
                left.append(both)
                right.append(jnp.concatenate(w, axis=0))
            out_ref[quad] = dot(
                jnp.concatenate(left, axis=1), jnp.concatenate(right, axis=1), NT
            ).astype(BF16)


def states_kernel(dec_hbm, k_hbm, v_hbm, g_hbm, q_hbm, xc_ref, w_ref, rate_ref, *rest):
    outs, rest = rest[: PLANE - 1], rest[PLANE - 1 :]
    dec_ref, dec_sem, bufs, sems, gs, cs = rest
    place, _ = places()
    modes, groups = dec_ref.shape
    work = Reducer((k_hbm, v_hbm, g_hbm, q_hbm), bufs, sems, w_ref, gs, cs)
    length = work.length
    rates_in = pltpu.make_async_copy(dec_hbm, dec_ref, dec_sem)
    rates_in.start()
    for slot in range(PLANE - 1):
        for copy in work.copies(slot, place ^ (slot + 1)):
            copy.start()
    rates_in.wait()
    dec = dec_ref[...]
    behind = float(length) - lane_iota((modes, length)).astype(F32)
    wide = (modes, 8 * modes)
    target = lane_iota(wide) % (4 * modes) - lax.broadcasted_iota(jnp.int32, wide, 0)

    def weights(index, _):
        rates = jnp.zeros(wide, F32)
        for side in range(4):
            group = 4 * index + side
            rate = column(dec, group)
            basis = jnp.exp(-rate * behind)
            w_ref[group, 0] = basis.astype(BF16)
            w_ref[group, 1] = (behind * basis).astype(BF16)
            rates = jnp.where(target == side * modes, rate, rates)
        rate_ref[pl.ds(index, 1), :] = jnp.sum(rates, axis=0, keepdims=True)
        return 0

    lax.fori_loop(0, groups // 4, weights, 0, unroll=4)
    for slot in range(PLANE):
        if slot < PLANE - 1:
            work.load(slot, place ^ (slot + 1))
        if slot > 0:
            work.reduce(slot - 1, place ^ slot, xc_ref.at[slot - 1], outs[slot - 1])


def sums_kernel(k_hbm, v_hbm, g_hbm, q_hbm, xc_ref, w_ref, dec_ref, own_ref, out_ref, sums_ref, *rest):
    bufs, sems, gs, cs, corr_ref = rest
    place, _ = places()
    work = Reducer((k_hbm, v_hbm, g_hbm, q_hbm), bufs, sems, w_ref, gs, cs)
    for copy in work.copies(0, place):
        copy.start()
    _, part, rows, length = xc_ref.shape
    rows = rows // 2
    modes = dec_ref.shape[0]
    paired = (
        lane_iota((length, length)) + lax.broadcasted_iota(jnp.int32, (length, length), 0) < length
    )

    def correlate(ref, base):
        for local in range(part):
            prods = jnp.where(paired, dot(ref[local, :rows], ref[local, rows:], TN), 0.0)
            prods = pltpu.roll(prods, 0, 1, stride=1, stride_axis=0)
            corr_ref[pl.ds(base + local, 1), :] = jnp.sum(prods, axis=0, keepdims=True)

    def others(slot, _):
        correlate(xc_ref.at[slot], part * (place ^ (slot + 1)))
        return 0

    lax.fori_loop(0, PLANE - 1, others, 0)
    work.load(0, place)
    work.reduce(0, place, own_ref, out_ref)
    correlate(own_ref, part * place)
    dec = dec_ref[...]
    lag = float(length - 1) - lane_iota((modes, length)).astype(F32)
    lane = lane_iota((modes, sums_ref.shape[1]))

    def contract(quarter, carry):
        plain, moment = carry
        for local in range(part):
            group = quarter * part + local
            terms = jnp.exp(-column(dec, group) * lag) * corr_ref[pl.ds(group, 1), :]
            plain = jnp.where(lane == group, jnp.sum(terms, axis=1, keepdims=True), plain)
            moment = jnp.where(lane == group, jnp.sum(terms * lag, axis=1, keepdims=True), moment)
        return plain, moment

    zero = jnp.zeros(lane.shape, F32)
    plain, moment = lax.fori_loop(0, PLANE, contract, (zero, zero))
    sums_ref[:modes] = plain
    sums_ref[modes:] = moment


def local_kernel(own_ref, xc_ref, dec_ref, res_ref, after_ref, out_ref, taps_ref, toep_ref):
    _, part, _, length = xc_ref.shape
    modes = dec_ref.shape[0]
    place, _ = places()
    dec, res = dec_ref[...], res_ref[...]
    ahead = lane_iota((modes, length)).astype(F32)
    later = lane_iota((length, length)) >= lax.broadcasted_iota(jnp.int32, (length, length), 0)

    def convolve(index, ref):
        for local in range(part):
            group = (place ^ index) * part + local
            taps = column(res, group) * jnp.exp(-column(dec, group) * ahead)
            taps_ref[index, local] = taps.astype(BF16)
            taps = jnp.sum(taps, axis=0, keepdims=True)
            toep = pltpu.roll(
                jnp.broadcast_to(taps, (length, length)), 0, 1, stride=1, stride_axis=0
            )
            toep_ref[local] = jnp.where(later, toep, 0.0).astype(BF16)
        for local in range(part):
            out_ref[index, local] = dot(ref[local], toep_ref[local], NN)

    convolve(0, own_ref)

    def others(index, _):
        convolve(index, xc_ref.at[index - 1])
        return 0

    lax.fori_loop(1, PLANE, others, 0)


def split_pair(x, half):
    head = x.astype(BF16).astype(F32)
    tail = (x - head).astype(BF16).astype(F32)
    low = lane_iota(x.shape) < half
    return jnp.where(low, head, pltpu.roll(jnp.where(low, tail, 0.0), half, x.ndim - 1)).astype(BF16)


def join_pair(x, half):
    x = x.astype(F32)
    low = lane_iota(x.shape) < half
    return jnp.where(low, x + pltpu.roll(x, half, x.ndim - 1), 0.0)


def in_order(arrays, place):
    arrays, bit = list(arrays), 1
    while bit < len(arrays):
        swap = (place & bit) != 0
        new = list(arrays)
        for i in range(len(arrays)):
            new[i] = jnp.where(swap, arrays[i ^ bit], arrays[i])
        arrays, bit = new, 2 * bit
    return arrays


def advance(state, decay, gap):
    half = state.shape[2] // 2
    shifted = pltpu.roll(state, half, 2)
    return decay * (state + jnp.where(lane_iota(state.shape) >= half, gap * shifted, 0.0))


def scan_blocks(heads, tails, start, rate, gap):
    decay = jnp.exp(-rate * gap)
    state, before = start[0], []
    for head in heads:
        before.append(state)
        state = advance(state, decay, gap) + head
    other, after = start[1], []
    for tail in tails[::-1]:
        after.insert(0, other)
        other = advance(other, decay, gap) + tail
    return before, after, state, other


def pair_terms(before, tails, rate):
    half = rate.shape[2] // 2
    plain, moment = 0.0, 0.0
    for state, tail in zip(before, tails, strict=True):
        plain = plain + state * tail
        moment = moment + state * pltpu.roll(tail, half, 2)
    plain, moment = jnp.sum(plain, axis=1), jnp.sum(moment, axis=1)
    moment = moment + pltpu.roll(moment, half, 1) - pltpu.roll(plain, half, 1)
    return jnp.where(lane_iota(plain.shape) < half, plain, moment) * jnp.exp(rate[:, 0])


def spread(terms, place, acc, modes):
    quads = terms.shape[0]
    shape = (quads, acc.shape[1])
    group = lane_iota(shape) - 4 * quads * place
    row = lax.broadcasted_iota(jnp.int32, shape, 0)
    for side in range(4):
        chosen = jnp.where(group == 4 * row + side, 1.0, 0.0)
        turned = lax.dot_general(
            terms, chosen, TN, precision=lax.Precision.HIGHEST, preferred_element_type=F32
        )
        acc[:modes] += turned[side * modes : (side + 1) * modes]
        acc[modes:] += turned[(4 + side) * modes : (5 + side) * modes]


def own_rates(rate_ref, place, quads):
    rate = rate_ref[pl.ds(place * quads, quads), :]
    return rate.reshape(quads, 1, rate.shape[1])


def halves(blocks, rows):
    return [b[:, :rows] for b in blocks], [b[:, rows:] for b in blocks]


def plane_kernel(length, rate_ref, *refs):
    *msgs, sums_ref, out_ref, acc = refs
    place, _ = places()
    quads, rows, lanes = msgs[0].shape
    rows, flat = rows // 2, quads * rows
    modes = lanes // 8
    heads, tails = halves(in_order([m[...].astype(F32) for m in msgs], place), rows)
    rate = own_rates(rate_ref, place, quads)
    nothing = jnp.zeros_like(heads[0])
    before, _, head, tail = scan_blocks(heads, tails, (nothing, nothing), rate, float(length))
    both = jnp.concatenate([head, tail], axis=1)
    out_ref[:flat] = both.astype(BF16).reshape(flat, lanes)
    acc[...] = sums_ref[...]
    spread(pair_terms(before, tails, rate), place, acc, modes)
    out_ref[flat:] = split_pair(acc[...], lanes // 2)


def line_kernel(length, rate_ref, after_ref, *refs):
    count = len(refs) - 2 * PLANE - 1
    msgs, lines = refs[:PLANE], refs[PLANE : PLANE + count]
    outs, acc = refs[PLANE + count : -1], refs[-1]
    place, level = places()
    quads, rows, lanes = msgs[0].shape
    shape = (quads, rows, lanes)
    rows, flat = rows // 2, quads * rows
    modes = lanes // 8
    rate = own_rates(rate_ref, place, quads)
    heads, tails = halves(
        in_order([r[:flat].astype(F32).reshape(shape) for r in lines], level), rows
    )
    nothing = jnp.zeros_like(heads[0])
    before, after, _, _ = scan_blocks(
        heads, tails, (nothing, nothing), rate, float(PLANE * length)
    )
    total = join_pair(lines[0][flat:], lanes // 2)
    for r in lines[1:]:
        total = total + join_pair(r[flat:], lanes // 2)
    acc[...] = total
    spread(pair_terms(before, tails, rate), place, acc, modes)
    sums = split_pair(acc[...], lanes // 2)
    start = [nothing, nothing]
    for i in range(count):
        start[0] = jnp.where(level == i, before[i], start[0])
        start[1] = jnp.where(level == i, after[i], start[1])
    heads, tails = halves(in_order([m[...].astype(F32) for m in msgs], place), rows)
    before, after, _, _ = scan_blocks(heads, tails, start, rate, float(length))
    found = [jnp.concatenate(pair, axis=1) for pair in zip(before, after, strict=True)]
    found = in_order(found, place)
    low = lane_iota((quads // 2,) + shape[1:]) < lanes // 2
    for i in range(PLANE):
        packed = jnp.where(low, found[i][: quads // 2], pltpu.roll(found[i][quads // 2 :], lanes // 2, 2))
        outs[i][: flat // 2] = packed.astype(BF16).reshape(flat // 2, lanes)
        outs[i][flat // 2 :] = sums


def outputs_kernel(index, tokens, k_ref, v_ref, g_ref, near_ref, taps_ref, state_ref, *refs):
    last = index == PLANE - 1
    if last:
        (total_ref, dec_ref, res_ref), refs = refs[:3], refs[3:]
    if index > 0:
        refs = refs[3:]
    results, refs = refs[:3], refs[3:]
    if last:
        grads, refs = refs[:2], refs[2:]
    outs, sems, cs, gs, *rest = refs
    place, _ = places()
    _, rows, part, length = outs.shape
    modes = taps_ref.shape[2]
    quads = part // 4
    quarter = place ^ index
    own = pl.ds(pl.multiple_of(quarter * part, part), part)
    stores = [
        pltpu.make_async_copy(outs.at[which], results[which].at[:, own, :], sems.at[which])
        for which in range(3)
    ]
    if last:
        sums, sums_sems = rest
        groups = dec_ref.shape[1]
        sums[0] = total_ref[:modes, :groups] / tokens
        sums[1] = -(res_ref[...] * dec_ref[...]) * total_ref[modes:, :groups] / tokens
        stores += [
            pltpu.make_async_copy(sums.at[which], grads[which], sums_sems.at[which])
            for which in range(2)
        ]
        for copy in stores[3:]:
            copy.start()
    mirror = mirror_of(length)
    zero = jnp.zeros((modes, length), BF16)
    for local in range(part):
        quad, side = local // 4, local % 4
        base = side + (4 if quad >= quads // 2 else 0)
        first = (quad % (quads // 2)) * 2 * rows
        taps = jnp.concatenate(
            [zero] * base + [taps_ref[index, local]] + [zero] * (7 - base), axis=0
        )
        both = dot(state_ref[first : first + 2 * rows], taps, NN) + near_ref[index, local]
        cs[local // 8, pl.ds(local % 8, rows, stride=8), :] = both[:rows]
        gs[local // 8, pl.ds(local % 8, rows, stride=8), :] = both[rows:]
    shape = (rows, part, length)
    conv, ig = (
        jnp.concatenate(
            [ref[i].reshape(rows, 8, length) for i in range(part // 8)], axis=1
        ).astype(BF16)
        for ref in (cs, gs)
    )
    outs[0] = product(g_ref[:, own, :], conv)
    stores[0].start()
    ig = dot(ig.reshape(rows * part, length), mirror, NN).reshape(shape)
    outs[1] = product(ig, v_ref[:, own, :])
    stores[1].start()
    outs[2] = product(ig, k_ref[:, own, :])
    stores[2].start()
    for copy in stores:
        copy.wait()


def per_device(queries, keys_in, values_in, grad_out, residue, decay_rate):
    chans, length = queries.shape
    groups, modes = residue.shape
    count = lax.axis_size("ctx")
    tp = lax.axis_size("tp")
    depth = count // PLANE
    rows = chans // groups
    part = groups // PLANE
    quads = part // 4
    lanes = 8 * modes

    def cube(x):
        return x.reshape(rows, groups, length)

    query, key, value, grad = cube(queries), cube(keys_in), cube(values_in), cube(grad_out)
    decay, resid = decay_rate.T, residue.T
    vmem = pl.BlockSpec(memory_space=pltpu.VMEM)
    anywhere = pl.BlockSpec(memory_space=pltpu.HBM)

    def shaped(shape, dtype):
        return jax.ShapeDtypeStruct(shape, dtype)

    def call(kernel, name, in_specs, out_specs, out_shape, scratch, flops, size, aliases=None):
        return pl.pallas_call(
            kernel,
            in_specs=in_specs,
            out_specs=out_specs,
            out_shape=out_shape,
            scratch_shapes=scratch,
            cost_estimate=pl.CostEstimate(flops=flops, bytes_accessed=size, transcendentals=0),
            compiler_params=pltpu.CompilerParams(vmem_limit_bytes=16 * 2**20),
            input_output_aliases=aliases or {},
            name=name,
        )

    def in_hbm(*arrays):
        return [pltpu.with_memory_space_constraint(x, pltpu.HBM) for x in arrays]

    def reducer(slots):
        return [
            pltpu.VMEM((4, slots, rows, part, length), BF16),
            pltpu.SemaphoreType.DMA((4, slots)),
        ] + [pltpu.VMEM((slots, part // 8, rows * 8, length), F32)] * 2

    quarter = (part, 2 * rows, length)
    block = shaped((quads, 2 * rows, lanes), BF16)
    xc, weights, rates, *own = call(
        states_kernel,
        "states",
        [anywhere] * 5,
        [vmem] * (2 + PLANE),
        [
            shaped((PLANE - 1,) + quarter, BF16),
            shaped((groups, 2, modes, length), BF16),
            shaped((groups // 4, lanes), F32),
        ]
        + [block] * (PLANE - 1),
        [pltpu.VMEM((modes, groups), F32), pltpu.SemaphoreType.DMA] + reducer(PLANE - 1),
        10**9,
        4 * 10**6,
    )(*in_hbm(decay, key, value, grad, query))

    def swap(x, bits):
        return lax.ppermute(x, "ctx", [(i, i ^ bits) for i in range(count)])

    near = [swap(own[i - 1], i) for i in range(1, PLANE)]
    xo, mine, sums = call(
        sums_kernel,
        "sums",
        [anywhere] * 4 + [vmem] * 3,
        [vmem] * 3,
        [shaped(quarter, BF16), block, shaped((2 * modes, lanes), F32)],
        reducer(1) + [pltpu.VMEM((groups, length), F32)],
        10**9,
        4 * 10**6,
    )(*in_hbm(key, value, grad, query), xc, weights, decay)
    near = [mine] + near
    flat = quads * 2 * rows
    plane = call(
        functools.partial(plane_kernel, length),
        "plane",
        [vmem] * (2 + PLANE),
        vmem,
        shaped((flat + 2 * modes, lanes), BF16),
        [pltpu.VMEM((2 * modes, lanes), F32)],
        10**7,
        10**6,
    )(rates, *near, sums)
    line = [plane] + [swap(plane, PLANE * i) for i in range(1, depth)]
    near_part, taps = call(
        local_kernel,
        "local",
        [vmem] * 5,
        [vmem] * 2,
        [
            shaped((PLANE,) + quarter, F32),
            shaped((PLANE, part, modes, length), BF16),
        ],
        [pltpu.VMEM((part, length, length), BF16)],
        10**9,
        4 * 10**6,
    )(xo, xc, decay, resid, plane)
    back = call(
        functools.partial(line_kernel, length),
        "line",
        [vmem] * (2 + PLANE + depth),
        [vmem] * PLANE,
        [shaped((flat // 2 + 2 * modes, lanes), BF16)] * PLANE,
        [pltpu.VMEM((2 * modes, lanes), F32)],
        10**7,
        10**6,
    )(rates, taps, *near, *line)
    back = [back[0]] + [swap(back[i], i) for i in range(1, PLANE)]

    total = sum(
        b[flat // 2 :, : lanes // 2].astype(F32) + b[flat // 2 :, lanes // 2 :].astype(F32)
        for b in back
    )
    bit = 1
    while bit < tp:
        total = total + lax.ppermute(total, "tp", [(i, i ^ bit) for i in range(tp)])
        bit *= 2

    tokens = count * length
    outs = ()
    for index in range(PLANE):
        last = index == PLANE - 1
        extra = (total, decay, resid) if last else ()
        *outs, = call(
            functools.partial(outputs_kernel, index, tokens),
            f"outputs{index}",
            [vmem] * (6 + len(extra)) + [anywhere] * len(outs),
            [anywhere] * (5 if last else 3),
            [shaped((rows, groups, length), BF16)] * 3
            + [shaped((modes, groups), F32)] * (2 if last else 0),
            [
                pltpu.VMEM((3, rows, part, length), BF16),
                pltpu.SemaphoreType.DMA((3,)),
                pltpu.VMEM((part // 8, rows * 8, length), F32),
                pltpu.VMEM((part // 8, rows * 8, length), F32),
            ]
            + (
                [pltpu.VMEM((2, modes, groups), F32), pltpu.SemaphoreType.DMA((2,))]
                if last
                else []
            ),
            2 * 10**8,
            10**6,
            {6 + len(extra) + i: i for i in range(len(outs))},
        )(key, value, grad, near_part, taps, back[index], *extra, *outs)
    return (*(x.reshape(chans, length) for x in outs[:3]), outs[3].T, outs[4].T)


def solution(mesh):
    in_specs = (P("tp", "ctx"), P("tp", "ctx"), P("tp", "ctx"), P("tp", "ctx"), P(), P())
    out_specs = (P("tp", "ctx"), P("tp", "ctx"), P("tp", "ctx"), P(), P())
    return jax.shard_map(
        per_device, mesh=mesh, in_specs=in_specs, out_specs=out_specs, check_vma=False
    )
```

```python
import functools

import jax
import jax.numpy as jnp
from jax import lax
from jax.experimental import pallas as pl
from jax.experimental.pallas import tpu as pltpu
from jax.sharding import PartitionSpec as P

F32 = jnp.float32
BF16 = jnp.bfloat16
PLANE = 4
NT = (((1,), (1,)), ((), ()))
NN = (((1,), (0,)), ((), ()))
TN = (((0,), (0,)), ((), ()))


def dot(a, b, dims):
    return lax.dot_general(a, b, dims, preferred_element_type=F32)


def product(a, b):
    return (a.astype(F32) * b.astype(F32)).astype(BF16)


def column(table, group):
    return jnp.sum(jnp.where(lane_iota(table.shape) == group, table, 0.0), axis=1, keepdims=True)


def mirror_of(length):
    total = lane_iota((length, length)) + lax.broadcasted_iota(jnp.int32, (length, length), 0)
    return jnp.where(total == length - 1, 1.0, 0.0).astype(BF16)


def places():
    me = lax.axis_index("ctx")
    return lax.rem(me, PLANE), lax.div(me, PLANE)


def lane_iota(shape):
    return lax.broadcasted_iota(jnp.int32, shape, len(shape) - 1)


class Reducer:
    def __init__(self, sources, bufs, sems, w_ref, gs, cs):
        self.sources, self.bufs, self.sems, self.w_ref, self.gs, self.cs = (
            sources, bufs, sems, w_ref, gs, cs
        )
        _, self.rows, self.part, self.length = bufs.shape[1:]
        self.mirror = mirror_of(self.length)

    def copies(self, slot, quarter):
        return [
            pltpu.make_async_copy(
                source.at[:, pl.ds(pl.multiple_of(quarter * self.part, self.part), self.part), :],
                self.bufs.at[which, slot],
                self.sems.at[which, slot],
            )
            for which, source in enumerate(self.sources)
        ]

    def load(self, slot, quarter):
        for copy in self.copies(slot, quarter):
            copy.wait()
        bufs, flat = self.bufs, self.rows * self.part
        x = product(bufs[0, slot], bufs[1, slot]).astype(F32)
        c = product(bufs[2, slot], bufs[3, slot]).reshape(flat, self.length)
        c = dot(c, self.mirror, NN).reshape(x.shape)
        for eight in range(self.part // 8):
            span = slice(8 * eight, 8 * eight + 8)
            self.gs[slot, eight] = x[:, span].reshape(8 * self.rows, self.length)
            self.cs[slot, eight] = c[:, span].reshape(8 * self.rows, self.length)

    def reduce(self, slot, quarter, xc_ref, out_ref):
        zero = jnp.zeros(self.w_ref.shape[2:], BF16)
        for quad in range(self.part // 4):
            left, right = [], []
            for side in range(4):
                local = 4 * quad + side
                group = quarter * self.part + local
                where = pl.ds(local % 8, self.rows, stride=8)
                both = jnp.concatenate(
                    [ref[slot, local // 8, where, :] for ref in (self.gs, self.cs)], axis=0
                ).astype(BF16)
                xc_ref[local] = both
                w = [zero] * 8
                w[side], w[4 + side] = self.w_ref[group, 0], self.w_ref[group, 1]
                left.append(both)
                right.append(jnp.concatenate(w, axis=0))
            out_ref[quad] = dot(
                jnp.concatenate(left, axis=1), jnp.concatenate(right, axis=1), NT
            ).astype(BF16)


def states_kernel(dec_hbm, k_hbm, v_hbm, g_hbm, q_hbm, xc_ref, w_ref, rate_ref, *rest):
    outs, rest = rest[: PLANE - 1], rest[PLANE - 1 :]
    dec_ref, dec_sem, bufs, sems, gs, cs = rest
    place, _ = places()
    modes, groups = dec_ref.shape
    work = Reducer((k_hbm, v_hbm, g_hbm, q_hbm), bufs, sems, w_ref, gs, cs)
    length = work.length
    rates_in = pltpu.make_async_copy(dec_hbm, dec_ref, dec_sem)
    rates_in.start()
    for slot in range(PLANE - 1):
        for copy in work.copies(slot, place ^ (slot + 1)):
            copy.start()
    rates_in.wait()
    dec = dec_ref[...]
    behind = float(length) - lane_iota((modes, length)).astype(F32)
    wide = (modes, 8 * modes)
    target = lane_iota(wide) % (4 * modes) - lax.broadcasted_iota(jnp.int32, wide, 0)

    def weights(index, _):
        rates = jnp.zeros(wide, F32)
        for side in range(4):
            group = 4 * index + side
            rate = column(dec, group)
            basis = jnp.exp(-rate * behind)
            w_ref[group, 0] = basis.astype(BF16)
            w_ref[group, 1] = (behind * basis).astype(BF16)
            rates = jnp.where(target == side * modes, rate, rates)
        rate_ref[pl.ds(index, 1), :] = jnp.sum(rates, axis=0, keepdims=True)
        return 0

    lax.fori_loop(0, groups // 4, weights, 0, unroll=4)
    for slot in range(PLANE):
        if slot < PLANE - 1:
            work.load(slot, place ^ (slot + 1))
        if slot > 0:
            work.reduce(slot - 1, place ^ slot, xc_ref.at[slot - 1], outs[slot - 1])


def sums_kernel(k_hbm, v_hbm, g_hbm, q_hbm, xc_ref, w_ref, dec_ref, own_ref, out_ref, sums_ref, *rest):
    bufs, sems, gs, cs, corr_ref = rest
    place, _ = places()
    work = Reducer((k_hbm, v_hbm, g_hbm, q_hbm), bufs, sems, w_ref, gs, cs)
    for copy in work.copies(0, place):
        copy.start()
    _, part, rows, length = xc_ref.shape
    rows = rows // 2
    modes = dec_ref.shape[0]
    paired = (
        lane_iota((length, length)) + lax.broadcasted_iota(jnp.int32, (length, length), 0) < length
    )

    def correlate(ref, base):
        for local in range(part):
            prods = jnp.where(paired, dot(ref[local, :rows], ref[local, rows:], TN), 0.0)
            prods = pltpu.roll(prods, 0, 1, stride=1, stride_axis=0)
            corr_ref[pl.ds(base + local, 1), :] = jnp.sum(prods, axis=0, keepdims=True)

    def others(slot, _):
        correlate(xc_ref.at[slot], part * (place ^ (slot + 1)))
        return 0

    lax.fori_loop(0, PLANE - 1, others, 0)
    work.load(0, place)
    work.reduce(0, place, own_ref, out_ref)
    correlate(own_ref, part * place)
    dec = dec_ref[...]
    lag = float(length - 1) - lane_iota((modes, length)).astype(F32)
    lane = lane_iota((modes, sums_ref.shape[1]))

    def contract(quarter, carry):
        plain, moment = carry
        for local in range(part):
            group = quarter * part + local
            terms = jnp.exp(-column(dec, group) * lag) * corr_ref[pl.ds(group, 1), :]
            plain = jnp.where(lane == group, jnp.sum(terms, axis=1, keepdims=True), plain)
            moment = jnp.where(lane == group, jnp.sum(terms * lag, axis=1, keepdims=True), moment)
        return plain, moment

    zero = jnp.zeros(lane.shape, F32)
    plain, moment = lax.fori_loop(0, PLANE, contract, (zero, zero))
    sums_ref[:modes] = plain
    sums_ref[modes:] = moment


def local_kernel(own_ref, xc_ref, dec_ref, res_ref, after_ref, out_ref, taps_ref, toep_ref):
    _, part, rows, length = xc_ref.shape
    rows = rows // 2
    modes = dec_ref.shape[0]
    place, _ = places()
    dec, res = dec_ref[...], res_ref[...]
    ahead = lane_iota((modes, length)).astype(F32)
    later = lane_iota((length, length)) >= lax.broadcasted_iota(jnp.int32, (length, length), 0)
    mirror = mirror_of(length)

    def convolve(index, ref):
        for local in range(part):
            group = (place ^ index) * part + local
            rate, weight = column(dec, group), column(res, group)
            taps = weight * jnp.exp(-rate * ahead)
            taps_ref[index, local, 0] = taps.astype(BF16)
            back = weight * jnp.exp(-rate * (float(length - 1) - ahead))
            taps_ref[index, local, 1] = back.astype(BF16)
            taps = jnp.sum(taps, axis=0, keepdims=True)
            toep = pltpu.roll(
                jnp.broadcast_to(taps, (length, length)), 0, 1, stride=1, stride_axis=0
            )
            toep_ref[local] = jnp.where(later, toep, 0.0).astype(BF16)
        for local in range(part):
            toep = toep_ref[local]
            out_ref[index, local, :rows] = dot(ref[local, :rows], toep, NN)
            tokens = dot(ref[local, rows:], mirror, NN).astype(BF16)
            out_ref[index, local, rows:] = dot(tokens, toep, NT)

    convolve(0, own_ref)

    def others(index, _):
        convolve(index, xc_ref.at[index - 1])
        return 0

    lax.fori_loop(1, PLANE, others, 0)


def split_pair(x, half):
    head = x.astype(BF16).astype(F32)
    tail = (x - head).astype(BF16).astype(F32)
    low = lane_iota(x.shape) < half
    return jnp.where(low, head, pltpu.roll(jnp.where(low, tail, 0.0), half, x.ndim - 1)).astype(BF16)


def join_pair(x, half):
    x = x.astype(F32)
    low = lane_iota(x.shape) < half
    return jnp.where(low, x + pltpu.roll(x, half, x.ndim - 1), 0.0)


def in_order(arrays, place):
    arrays, bit = list(arrays), 1
    while bit < len(arrays):
        swap = (place & bit) != 0
        new = list(arrays)
        for i in range(len(arrays)):
            new[i] = jnp.where(swap, arrays[i ^ bit], arrays[i])
        arrays, bit = new, 2 * bit
    return arrays


def advance(state, decay, gap):
    half = state.shape[2] // 2
    shifted = pltpu.roll(state, half, 2)
    return decay * (state + jnp.where(lane_iota(state.shape) >= half, gap * shifted, 0.0))


def scan_blocks(heads, tails, start, rate, gap):
    decay = jnp.exp(-rate * gap)
    state, before = start[0], []
    for head in heads:
        before.append(state)
        state = advance(state, decay, gap) + head
    other, after = start[1], []
    for tail in tails[::-1]:
        after.insert(0, other)
        other = advance(other, decay, gap) + tail
    return before, after, state, other


def pair_terms(before, tails, rate):
    half = rate.shape[2] // 2
    plain, moment = 0.0, 0.0
    for state, tail in zip(before, tails, strict=True):
        plain = plain + state * tail
        moment = moment + state * pltpu.roll(tail, half, 2)
    plain, moment = jnp.sum(plain, axis=1), jnp.sum(moment, axis=1)
    moment = moment + pltpu.roll(moment, half, 1) - pltpu.roll(plain, half, 1)
    return jnp.where(lane_iota(plain.shape) < half, plain, moment) * jnp.exp(rate[:, 0])


def spread(terms, place, acc, modes):
    quads = terms.shape[0]
    shape = (quads, acc.shape[1])
    group = lane_iota(shape) - 4 * quads * place
    row = lax.broadcasted_iota(jnp.int32, shape, 0)
    for side in range(4):
        chosen = jnp.where(group == 4 * row + side, 1.0, 0.0)
        turned = lax.dot_general(
            terms, chosen, TN, precision=lax.Precision.HIGHEST, preferred_element_type=F32
        )
        acc[:modes] += turned[side * modes : (side + 1) * modes]
        acc[modes:] += turned[(4 + side) * modes : (5 + side) * modes]


def own_rates(rate_ref, place, quads):
    rate = rate_ref[pl.ds(place * quads, quads), :]
    return rate.reshape(quads, 1, rate.shape[1])


def halves(blocks, rows):
    return [b[:, :rows] for b in blocks], [b[:, rows:] for b in blocks]


def plane_kernel(length, rate_ref, *refs):
    *msgs, sums_ref, out_ref, acc = refs
    place, _ = places()
    quads, rows, lanes = msgs[0].shape
    rows, flat = rows // 2, quads * rows
    modes = lanes // 8
    heads, tails = halves(in_order([m[...].astype(F32) for m in msgs], place), rows)
    rate = own_rates(rate_ref, place, quads)
    nothing = jnp.zeros_like(heads[0])
    before, _, head, tail = scan_blocks(heads, tails, (nothing, nothing), rate, float(length))
    both = jnp.concatenate([head, tail], axis=1)
    out_ref[:flat] = both.astype(BF16).reshape(flat, lanes)
    acc[...] = sums_ref[...]
    spread(pair_terms(before, tails, rate), place, acc, modes)
    out_ref[flat:] = split_pair(acc[...], lanes // 2)


def line_kernel(length, rate_ref, after_ref, *refs):
    count = len(refs) - 2 * PLANE - 1
    msgs, lines = refs[:PLANE], refs[PLANE : PLANE + count]
    outs, acc = refs[PLANE + count : -1], refs[-1]
    place, level = places()
    quads, rows, lanes = msgs[0].shape
    shape = (quads, rows, lanes)
    rows, flat = rows // 2, quads * rows
    modes = lanes // 8
    rate = own_rates(rate_ref, place, quads)
    heads, tails = halves(
        in_order([r[:flat].astype(F32).reshape(shape) for r in lines], level), rows
    )
    nothing = jnp.zeros_like(heads[0])
    before, after, _, _ = scan_blocks(
        heads, tails, (nothing, nothing), rate, float(PLANE * length)
    )
    total = join_pair(lines[0][flat:], lanes // 2)
    for r in lines[1:]:
        total = total + join_pair(r[flat:], lanes // 2)
    acc[...] = total
    spread(pair_terms(before, tails, rate), place, acc, modes)
    sums = split_pair(acc[...], lanes // 2)
    start = [nothing, nothing]
    for i in range(count):
        start[0] = jnp.where(level == i, before[i], start[0])
        start[1] = jnp.where(level == i, after[i], start[1])
    heads, tails = halves(in_order([m[...].astype(F32) for m in msgs], place), rows)
    before, after, _, _ = scan_blocks(heads, tails, start, rate, float(length))
    found = [jnp.concatenate(pair, axis=1) for pair in zip(before, after, strict=True)]
    found = in_order(found, place)
    low = lane_iota((quads // 2,) + shape[1:]) < lanes // 2
    for i in range(PLANE):
        packed = jnp.where(low, found[i][: quads // 2], pltpu.roll(found[i][quads // 2 :], lanes // 2, 2))
        outs[i][: flat // 2] = packed.astype(BF16).reshape(flat // 2, lanes)
        outs[i][flat // 2 :] = sums


def outputs_kernel(indices, k_ref, v_ref, g_ref, near_ref, taps_ref, *refs):
    count = len(indices)
    states, refs = refs[:count], refs[count:]
    results, (outs, sems, cs, gs) = refs[-7:-4], refs[-4:]
    place, _ = places()
    _, _, rows, part, length = outs.shape
    modes = taps_ref.shape[3]
    quads = part // 4
    zero = jnp.zeros((modes, length), BF16)
    spans = [
        pl.ds(pl.multiple_of((place ^ index) * part, part), part) for index in indices
    ]

    def store(which, slot):
        return pltpu.make_async_copy(
            outs.at[which, slot], results[which].at[:, spans[slot], :], sems.at[which, slot]
        )

    def expand(slot):
        index, state_ref = indices[slot], states[slot]
        for local in range(part):
            quad, side = local // 4, local % 4
            base = side + (4 if quad >= quads // 2 else 0)
            first = (quad % (quads // 2)) * 2 * rows
            for half, ref in enumerate((cs, gs)):
                taps = jnp.concatenate(
                    [zero] * base + [taps_ref[index, local, half]] + [zero] * (7 - base), axis=0
                )
                where = slice(half * rows, (half + 1) * rows)
                state = state_ref[first + half * rows : first + (half + 1) * rows]
                ref[slot, local // 8, pl.ds(local % 8, rows, stride=8), :] = (
                    dot(state, taps, NN) + near_ref[index, local, where]
                )

    def finish(slot):
        conv, ig = (
            jnp.concatenate(
                [ref[slot, i].reshape(rows, 8, length) for i in range(part // 8)], axis=1
            ).astype(BF16)
            for ref in (cs, gs)
        )
        own = spans[slot]
        outs[0, slot] = product(g_ref[:, own, :], conv)
        outs[1, slot] = product(ig, v_ref[:, own, :])
        outs[2, slot] = product(ig, k_ref[:, own, :])
        for which in range(3):
            store(which, slot).start()

    for slot in range(count + 1):
        if slot < count:
            expand(slot)
        if slot > 0:
            finish(slot - 1)
    for slot in range(count):
        for which in range(3):
            store(which, slot).wait()


def gradients(queries, keys_in, values_in, grad_out, residue, decay_rate):
    chans, length = queries.shape
    groups, modes = residue.shape
    count = lax.axis_size("ctx")
    tp = lax.axis_size("tp")
    depth = count // PLANE
    rows = chans // groups
    part = groups // PLANE
    quads = part // 4
    lanes = 8 * modes

    def cube(x):
        return x.reshape(rows, groups, length)

    query, key, value, grad = cube(queries), cube(keys_in), cube(values_in), cube(grad_out)
    decay, resid = decay_rate.T, residue.T
    vmem = pl.BlockSpec(memory_space=pltpu.VMEM)
    anywhere = pl.BlockSpec(memory_space=pltpu.HBM)

    def shaped(shape, dtype):
        return jax.ShapeDtypeStruct(shape, dtype)

    def call(kernel, in_specs, out_specs, out_shape, scratch, flops, size, aliases=None):
        return pl.pallas_call(
            kernel,
            in_specs=in_specs,
            out_specs=out_specs,
            out_shape=out_shape,
            scratch_shapes=scratch,
            cost_estimate=pl.CostEstimate(flops=flops, bytes_accessed=size, transcendentals=0),
            compiler_params=pltpu.CompilerParams(vmem_limit_bytes=16 * 2**20),
            input_output_aliases=aliases or {},
        )

    def in_hbm(*arrays):
        return [pltpu.with_memory_space_constraint(x, pltpu.HBM) for x in arrays]

    def reducer(slots):
        return [
            pltpu.VMEM((4, slots, rows, part, length), BF16),
            pltpu.SemaphoreType.DMA((4, slots)),
        ] + [pltpu.VMEM((slots, part // 8, rows * 8, length), F32)] * 2

    quarter = (part, 2 * rows, length)
    block = shaped((quads, 2 * rows, lanes), BF16)
    xc, weights, rates, *own = call(
        states_kernel,
        [anywhere] * 5,
        [vmem] * (2 + PLANE),
        [
            shaped((PLANE - 1,) + quarter, BF16),
            shaped((groups, 2, modes, length), BF16),
            shaped((groups // 4, lanes), F32),
        ]
        + [block] * (PLANE - 1),
        [pltpu.VMEM((modes, groups), F32), pltpu.SemaphoreType.DMA] + reducer(PLANE - 1),
        10**9,
        4 * 10**6,
    )(*in_hbm(decay, key, value, grad, query))

    def swap(x, bits):
        return lax.ppermute(x, "ctx", [(i, i ^ bits) for i in range(count)])

    near = [swap(own[i - 1], i) for i in range(1, PLANE)]
    xo, mine, sums = call(
        sums_kernel,
        [anywhere] * 4 + [vmem] * 3,
        [vmem] * 3,
        [shaped(quarter, BF16), block, shaped((2 * modes, lanes), F32)],
        reducer(1) + [pltpu.VMEM((groups, length), F32)],
        10**9,
        4 * 10**6,
    )(*in_hbm(key, value, grad, query), xc, weights, decay)
    near = [mine] + near
    flat = quads * 2 * rows
    plane = call(
        functools.partial(plane_kernel, length),
        [vmem] * (2 + PLANE),
        vmem,
        shaped((flat + 2 * modes, lanes), BF16),
        [pltpu.VMEM((2 * modes, lanes), F32)],
        10**7,
        10**6,
    )(rates, *near, sums)
    line = [plane] + [swap(plane, PLANE * i) for i in range(1, depth)]
    near_part, taps = call(
        local_kernel,
        [vmem] * 5,
        [vmem] * 2,
        [
            shaped((PLANE,) + quarter, F32),
            shaped((PLANE, part, 2, modes, length), BF16),
        ],
        [pltpu.VMEM((part, length, length), BF16)],
        10**9,
        4 * 10**6,
    )(xo, xc, decay, resid, plane)
    sent = call(
        functools.partial(line_kernel, length),
        [vmem] * (2 + PLANE + depth),
        [vmem] * PLANE,
        [shaped((flat // 2 + 2 * modes, lanes), BF16)] * PLANE,
        [pltpu.VMEM((2 * modes, lanes), F32)],
        10**7,
        10**6,
    )(rates, taps, *near, *line)
    back = [sent[0]]
    for i in range(1, PLANE):
        back.append(swap(sent[i], i))

    total = sum(
        b[flat // 2 :, : lanes // 2].astype(F32) + b[flat // 2 :, lanes // 2 :].astype(F32)
        for b in back
    )
    bit = 1
    while bit < tp:
        total = total + lax.ppermute(total, "tp", [(i, i ^ bit) for i in range(tp)])
        bit *= 2

    outs = ()
    for indices in ((0,), tuple(range(1, PLANE - 1)), (PLANE - 1,)):
        slots = len(indices)
        outs = call(
            functools.partial(outputs_kernel, indices),
            [vmem] * (5 + slots) + [anywhere] * len(outs),
            [anywhere] * 3,
            [shaped((rows, groups, length), BF16)] * 3,
            [
                pltpu.VMEM((3, slots, rows, part, length), BF16),
                pltpu.SemaphoreType.DMA((3, slots)),
                pltpu.VMEM((slots, part // 8, rows * 8, length), F32),
                pltpu.VMEM((slots, part // 8, rows * 8, length), F32),
            ],
            2 * 10**8 * slots,
            10**6 * slots,
            {5 + slots + i: i for i in range(len(outs))},
        )(key, value, grad, near_part, taps, *(back[i] for i in indices), *outs)
    tokens = count * length
    plain, moment = total[:modes, :groups], total[modes:, :groups]
    return (
        *(x.reshape(chans, length) for x in outs),
        (plain / tokens).T,
        (-(resid * decay) * moment / tokens).T,
    )


def solution(mesh):
    in_specs = (P("tp", "ctx"), P("tp", "ctx"), P("tp", "ctx"), P("tp", "ctx"), P(), P())
    out_specs = (P("tp", "ctx"), P("tp", "ctx"), P("tp", "ctx"), P(), P())
    return jax.shard_map(
        gradients, mesh=mesh, in_specs=in_specs, out_specs=out_specs, check_vma=False
    )
```

```python
import functools

import jax
import jax.numpy as jnp
from jax import lax
from jax.experimental import pallas as pl
from jax.experimental.pallas import tpu as pltpu
from jax.sharding import PartitionSpec as P

F32 = jnp.float32
BF16 = jnp.bfloat16
PLANE = 4
NT = (((1,), (1,)), ((), ()))
NN = (((1,), (0,)), ((), ()))
TN = (((0,), (0,)), ((), ()))


def dot(a, b, dims):
    return lax.dot_general(a, b, dims, preferred_element_type=F32)


def product(a, b):
    return (a.astype(F32) * b.astype(F32)).astype(BF16)


def column(table, group):
    return jnp.sum(jnp.where(lane_iota(table.shape) == group, table, 0.0), axis=1, keepdims=True)


def mirror_of(length):
    total = lane_iota((length, length)) + lax.broadcasted_iota(jnp.int32, (length, length), 0)
    return jnp.where(total == length - 1, 1.0, 0.0).astype(BF16)


def places():
    me = lax.axis_index("ctx")
    return lax.rem(me, PLANE), lax.div(me, PLANE)


def lane_iota(shape):
    return lax.broadcasted_iota(jnp.int32, shape, len(shape) - 1)


class Reducer:
    def __init__(self, sources, bufs, sems, w_ref, gs, cs):
        self.sources, self.bufs, self.sems, self.w_ref, self.gs, self.cs = (
            sources, bufs, sems, w_ref, gs, cs
        )
        _, self.rows, self.part, self.length = bufs.shape[1:]
        self.mirror = mirror_of(self.length)

    def copies(self, slot, quarter):
        return [
            pltpu.make_async_copy(
                source.at[:, pl.ds(pl.multiple_of(quarter * self.part, self.part), self.part), :],
                self.bufs.at[which, slot],
                self.sems.at[which, slot],
            )
            for which, source in enumerate(self.sources)
        ]

    def load(self, slot, quarter):
        for copy in self.copies(slot, quarter):
            copy.wait()
        bufs, flat = self.bufs, self.rows * self.part
        x = product(bufs[0, slot], bufs[1, slot]).astype(F32)
        c = product(bufs[2, slot], bufs[3, slot]).reshape(flat, self.length)
        c = dot(c, self.mirror, NN).reshape(x.shape)
        for eight in range(self.part // 8):
            span = slice(8 * eight, 8 * eight + 8)
            self.gs[slot, eight] = x[:, span].reshape(8 * self.rows, self.length)
            self.cs[slot, eight] = c[:, span].reshape(8 * self.rows, self.length)

    def reduce(self, slot, quarter, xc_ref, out_ref):
        zero = jnp.zeros(self.w_ref.shape[2:], BF16)
        for quad in range(self.part // 4):
            left, right = [], []
            for side in range(4):
                local = 4 * quad + side
                group = quarter * self.part + local
                where = pl.ds(local % 8, self.rows, stride=8)
                both = jnp.concatenate(
                    [ref[slot, local // 8, where, :] for ref in (self.gs, self.cs)], axis=0
                ).astype(BF16)
                xc_ref[local] = both
                w = [zero] * 8
                w[side], w[4 + side] = self.w_ref[group, 0], self.w_ref[group, 1]
                left.append(both)
                right.append(jnp.concatenate(w, axis=0))
            out_ref[quad] = dot(
                jnp.concatenate(left, axis=1), jnp.concatenate(right, axis=1), NT
            ).astype(BF16)


def states_kernel(dec_hbm, k_hbm, v_hbm, g_hbm, q_hbm, xc_ref, w_ref, rate_ref, *rest):
    outs, rest = rest[: PLANE - 1], rest[PLANE - 1 :]
    dec_ref, dec_sem, bufs, sems, gs, cs = rest
    place, _ = places()
    modes, groups = dec_ref.shape
    work = Reducer((k_hbm, v_hbm, g_hbm, q_hbm), bufs, sems, w_ref, gs, cs)
    length = work.length
    rates_in = pltpu.make_async_copy(dec_hbm, dec_ref, dec_sem)
    rates_in.start()
    for slot in range(PLANE - 1):
        for copy in work.copies(slot, place ^ (slot + 1)):
            copy.start()
    rates_in.wait()
    dec = dec_ref[...]
    behind = float(length) - lane_iota((modes, length)).astype(F32)
    wide = (modes, 8 * modes)
    target = lane_iota(wide) % (4 * modes) - lax.broadcasted_iota(jnp.int32, wide, 0)

    def weights(index, _):
        rates = jnp.zeros(wide, F32)
        for side in range(4):
            group = 4 * index + side
            rate = column(dec, group)
            basis = jnp.exp(-rate * behind)
            w_ref[group, 0] = basis.astype(BF16)
            w_ref[group, 1] = (behind * basis).astype(BF16)
            rates = jnp.where(target == side * modes, rate, rates)
        rate_ref[pl.ds(index, 1), :] = jnp.sum(rates, axis=0, keepdims=True)
        return 0

    lax.fori_loop(0, groups // 4, weights, 0, unroll=4)
    for slot in range(PLANE):
        if slot < PLANE - 1:
            work.load(slot, place ^ (slot + 1))
        if slot > 0:
            work.reduce(slot - 1, place ^ slot, xc_ref.at[slot - 1], outs[slot - 1])


def sums_kernel(k_hbm, v_hbm, g_hbm, q_hbm, xc_ref, w_ref, dec_ref, own_ref, out_ref, sums_ref, *rest):
    bufs, sems, gs, cs, corr_ref = rest
    place, _ = places()
    work = Reducer((k_hbm, v_hbm, g_hbm, q_hbm), bufs, sems, w_ref, gs, cs)
    for copy in work.copies(0, place):
        copy.start()
    _, part, rows, length = xc_ref.shape
    rows = rows // 2
    modes = dec_ref.shape[0]
    paired = (
        lane_iota((length, length)) + lax.broadcasted_iota(jnp.int32, (length, length), 0) < length
    )

    def correlate(ref, base):
        for local in range(part):
            prods = jnp.where(paired, dot(ref[local, :rows], ref[local, rows:], TN), 0.0)
            prods = pltpu.roll(prods, 0, 1, stride=1, stride_axis=0)
            corr_ref[pl.ds(base + local, 1), :] = jnp.sum(prods, axis=0, keepdims=True)

    def others(slot, _):
        correlate(xc_ref.at[slot], part * (place ^ (slot + 1)))
        return 0

    lax.fori_loop(0, PLANE - 1, others, 0)
    work.load(0, place)
    work.reduce(0, place, own_ref, out_ref)
    correlate(own_ref, part * place)
    dec = dec_ref[...]
    lag = float(length - 1) - lane_iota((modes, length)).astype(F32)
    lane = lane_iota((modes, sums_ref.shape[1]))

    def contract(quarter, carry):
        plain, moment = carry
        for local in range(part):
            group = quarter * part + local
            terms = jnp.exp(-column(dec, group) * lag) * corr_ref[pl.ds(group, 1), :]
            plain = jnp.where(lane == group, jnp.sum(terms, axis=1, keepdims=True), plain)
            moment = jnp.where(lane == group, jnp.sum(terms * lag, axis=1, keepdims=True), moment)
        return plain, moment

    zero = jnp.zeros(lane.shape, F32)
    plain, moment = lax.fori_loop(0, PLANE, contract, (zero, zero))
    sums_ref[:modes] = plain
    sums_ref[modes:] = moment


def local_kernel(own_ref, xc_ref, dec_ref, res_ref, after_ref, out_ref, taps_ref, *scratch):
    toep_ref, rows_ref, bands_ref = scratch
    _, part, _, length = xc_ref.shape
    modes = dec_ref.shape[0]
    place, _ = places()
    dec, res = dec_ref[...], res_ref[...]
    ahead = lane_iota((modes, length)).astype(F32)
    step = 16
    lane = lane_iota((step, length))
    row = lax.broadcasted_iota(jnp.int32, (step, length), 0)

    def each(body):
        def run(index, _):
            body(index)
            return 0

        lax.fori_loop(0, PLANE, run, 0)

    @each
    def _(index):
        first_group = (place ^ index) * part
        for local in range(part):
            rate, weight = column(dec, first_group + local), column(res, first_group + local)
            taps = weight * jnp.exp(-rate * ahead)
            taps_ref[index, local] = taps.astype(BF16)
            rows_ref[index, local : local + 1] = jnp.sum(taps, axis=0, keepdims=True)

    @each
    def _(index):
        for local in range(part):
            taps = jnp.broadcast_to(rows_ref[index, local : local + 1], (step, length))
            bands_ref[index, local] = pltpu.roll(taps, 0, 1, stride=1, stride_axis=0).astype(BF16)

    @each
    def _(index):
        for local in range(part):
            band = bands_ref[index, local]
            for first in range(0, length, step):
                toep_ref[index, local, first : first + step] = jnp.where(
                    lane >= row + first, pltpu.roll(band, first, 1), 0.0
                )

    def convolve(index, ref):
        for local in range(part):
            out_ref[index, local] = dot(ref[local], toep_ref[index, local], NN)

    convolve(0, own_ref)

    def others(index, _):
        convolve(index, xc_ref.at[index - 1])
        return 0

    lax.fori_loop(1, PLANE, others, 0)


def split_pair(x, half):
    head = x.astype(BF16).astype(F32)
    tail = (x - head).astype(BF16).astype(F32)
    low = lane_iota(x.shape) < half
    return jnp.where(low, head, pltpu.roll(jnp.where(low, tail, 0.0), half, x.ndim - 1)).astype(BF16)


def join_pair(x, half):
    x = x.astype(F32)
    low = lane_iota(x.shape) < half
    return jnp.where(low, x + pltpu.roll(x, half, x.ndim - 1), 0.0)


def in_order(arrays, place):
    arrays, bit = list(arrays), 1
    while bit < len(arrays):
        swap = (place & bit) != 0
        new = list(arrays)
        for i in range(len(arrays)):
            new[i] = jnp.where(swap, arrays[i ^ bit], arrays[i])
        arrays, bit = new, 2 * bit
    return arrays


def advance(state, decay, gap):
    half = state.shape[2] // 2
    shifted = pltpu.roll(state, half, 2)
    return decay * (state + jnp.where(lane_iota(state.shape) >= half, gap * shifted, 0.0))


def scan_blocks(heads, tails, start, rate, gap):
    decay = jnp.exp(-rate * gap)
    state, before = start[0], []
    for head in heads:
        before.append(state)
        state = advance(state, decay, gap) + head
    other, after = start[1], []
    for tail in tails[::-1]:
        after.insert(0, other)
        other = advance(other, decay, gap) + tail
    return before, after, state, other


def pair_terms(before, tails, rate):
    half = rate.shape[2] // 2
    plain, moment = 0.0, 0.0
    for state, tail in zip(before, tails, strict=True):
        plain = plain + state * tail
        moment = moment + state * pltpu.roll(tail, half, 2)
    plain, moment = jnp.sum(plain, axis=1), jnp.sum(moment, axis=1)
    moment = moment + pltpu.roll(moment, half, 1) - pltpu.roll(plain, half, 1)
    return jnp.where(lane_iota(plain.shape) < half, plain, moment) * jnp.exp(rate[:, 0])


def spread(terms, place, acc, modes):
    quads = terms.shape[0]
    shape = (quads, acc.shape[1])
    group = lane_iota(shape) - 4 * quads * place
    row = lax.broadcasted_iota(jnp.int32, shape, 0)
    for side in range(4):
        chosen = jnp.where(group == 4 * row + side, 1.0, 0.0)
        turned = lax.dot_general(
            terms, chosen, TN, precision=lax.Precision.HIGHEST, preferred_element_type=F32
        )
        acc[:modes] += turned[side * modes : (side + 1) * modes]
        acc[modes:] += turned[(4 + side) * modes : (5 + side) * modes]


def own_rates(rate_ref, place, quads):
    rate = rate_ref[pl.ds(place * quads, quads), :]
    return rate.reshape(quads, 1, rate.shape[1])


def halves(blocks, rows):
    return [b[:, :rows] for b in blocks], [b[:, rows:] for b in blocks]


def plane_kernel(length, rate_ref, *refs):
    *msgs, sums_ref, out_ref, acc = refs
    place, _ = places()
    quads, rows, lanes = msgs[0].shape
    rows, flat = rows // 2, quads * rows
    modes = lanes // 8
    heads, tails = halves(in_order([m[...].astype(F32) for m in msgs], place), rows)
    rate = own_rates(rate_ref, place, quads)
    nothing = jnp.zeros_like(heads[0])
    before, _, head, tail = scan_blocks(heads, tails, (nothing, nothing), rate, float(length))
    both = jnp.concatenate([head, tail], axis=1)
    out_ref[:flat] = both.astype(BF16).reshape(flat, lanes)
    acc[...] = sums_ref[...]
    spread(pair_terms(before, tails, rate), place, acc, modes)
    out_ref[flat:] = split_pair(acc[...], lanes // 2)


def line_kernel(length, rate_ref, after_ref, *refs):
    count = len(refs) - 2 * PLANE - 1
    msgs, lines = refs[:PLANE], refs[PLANE : PLANE + count]
    outs, acc = refs[PLANE + count : -1], refs[-1]
    place, level = places()
    quads, rows, lanes = msgs[0].shape
    shape = (quads, rows, lanes)
    rows, flat = rows // 2, quads * rows
    modes = lanes // 8
    rate = own_rates(rate_ref, place, quads)
    heads, tails = halves(
        in_order([r[:flat].astype(F32).reshape(shape) for r in lines], level), rows
    )
    nothing = jnp.zeros_like(heads[0])
    before, after, _, _ = scan_blocks(
        heads, tails, (nothing, nothing), rate, float(PLANE * length)
    )
    total = join_pair(lines[0][flat:], lanes // 2)
    for r in lines[1:]:
        total = total + join_pair(r[flat:], lanes // 2)
    acc[...] = total
    spread(pair_terms(before, tails, rate), place, acc, modes)
    sums = split_pair(acc[...], lanes // 2)
    start = [nothing, nothing]
    for i in range(count):
        start[0] = jnp.where(level == i, before[i], start[0])
        start[1] = jnp.where(level == i, after[i], start[1])
    heads, tails = halves(in_order([m[...].astype(F32) for m in msgs], place), rows)
    before, after, _, _ = scan_blocks(heads, tails, start, rate, float(length))
    found = [jnp.concatenate(pair, axis=1) for pair in zip(before, after, strict=True)]
    found = in_order(found, place)
    low = lane_iota((quads // 2,) + shape[1:]) < lanes // 2
    for i in range(PLANE):
        packed = jnp.where(low, found[i][: quads // 2], pltpu.roll(found[i][quads // 2 :], lanes // 2, 2))
        outs[i][: flat // 2] = packed.astype(BF16).reshape(flat // 2, lanes)
        outs[i][flat // 2 :] = sums


def outputs_kernel(indices, k_ref, v_ref, g_ref, near_ref, taps_ref, *refs):
    count = len(indices)
    states, refs = refs[:count], refs[count:]
    results, (outs, sems, cs, gs) = refs[-7:-4], refs[-4:]
    place, _ = places()
    _, _, rows, part, length = outs.shape
    modes = taps_ref.shape[2]
    quads = part // 4
    mirror = mirror_of(length)
    zero = jnp.zeros((modes, length), BF16)
    spans = [
        pl.ds(pl.multiple_of((place ^ index) * part, part), part) for index in indices
    ]

    def store(which, slot):
        return pltpu.make_async_copy(
            outs.at[which, slot], results[which].at[:, spans[slot], :], sems.at[which, slot]
        )

    def expand(slot):
        index, state_ref = indices[slot], states[slot]
        for local in range(part):
            quad, side = local // 4, local % 4
            base = side + (4 if quad >= quads // 2 else 0)
            first = (quad % (quads // 2)) * 2 * rows
            taps = jnp.concatenate(
                [zero] * base + [taps_ref[index, local]] + [zero] * (7 - base), axis=0
            )
            both = dot(state_ref[first : first + 2 * rows], taps, NN) + near_ref[index, local]
            where = pl.ds(local % 8, rows, stride=8)
            cs[slot, local // 8, where, :] = both[:rows]
            gs[slot, local // 8, where, :] = both[rows:]

    def finish(slot):
        conv, ig = (
            jnp.concatenate(
                [ref[slot, i].reshape(rows, 8, length) for i in range(part // 8)], axis=1
            ).astype(BF16)
            for ref in (cs, gs)
        )
        own = spans[slot]
        outs[0, slot] = product(g_ref[:, own, :], conv)
        ig = dot(ig.reshape(rows * part, length), mirror, NN).reshape(conv.shape)
        outs[1, slot] = product(ig, v_ref[:, own, :])
        outs[2, slot] = product(ig, k_ref[:, own, :])
        for which in range(3):
            store(which, slot).start()

    for slot in range(count + 1):
        if slot < count:
            expand(slot)
        if slot > 0:
            finish(slot - 1)
    for slot in range(count):
        for which in range(3):
            store(which, slot).wait()


def gradients(queries, keys_in, values_in, grad_out, residue, decay_rate):
    chans, length = queries.shape
    groups, modes = residue.shape
    count = lax.axis_size("ctx")
    tp = lax.axis_size("tp")
    depth = count // PLANE
    rows = chans // groups
    part = groups // PLANE
    quads = part // 4
    lanes = 8 * modes

    def cube(x):
        return x.reshape(rows, groups, length)

    query, key, value, grad = cube(queries), cube(keys_in), cube(values_in), cube(grad_out)
    decay, resid = decay_rate.T, residue.T
    vmem = pl.BlockSpec(memory_space=pltpu.VMEM)
    anywhere = pl.BlockSpec(memory_space=pltpu.HBM)

    def shaped(shape, dtype):
        return jax.ShapeDtypeStruct(shape, dtype)

    def call(kernel, in_specs, out_specs, out_shape, scratch, flops, size, aliases=None):
        return pl.pallas_call(
            kernel,
            in_specs=in_specs,
            out_specs=out_specs,
            out_shape=out_shape,
            scratch_shapes=scratch,
            cost_estimate=pl.CostEstimate(flops=flops, bytes_accessed=size, transcendentals=0),
            compiler_params=pltpu.CompilerParams(vmem_limit_bytes=16 * 2**20),
            input_output_aliases=aliases or {},
        )

    def in_hbm(*arrays):
        return [pltpu.with_memory_space_constraint(x, pltpu.HBM) for x in arrays]

    def reducer(slots):
        return [
            pltpu.VMEM((4, slots, rows, part, length), BF16),
            pltpu.SemaphoreType.DMA((4, slots)),
        ] + [pltpu.VMEM((slots, part // 8, rows * 8, length), F32)] * 2

    quarter = (part, 2 * rows, length)
    block = shaped((quads, 2 * rows, lanes), BF16)
    xc, weights, rates, *own = call(
        states_kernel,
        [anywhere] * 5,
        [vmem] * (2 + PLANE),
        [
            shaped((PLANE - 1,) + quarter, BF16),
            shaped((groups, 2, modes, length), BF16),
            shaped((groups // 4, lanes), F32),
        ]
        + [block] * (PLANE - 1),
        [pltpu.VMEM((modes, groups), F32), pltpu.SemaphoreType.DMA] + reducer(PLANE - 1),
        10**9,
        4 * 10**6,
    )(*in_hbm(decay, key, value, grad, query))

    def swap(x, bits):
        return lax.ppermute(x, "ctx", [(i, i ^ bits) for i in range(count)])

    near = [swap(own[i - 1], i) for i in range(1, PLANE)]
    xo, mine, sums = call(
        sums_kernel,
        [anywhere] * 4 + [vmem] * 3,
        [vmem] * 3,
        [shaped(quarter, BF16), block, shaped((2 * modes, lanes), F32)],
        reducer(1) + [pltpu.VMEM((groups, length), F32)],
        10**9,
        4 * 10**6,
    )(*in_hbm(key, value, grad, query), xc, weights, decay)
    near = [mine] + near
    flat = quads * 2 * rows
    plane = call(
        functools.partial(plane_kernel, length),
        [vmem] * (2 + PLANE),
        vmem,
        shaped((flat + 2 * modes, lanes), BF16),
        [pltpu.VMEM((2 * modes, lanes), F32)],
        10**7,
        10**6,
    )(rates, *near, sums)
    line = [plane] + [swap(plane, PLANE * i) for i in range(1, depth)]
    near_part, taps = call(
        local_kernel,
        [vmem] * 5,
        [vmem] * 2,
        [
            shaped((PLANE,) + quarter, F32),
            shaped((PLANE, part, modes, length), BF16),
        ],
        [
            pltpu.VMEM((PLANE, part, length, length), BF16),
            pltpu.VMEM((PLANE, part, length), F32),
            pltpu.VMEM((PLANE, part, 16, length), BF16),
        ],
        10**9,
        4 * 10**6,
    )(xo, xc, decay, resid, plane)
    sent = call(
        functools.partial(line_kernel, length),
        [vmem] * (2 + PLANE + depth),
        [vmem] * PLANE,
        [shaped((flat // 2 + 2 * modes, lanes), BF16)] * PLANE,
        [pltpu.VMEM((2 * modes, lanes), F32)],
        10**7,
        10**6,
    )(rates, taps, *near, *line)
    back = [sent[0]]
    for i in range(1, PLANE):
        back.append(swap(sent[i], i))

    total = sum(
        b[flat // 2 :, : lanes // 2].astype(F32) + b[flat // 2 :, lanes // 2 :].astype(F32)
        for b in back
    )
    bit = 1
    while bit < tp:
        total = total + lax.ppermute(total, "tp", [(i, i ^ bit) for i in range(tp)])
        bit *= 2

    outs = ()
    for indices in ((0,), tuple(range(1, PLANE - 1)), (PLANE - 1,)):
        slots = len(indices)
        outs = call(
            functools.partial(outputs_kernel, indices),
            [vmem] * (5 + slots) + [anywhere] * len(outs),
            [anywhere] * 3,
            [shaped((rows, groups, length), BF16)] * 3,
            [
                pltpu.VMEM((3, slots, rows, part, length), BF16),
                pltpu.SemaphoreType.DMA((3, slots)),
                pltpu.VMEM((slots, part // 8, rows * 8, length), F32),
                pltpu.VMEM((slots, part // 8, rows * 8, length), F32),
            ],
            2 * 10**8 * slots,
            10**6 * slots,
            {5 + slots + i: i for i in range(len(outs))},
        )(key, value, grad, near_part, taps, *(back[i] for i in indices), *outs)
    tokens = count * length
    plain, moment = total[:modes, :groups], total[modes:, :groups]
    return (
        *(x.reshape(chans, length) for x in outs),
        (plain / tokens).T,
        (-(resid * decay) * moment / tokens).T,
    )


def solution(mesh):
    in_specs = (P("tp", "ctx"), P("tp", "ctx"), P("tp", "ctx"), P("tp", "ctx"), P(), P())
    out_specs = (P("tp", "ctx"), P("tp", "ctx"), P("tp", "ctx"), P(), P())
    return jax.shard_map(
        gradients, mesh=mesh, in_specs=in_specs, out_specs=out_specs, check_vma=False
    )
```

```python
import functools

import jax
import jax.numpy as jnp
from jax import lax
from jax.experimental import pallas as pl
from jax.experimental.pallas import tpu as pltpu
from jax.sharding import PartitionSpec as P

F32 = jnp.float32
BF16 = jnp.bfloat16
PLANE = 4
NT = (((1,), (1,)), ((), ()))
NN = (((1,), (0,)), ((), ()))
TN = (((0,), (0,)), ((), ()))


def dot(a, b, dims):
    return lax.dot_general(a, b, dims, preferred_element_type=F32)


def product(a, b):
    return a.astype(BF16) * b.astype(BF16)


def column(table, group):
    return jnp.sum(jnp.where(lane_iota(table.shape) == group, table, 0.0), axis=1, keepdims=True)


def mirror_of(length):
    total = lane_iota((length, length)) + lax.broadcasted_iota(jnp.int32, (length, length), 0)
    return jnp.where(total == length - 1, 1.0, 0.0).astype(BF16)


def places():
    me = lax.axis_index("ctx")
    return lax.rem(me, PLANE), lax.div(me, PLANE)


def lane_iota(shape):
    return lax.broadcasted_iota(jnp.int32, shape, len(shape) - 1)


class Reducer:
    def __init__(self, sources, bufs, sems, w_ref, gs, cs):
        self.sources, self.bufs, self.sems, self.w_ref, self.gs, self.cs = (
            sources, bufs, sems, w_ref, gs, cs
        )
        _, self.rows, self.part, self.length = bufs.shape[1:]
        self.mirror = mirror_of(self.length)

    def copies(self, slot, quarter):
        return [
            pltpu.make_async_copy(
                source.at[:, pl.ds(pl.multiple_of(quarter * self.part, self.part), self.part), :],
                self.bufs.at[which, slot],
                self.sems.at[which, slot],
            )
            for which, source in enumerate(self.sources)
        ]

    def load(self, slot, quarter):
        for copy in self.copies(slot, quarter):
            copy.wait()
        bufs, flat = self.bufs, self.rows * self.part
        x = product(bufs[0, slot], bufs[1, slot]).astype(F32)
        c = product(bufs[2, slot], bufs[3, slot]).reshape(flat, self.length)
        c = dot(c, self.mirror, NN).reshape(x.shape)
        for eight in range(self.part // 8):
            span = slice(8 * eight, 8 * eight + 8)
            self.gs[slot, eight] = x[:, span].reshape(8 * self.rows, self.length)
            self.cs[slot, eight] = c[:, span].reshape(8 * self.rows, self.length)

    def reduce(self, slot, quarter, xc_ref, out_ref):
        modes = self.w_ref.shape[2]
        lane = lane_iota((2 * self.rows, 8 * modes)) % (4 * modes)
        for quad in range(self.part // 4):
            left, right = [], [[], []]
            for side in range(4):
                local = 4 * quad + side
                group = quarter * self.part + local
                where = pl.ds(local % 8, self.rows, stride=8)
                both = jnp.concatenate(
                    [ref[slot, local // 8, where, :] for ref in (self.gs, self.cs)], axis=0
                ).astype(BF16)
                xc_ref[local] = both
                left.append(both)
                right[0].append(self.w_ref[group, 0])
                right[1].append(self.w_ref[group, 1])
            every = dot(
                jnp.concatenate(left, axis=0), jnp.concatenate(right[0] + right[1], axis=0), NT
            )
            every = every.reshape(4, 2 * self.rows, 8 * modes)
            found = every[0]
            for side in range(1, 4):
                found = jnp.where(lane >= side * modes, every[side], found)
            out_ref[quad] = found.astype(BF16)


def states_kernel(dec_hbm, k_hbm, v_hbm, g_hbm, q_hbm, xc_ref, w_ref, rate_ref, *rest):
    outs, rest = rest[: PLANE - 1], rest[PLANE - 1 :]
    dec_ref, dec_sem, bufs, sems, gs, cs = rest
    place, _ = places()
    modes, groups = dec_ref.shape
    work = Reducer((k_hbm, v_hbm, g_hbm, q_hbm), bufs, sems, w_ref, gs, cs)
    length = work.length
    rates_in = pltpu.make_async_copy(dec_hbm, dec_ref, dec_sem)
    rates_in.start()
    for slot in range(PLANE - 1):
        for copy in work.copies(slot, place ^ (slot + 1)):
            copy.start()
    rates_in.wait()
    dec = dec_ref[...]
    behind = float(length) - lane_iota((modes, length)).astype(F32)
    wide = (modes, 8 * modes)
    target = lane_iota(wide) % (4 * modes) - lax.broadcasted_iota(jnp.int32, wide, 0)

    def weights(index, _):
        rates = jnp.zeros(wide, F32)
        for side in range(4):
            group = 4 * index + side
            rate = column(dec, group)
            basis = jnp.exp(-rate * behind)
            w_ref[group, 0] = basis.astype(BF16)
            w_ref[group, 1] = (behind * basis).astype(BF16)
            rates = jnp.where(target == side * modes, rate, rates)
        rate_ref[pl.ds(index, 1), :] = jnp.sum(rates, axis=0, keepdims=True)
        return 0

    lax.fori_loop(0, groups // 4, weights, 0, unroll=4)
    for slot in range(PLANE):
        if slot < PLANE - 1:
            work.load(slot, place ^ (slot + 1))
        if slot > 0:
            work.reduce(slot - 1, place ^ slot, xc_ref.at[slot - 1], outs[slot - 1])


def sums_kernel(k_hbm, v_hbm, g_hbm, q_hbm, xc_ref, w_ref, dec_ref, own_ref, out_ref, sums_ref, *rest):
    bufs, sems, gs, cs, corr_ref = rest
    place, _ = places()
    work = Reducer((k_hbm, v_hbm, g_hbm, q_hbm), bufs, sems, w_ref, gs, cs)
    for copy in work.copies(0, place):
        copy.start()
    _, part, rows, length = xc_ref.shape
    rows = rows // 2
    modes = dec_ref.shape[0]
    paired = (
        lane_iota((length, length)) + lax.broadcasted_iota(jnp.int32, (length, length), 0) < length
    )

    def correlate(ref, base):
        for local in range(part):
            prods = jnp.where(paired, dot(ref[local, :rows], ref[local, rows:], TN), 0.0)
            prods = pltpu.roll(prods, 0, 1, stride=1, stride_axis=0)
            corr_ref[pl.ds(base + local, 1), :] = jnp.sum(prods, axis=0, keepdims=True)

    def others(slot, _):
        correlate(xc_ref.at[slot], part * (place ^ (slot + 1)))
        return 0

    lax.fori_loop(0, PLANE - 1, others, 0)
    work.load(0, place)
    work.reduce(0, place, own_ref, out_ref)
    correlate(own_ref, part * place)
    dec = dec_ref[...]
    lag = float(length - 1) - lane_iota((modes, length)).astype(F32)
    lane = lane_iota((modes, sums_ref.shape[1]))

    def contract(quarter, carry):
        plain, moment = carry
        for local in range(part):
            group = quarter * part + local
            terms = jnp.exp(-column(dec, group) * lag) * corr_ref[pl.ds(group, 1), :]
            plain = jnp.where(lane == group, jnp.sum(terms, axis=1, keepdims=True), plain)
            moment = jnp.where(lane == group, jnp.sum(terms * lag, axis=1, keepdims=True), moment)
        return plain, moment

    zero = jnp.zeros(lane.shape, F32)
    plain, moment = lax.fori_loop(0, PLANE, contract, (zero, zero))
    sums_ref[:modes] = plain
    sums_ref[modes:] = moment


def local_kernel(own_ref, xc_ref, dec_ref, res_ref, after_ref, out_ref, taps_ref, *scratch):
    toep_ref, rows_ref, bands_ref = scratch
    _, part, _, length = xc_ref.shape
    modes = dec_ref.shape[0]
    place, _ = places()
    dec, res = dec_ref[...], res_ref[...]
    ahead = lane_iota((modes, length)).astype(F32)
    step = 16
    lane = lane_iota((step, length))
    row = lax.broadcasted_iota(jnp.int32, (step, length), 0)

    def each(body):
        def run(index, _):
            body(index)
            return 0

        lax.fori_loop(0, PLANE, run, 0)

    @each
    def _(index):
        first_group = (place ^ index) * part
        for local in range(part):
            rate, weight = column(dec, first_group + local), column(res, first_group + local)
            taps = weight * jnp.exp(-rate * ahead)
            taps_ref[index, local] = taps.astype(BF16)
            rows_ref[index, local : local + 1] = jnp.sum(taps, axis=0, keepdims=True)

    @each
    def _(index):
        for local in range(part):
            taps = jnp.broadcast_to(rows_ref[index, local : local + 1], (step, length))
            bands_ref[index, local] = pltpu.roll(taps, 0, 1, stride=1, stride_axis=0).astype(BF16)

    @each
    def _(index):
        for local in range(part):
            band = bands_ref[index, local]
            for first in range(0, length, step):
                toep_ref[index, local, first : first + step] = jnp.where(
                    lane >= row + first, pltpu.roll(band, first, 1), 0.0
                )

    def convolve(index, ref):
        for local in range(part):
            out_ref[index, local] = dot(ref[local], toep_ref[index, local], NN)

    convolve(0, own_ref)

    def others(index, _):
        convolve(index, xc_ref.at[index - 1])
        return 0

    lax.fori_loop(1, PLANE, others, 0)


def split_pair(x, half):
    head = x.astype(BF16).astype(F32)
    tail = (x - head).astype(BF16).astype(F32)
    low = lane_iota(x.shape) < half
    return jnp.where(low, head, pltpu.roll(jnp.where(low, tail, 0.0), half, x.ndim - 1)).astype(BF16)


def join_pair(x, half):
    x = x.astype(F32)
    low = lane_iota(x.shape) < half
    return jnp.where(low, x + pltpu.roll(x, half, x.ndim - 1), 0.0)


def in_order(arrays, place):
    arrays, bit = list(arrays), 1
    while bit < len(arrays):
        swap = (place & bit) != 0
        new = list(arrays)
        for i in range(len(arrays)):
            new[i] = jnp.where(swap, arrays[i ^ bit], arrays[i])
        arrays, bit = new, 2 * bit
    return arrays


def advance(state, decay, gap):
    half = state.shape[2] // 2
    shifted = pltpu.roll(state, half, 2)
    return decay * (state + jnp.where(lane_iota(state.shape) >= half, gap * shifted, 0.0))


def scan_blocks(heads, tails, start, rate, gap):
    decay = jnp.exp(-rate * gap)
    state, before = start[0], []
    for head in heads:
        before.append(state)
        state = advance(state, decay, gap) + head
    other, after = start[1], []
    for tail in tails[::-1]:
        after.insert(0, other)
        other = advance(other, decay, gap) + tail
    return before, after, state, other


def pair_terms(before, tails, rate):
    half = rate.shape[2] // 2
    plain, moment = 0.0, 0.0
    for state, tail in zip(before, tails, strict=True):
        plain = plain + state * tail
        moment = moment + state * pltpu.roll(tail, half, 2)
    plain, moment = jnp.sum(plain, axis=1), jnp.sum(moment, axis=1)
    moment = moment + pltpu.roll(moment, half, 1) - pltpu.roll(plain, half, 1)
    return jnp.where(lane_iota(plain.shape) < half, plain, moment) * jnp.exp(rate[:, 0])


def spread(terms, place, acc, modes):
    quads, lanes = terms.shape
    parts = []
    for _ in range(3):
        parts.append(terms.astype(BF16))
        terms = terms - parts[-1].astype(F32)
    parts = jnp.concatenate([x.astype(F32) for x in parts], axis=0)
    shape = (3 * quads, 4 * lanes)
    lane = lane_iota(shape)
    row = lax.broadcasted_iota(jnp.int32, shape, 0) % quads
    group = lane % lanes - 4 * quads * place
    chosen = jnp.where(group == 4 * row + lane // lanes, 1.0, 0.0)
    turned = dot(parts.astype(BF16), chosen.astype(BF16), TN)
    for side in range(4):
        span = slice(side * lanes, (side + 1) * lanes)
        acc[:modes] += turned[side * modes : (side + 1) * modes, span]
        acc[modes:] += turned[(4 + side) * modes : (5 + side) * modes, span]


def own_rates(rate_ref, place, quads):
    rate = rate_ref[pl.ds(place * quads, quads), :]
    return rate.reshape(quads, 1, rate.shape[1])


def halves(blocks, rows):
    return [b[:, :rows] for b in blocks], [b[:, rows:] for b in blocks]


def plane_kernel(length, rate_ref, *refs):
    *msgs, sums_ref, out_ref, acc = refs
    place, _ = places()
    quads, rows, lanes = msgs[0].shape
    rows, flat = rows // 2, quads * rows
    modes = lanes // 8
    heads, tails = halves(in_order([m[...].astype(F32) for m in msgs], place), rows)
    rate = own_rates(rate_ref, place, quads)
    nothing = jnp.zeros_like(heads[0])
    before, _, head, tail = scan_blocks(heads, tails, (nothing, nothing), rate, float(length))
    both = jnp.concatenate([head, tail], axis=1)
    out_ref[:flat] = both.astype(BF16).reshape(flat, lanes)
    acc[...] = sums_ref[...]
    spread(pair_terms(before, tails, rate), place, acc, modes)
    out_ref[flat:] = split_pair(acc[...], lanes // 2)


def line_kernel(length, rate_ref, after_ref, *refs):
    count = len(refs) - 2 * PLANE - 1
    msgs, lines = refs[:PLANE], refs[PLANE : PLANE + count]
    outs, acc = refs[PLANE + count : -1], refs[-1]
    place, level = places()
    quads, rows, lanes = msgs[0].shape
    shape = (quads, rows, lanes)
    rows, flat = rows // 2, quads * rows
    modes = lanes // 8
    rate = own_rates(rate_ref, place, quads)
    heads, tails = halves(
        in_order([r[:flat].astype(F32).reshape(shape) for r in lines], level), rows
    )
    nothing = jnp.zeros_like(heads[0])
    before, after, _, _ = scan_blocks(
        heads, tails, (nothing, nothing), rate, float(PLANE * length)
    )
    total = join_pair(lines[0][flat:], lanes // 2)
    for r in lines[1:]:
        total = total + join_pair(r[flat:], lanes // 2)
    acc[...] = total
    spread(pair_terms(before, tails, rate), place, acc, modes)
    sums = split_pair(acc[...], lanes // 2)
    start = [nothing, nothing]
    for i in range(count):
        start[0] = jnp.where(level == i, before[i], start[0])
        start[1] = jnp.where(level == i, after[i], start[1])
    heads, tails = halves(in_order([m[...].astype(F32) for m in msgs], place), rows)
    before, after, _, _ = scan_blocks(heads, tails, start, rate, float(length))
    found = [jnp.concatenate(pair, axis=1) for pair in zip(before, after, strict=True)]
    found = in_order(found, place)
    low = lane_iota((quads // 2,) + shape[1:]) < lanes // 2
    for i in range(PLANE):
        packed = jnp.where(low, found[i][: quads // 2], pltpu.roll(found[i][quads // 2 :], lanes // 2, 2))
        outs[i][: flat // 2] = packed.astype(BF16).reshape(flat // 2, lanes)
        outs[i][flat // 2 :] = sums


def outputs_kernel(indices, k_ref, v_ref, g_ref, near_ref, taps_ref, *refs):
    count = len(indices)
    states, refs = refs[:count], refs[count:]
    results, (outs, sems, cs, gs) = refs[-7:-4], refs[-4:]
    place, _ = places()
    _, _, rows, part, length = outs.shape
    modes = taps_ref.shape[2]
    quads = part // 4
    mirror = mirror_of(length)
    spans = [
        pl.ds(pl.multiple_of((place ^ index) * part, part), part) for index in indices
    ]

    def store(which, slot):
        return pltpu.make_async_copy(
            outs.at[which, slot], results[which].at[:, spans[slot], :], sems.at[which, slot]
        )

    def expand(slot):
        index, state_ref = indices[slot], states[slot]
        half = quads // 2
        lane = lane_iota((2 * rows, 8 * modes))
        for quad in range(half):
            state = state_ref[2 * rows * quad : 2 * rows * (quad + 1)]
            locals_ = [4 * (quad + half * (i // 4)) + i % 4 for i in range(8)]
            left = [
                jnp.where((lane >= modes * i) & (lane < modes * (i + 1)), state, 0.0)
                for i in range(8)
            ]
            right = [taps_ref[index, local] for local in locals_]
            every = dot(jnp.concatenate(left, axis=0), jnp.concatenate(right, axis=0), NN)
            every = every.reshape(8, 2 * rows, length)
            for i, local in enumerate(locals_):
                both = every[i] + near_ref[index, local]
                where = pl.ds(local % 8, rows, stride=8)
                cs[slot, local // 8, where, :] = both[:rows]
                gs[slot, local // 8, where, :] = both[rows:]

    def finish(slot):
        conv, ig = (
            jnp.concatenate(
                [ref[slot, i].reshape(rows, 8, length) for i in range(part // 8)], axis=1
            ).astype(BF16)
            for ref in (cs, gs)
        )
        own = spans[slot]
        outs[0, slot] = product(g_ref[:, own, :], conv)
        ig = dot(ig.reshape(rows * part, length), mirror, NN).reshape(conv.shape)
        outs[1, slot] = product(ig, v_ref[:, own, :])
        outs[2, slot] = product(ig, k_ref[:, own, :])
        for which in range(3):
            store(which, slot).start()

    for slot in range(count + 1):
        if slot < count:
            expand(slot)
        if slot > 0:
            finish(slot - 1)
    for slot in range(count):
        for which in range(3):
            store(which, slot).wait()


def gradients(queries, keys_in, values_in, grad_out, residue, decay_rate):
    chans, length = queries.shape
    groups, modes = residue.shape
    count = lax.axis_size("ctx")
    tp = lax.axis_size("tp")
    depth = count // PLANE
    rows = chans // groups
    part = groups // PLANE
    quads = part // 4
    lanes = 8 * modes

    def cube(x):
        return x.reshape(rows, groups, length)

    query, key, value, grad = cube(queries), cube(keys_in), cube(values_in), cube(grad_out)
    decay, resid = decay_rate.T, residue.T
    vmem = pl.BlockSpec(memory_space=pltpu.VMEM)
    anywhere = pl.BlockSpec(memory_space=pltpu.HBM)

    def shaped(shape, dtype):
        return jax.ShapeDtypeStruct(shape, dtype)

    def call(kernel, in_specs, out_specs, out_shape, scratch, flops, size, aliases=None):
        return pl.pallas_call(
            kernel,
            in_specs=in_specs,
            out_specs=out_specs,
            out_shape=out_shape,
            scratch_shapes=scratch,
            cost_estimate=pl.CostEstimate(flops=flops, bytes_accessed=size, transcendentals=0),
            compiler_params=pltpu.CompilerParams(vmem_limit_bytes=16 * 2**20),
            input_output_aliases=aliases or {},
        )

    def in_hbm(*arrays):
        return [pltpu.with_memory_space_constraint(x, pltpu.HBM) for x in arrays]

    def reducer(slots):
        return [
            pltpu.VMEM((4, slots, rows, part, length), BF16),
            pltpu.SemaphoreType.DMA((4, slots)),
        ] + [pltpu.VMEM((slots, part // 8, rows * 8, length), F32)] * 2

    quarter = (part, 2 * rows, length)
    block = shaped((quads, 2 * rows, lanes), BF16)
    xc, weights, rates, *own = call(
        states_kernel,
        [anywhere] * 5,
        [vmem] * (2 + PLANE),
        [
            shaped((PLANE - 1,) + quarter, BF16),
            shaped((groups, 2, modes, length), BF16),
            shaped((groups // 4, lanes), F32),
        ]
        + [block] * (PLANE - 1),
        [pltpu.VMEM((modes, groups), F32), pltpu.SemaphoreType.DMA] + reducer(PLANE - 1),
        10**9,
        4 * 10**6,
    )(*in_hbm(decay, key, value, grad, query))

    def swap(x, bits):
        return lax.ppermute(x, "ctx", [(i, i ^ bits) for i in range(count)])

    near = [swap(own[i - 1], i) for i in range(1, PLANE)]
    xo, mine, sums = call(
        sums_kernel,
        [anywhere] * 4 + [vmem] * 3,
        [vmem] * 3,
        [shaped(quarter, BF16), block, shaped((2 * modes, lanes), F32)],
        reducer(1) + [pltpu.VMEM((groups, length), F32)],
        10**9,
        4 * 10**6,
    )(*in_hbm(key, value, grad, query), xc, weights, decay)
    near = [mine] + near
    flat = quads * 2 * rows
    plane = call(
        functools.partial(plane_kernel, length),
        [vmem] * (2 + PLANE),
        vmem,
        shaped((flat + 2 * modes, lanes), BF16),
        [pltpu.VMEM((2 * modes, lanes), F32)],
        10**7,
        10**6,
    )(rates, *near, sums)
    line = [plane] + [swap(plane, PLANE * i) for i in range(1, depth)]
    near_part, taps = call(
        local_kernel,
        [vmem] * 5,
        [vmem] * 2,
        [
            shaped((PLANE,) + quarter, F32),
            shaped((PLANE, part, modes, length), BF16),
        ],
        [
            pltpu.VMEM((PLANE, part, length, length), BF16),
            pltpu.VMEM((PLANE, part, length), F32),
            pltpu.VMEM((PLANE, part, 16, length), BF16),
        ],
        10**9,
        4 * 10**6,
    )(xo, xc, decay, resid, plane)
    sent = call(
        functools.partial(line_kernel, length),
        [vmem] * (2 + PLANE + depth),
        [vmem] * PLANE,
        [shaped((flat // 2 + 2 * modes, lanes), BF16)] * PLANE,
        [pltpu.VMEM((2 * modes, lanes), F32)],
        10**7,
        10**6,
    )(rates, taps, *near, *line)
    back = [sent[0]]
    for i in range(1, PLANE):
        back.append(swap(sent[i], i))

    total = sum(
        b[flat // 2 :, : lanes // 2].astype(F32) + b[flat // 2 :, lanes // 2 :].astype(F32)
        for b in back
    )
    bit = 1
    while bit < tp:
        total = total + lax.ppermute(total, "tp", [(i, i ^ bit) for i in range(tp)])
        bit *= 2

    outs = ()
    for indices in ((0,), tuple(range(1, PLANE - 1)), (PLANE - 1,)):
        slots = len(indices)
        outs = call(
            functools.partial(outputs_kernel, indices),
            [vmem] * (5 + slots) + [anywhere] * len(outs),
            [anywhere] * 3,
            [shaped((rows, groups, length), BF16)] * 3,
            [
                pltpu.VMEM((3, slots, rows, part, length), BF16),
                pltpu.SemaphoreType.DMA((3, slots)),
                pltpu.VMEM((slots, part // 8, rows * 8, length), F32),
                pltpu.VMEM((slots, part // 8, rows * 8, length), F32),
            ],
            2 * 10**8 * slots,
            10**6 * slots,
            {5 + slots + i: i for i in range(len(outs))},
        )(key, value, grad, near_part, taps, *(back[i] for i in indices), *outs)
    tokens = count * length
    plain, moment = total[:modes, :groups], total[modes:, :groups]
    return (
        *(x.reshape(chans, length) for x in outs),
        (plain / tokens).T,
        (-(resid * decay) * moment / tokens).T,
    )


def solution(mesh):
    in_specs = (P("tp", "ctx"), P("tp", "ctx"), P("tp", "ctx"), P("tp", "ctx"), P(), P())
    out_specs = (P("tp", "ctx"), P("tp", "ctx"), P("tp", "ctx"), P(), P())
    return jax.shard_map(
        gradients, mesh=mesh, in_specs=in_specs, out_specs=out_specs, check_vma=False
    )
```

```python
import functools

import jax
import jax.numpy as jnp
from jax import lax
from jax.experimental import pallas as pl
from jax.experimental.pallas import tpu as pltpu
from jax.sharding import PartitionSpec as P

F32 = jnp.float32
BF16 = jnp.bfloat16
PLANE = 4
NT = (((1,), (1,)), ((), ()))
NN = (((1,), (0,)), ((), ()))
TN = (((0,), (0,)), ((), ()))


def dot(a, b, dims):
    return lax.dot_general(a, b, dims, preferred_element_type=F32)


def product(a, b):
    return a.astype(BF16) * b.astype(BF16)


def column(table, group):
    return jnp.sum(jnp.where(lane_iota(table.shape) == group, table, 0.0), axis=1, keepdims=True)


def mirror_of(length):
    total = lane_iota((length, length)) + lax.broadcasted_iota(jnp.int32, (length, length), 0)
    return jnp.where(total == length - 1, 1.0, 0.0).astype(BF16)


def places():
    me = lax.axis_index("ctx")
    return lax.rem(me, PLANE), lax.div(me, PLANE)


def lane_iota(shape):
    return lax.broadcasted_iota(jnp.int32, shape, len(shape) - 1)


class Reducer:
    def __init__(self, sources, bufs, sems, w_ref, gs, cs):
        self.sources, self.bufs, self.sems, self.w_ref, self.gs, self.cs = (
            sources, bufs, sems, w_ref, gs, cs
        )
        _, self.rows, self.part, self.length = bufs.shape[1:]
        self.mirror = mirror_of(self.length)

    def copies(self, slot, quarter):
        return [
            pltpu.make_async_copy(
                source.at[:, pl.ds(pl.multiple_of(quarter * self.part, self.part), self.part), :],
                self.bufs.at[which, slot],
                self.sems.at[which, slot],
            )
            for which, source in enumerate(self.sources)
        ]

    def load(self, slot, quarter):
        for copy in self.copies(slot, quarter):
            copy.wait()
        bufs, flat = self.bufs, self.rows * self.part
        x = product(bufs[0, slot], bufs[1, slot]).astype(F32)
        c = product(bufs[2, slot], bufs[3, slot]).reshape(flat, self.length)
        c = dot(c, self.mirror, NN).reshape(x.shape)
        for eight in range(self.part // 8):
            span = slice(8 * eight, 8 * eight + 8)
            self.gs[slot, eight] = x[:, span].reshape(8 * self.rows, self.length)
            self.cs[slot, eight] = c[:, span].reshape(8 * self.rows, self.length)

    def reduce(self, slot, quarter, xc_ref, out_ref):
        modes = self.w_ref.shape[2]
        lane = lane_iota((2 * self.rows, 8 * modes)) % (4 * modes)
        for quad in range(self.part // 4):
            left, right = [], [[], []]
            for side in range(4):
                local = 4 * quad + side
                group = quarter * self.part + local
                where = pl.ds(local % 8, self.rows, stride=8)
                both = jnp.concatenate(
                    [ref[slot, local // 8, where, :] for ref in (self.gs, self.cs)], axis=0
                ).astype(BF16)
                xc_ref[local] = both
                left.append(both)
                right[0].append(self.w_ref[group, 0])
                right[1].append(self.w_ref[group, 1])
            every = dot(
                jnp.concatenate(left, axis=0), jnp.concatenate(right[0] + right[1], axis=0), NT
            )
            every = every.reshape(4, 2 * self.rows, 8 * modes)
            found = every[0]
            for side in range(1, 4):
                found = jnp.where(lane >= side * modes, every[side], found)
            out_ref[quad] = found.astype(BF16)


def states_kernel(dec_hbm, k_hbm, v_hbm, g_hbm, q_hbm, xc_ref, w_ref, rate_ref, *rest):
    outs, rest = rest[: PLANE - 1], rest[PLANE - 1 :]
    dec_ref, dec_sem, bufs, sems, gs, cs = rest
    place, _ = places()
    modes, groups = dec_ref.shape
    work = Reducer((k_hbm, v_hbm, g_hbm, q_hbm), bufs, sems, w_ref, gs, cs)
    length = work.length
    rates_in = pltpu.make_async_copy(dec_hbm, dec_ref, dec_sem)
    rates_in.start()
    for slot in range(PLANE - 1):
        for copy in work.copies(slot, place ^ (slot + 1)):
            copy.start()
    rates_in.wait()
    dec = dec_ref[...]
    behind = float(length) - lane_iota((modes, length)).astype(F32)
    wide = (modes, 8 * modes)
    target = lane_iota(wide) % (4 * modes) - lax.broadcasted_iota(jnp.int32, wide, 0)

    def weights(index, _):
        rates = jnp.zeros(wide, F32)
        for side in range(4):
            group = 4 * index + side
            rate = column(dec, group)
            basis = jnp.exp(-rate * behind)
            w_ref[group, 0] = basis.astype(BF16)
            w_ref[group, 1] = (behind * basis).astype(BF16)
            rates = jnp.where(target == side * modes, rate, rates)
        rate_ref[pl.ds(index, 1), :] = jnp.sum(rates, axis=0, keepdims=True)
        return 0

    lax.fori_loop(0, groups // 4, weights, 0, unroll=4)
    for slot in range(PLANE):
        if slot < PLANE - 1:
            work.load(slot, place ^ (slot + 1))
        if slot > 0:
            work.reduce(slot - 1, place ^ slot, xc_ref.at[slot - 1], outs[slot - 1])


def sums_kernel(k_hbm, v_hbm, g_hbm, q_hbm, xc_ref, w_ref, dec_ref, own_ref, out_ref, sums_ref, *rest):
    bufs, sems, gs, cs, corr_ref = rest
    place, _ = places()
    work = Reducer((k_hbm, v_hbm, g_hbm, q_hbm), bufs, sems, w_ref, gs, cs)
    for copy in work.copies(0, place):
        copy.start()
    _, part, rows, length = xc_ref.shape
    rows = rows // 2
    modes = dec_ref.shape[0]
    paired = (
        lane_iota((length, length)) + lax.broadcasted_iota(jnp.int32, (length, length), 0) < length
    )

    def correlate(ref, base):
        for local in range(part):
            prods = jnp.where(paired, dot(ref[local, :rows], ref[local, rows:], TN), 0.0)
            prods = pltpu.roll(prods, 0, 1, stride=1, stride_axis=0)
            corr_ref[pl.ds(base + local, 1), :] = jnp.sum(prods, axis=0, keepdims=True)

    def others(slot, _):
        correlate(xc_ref.at[slot], part * (place ^ (slot + 1)))
        return 0

    lax.fori_loop(0, PLANE - 1, others, 0)
    work.load(0, place)
    work.reduce(0, place, own_ref, out_ref)
    correlate(own_ref, part * place)
    dec = dec_ref[...]
    lag = float(length - 1) - lane_iota((modes, length)).astype(F32)
    lane = lane_iota((modes, sums_ref.shape[1]))

    def contract(quarter, carry):
        plain, moment = carry
        for local in range(part):
            group = quarter * part + local
            terms = jnp.exp(-column(dec, group) * lag) * corr_ref[pl.ds(group, 1), :]
            plain = jnp.where(lane == group, jnp.sum(terms, axis=1, keepdims=True), plain)
            moment = jnp.where(lane == group, jnp.sum(terms * lag, axis=1, keepdims=True), moment)
        return plain, moment

    zero = jnp.zeros(lane.shape, F32)
    plain, moment = lax.fori_loop(0, PLANE, contract, (zero, zero))
    sums_ref[:modes] = plain
    sums_ref[modes:] = moment


def local_kernel(own_ref, xc_ref, dec_ref, res_ref, after_ref, out_ref, taps_ref, *scratch):
    toep_ref, rows_ref, bands_ref = scratch
    _, part, _, length = xc_ref.shape
    modes = dec_ref.shape[0]
    place, _ = places()
    dec, res = dec_ref[...], res_ref[...]
    ahead = lane_iota((modes, length)).astype(F32)
    step = 16
    lane = lane_iota((step, length))
    row = lax.broadcasted_iota(jnp.int32, (step, length), 0)

    def each(body):
        def run(index, _):
            body(index)
            return 0

        lax.fori_loop(0, PLANE, run, 0)

    @each
    def _(index):
        first_group = (place ^ index) * part
        for local in range(part):
            rate, weight = column(dec, first_group + local), column(res, first_group + local)
            taps = weight * jnp.exp(-rate * ahead)
            taps_ref[index, local] = taps.astype(BF16)
            rows_ref[index, local : local + 1] = jnp.sum(taps, axis=0, keepdims=True)

    @each
    def _(index):
        for local in range(part):
            taps = jnp.broadcast_to(rows_ref[index, local : local + 1], (step, length))
            bands_ref[index, local] = pltpu.roll(taps, 0, 1, stride=1, stride_axis=0).astype(BF16)

    @each
    def _(index):
        for local in range(part):
            band = bands_ref[index, local]
            for first in range(0, length, step):
                toep_ref[index, local, first : first + step] = jnp.where(
                    lane >= row + first, pltpu.roll(band, first, 1), 0.0
                )

    def convolve(index, ref):
        for local in range(part):
            out_ref[index, local] = dot(ref[local], toep_ref[index, local], NN)

    convolve(0, own_ref)

    def others(index, _):
        convolve(index, xc_ref.at[index - 1])
        return 0

    lax.fori_loop(1, PLANE, others, 0)


def split_pair(x, half):
    head = x.astype(BF16).astype(F32)
    tail = (x - head).astype(BF16).astype(F32)
    low = lane_iota(x.shape) < half
    return jnp.where(low, head, pltpu.roll(jnp.where(low, tail, 0.0), half, x.ndim - 1)).astype(BF16)


def join_pair(x, half):
    x = x.astype(F32)
    low = lane_iota(x.shape) < half
    return jnp.where(low, x + pltpu.roll(x, half, x.ndim - 1), 0.0)


def in_order(arrays, place):
    arrays, bit = list(arrays), 1
    while bit < len(arrays):
        swap = (place & bit) != 0
        new = list(arrays)
        for i in range(len(arrays)):
            new[i] = jnp.where(swap, arrays[i ^ bit], arrays[i])
        arrays, bit = new, 2 * bit
    return arrays


def advance(state, decay, gap):
    half = state.shape[2] // 2
    shifted = pltpu.roll(state, half, 2)
    return decay * (state + jnp.where(lane_iota(state.shape) >= half, gap * shifted, 0.0))


def scan_blocks(heads, tails, start, rate, gap):
    decay = jnp.exp(-rate * gap)
    state, before = start[0], []
    for head in heads:
        before.append(state)
        state = advance(state, decay, gap) + head
    other, after = start[1], []
    for tail in tails[::-1]:
        after.insert(0, other)
        other = advance(other, decay, gap) + tail
    return before, after, state, other


def pair_terms(before, tails, rate):
    half = rate.shape[2] // 2
    plain, moment = 0.0, 0.0
    for state, tail in zip(before, tails, strict=True):
        plain = plain + state * tail
        moment = moment + state * pltpu.roll(tail, half, 2)
    plain, moment = jnp.sum(plain, axis=1), jnp.sum(moment, axis=1)
    moment = moment + pltpu.roll(moment, half, 1) - pltpu.roll(plain, half, 1)
    return jnp.where(lane_iota(plain.shape) < half, plain, moment) * jnp.exp(rate[:, 0])


def spread(terms, place, acc, modes):
    quads, lanes = terms.shape
    parts = []
    for _ in range(3):
        parts.append(terms.astype(BF16))
        terms = terms - parts[-1].astype(F32)
    parts = jnp.concatenate([x.astype(F32) for x in parts], axis=0)
    shape = (3 * quads, 4 * lanes)
    lane = lane_iota(shape)
    row = lax.broadcasted_iota(jnp.int32, shape, 0) % quads
    group = lane % lanes - 4 * quads * place
    chosen = jnp.where(group == 4 * row + lane // lanes, 1.0, 0.0)
    turned = dot(parts.astype(BF16), chosen.astype(BF16), TN)
    for side in range(4):
        span = slice(side * lanes, (side + 1) * lanes)
        acc[:modes] += turned[side * modes : (side + 1) * modes, span]
        acc[modes:] += turned[(4 + side) * modes : (5 + side) * modes, span]


def own_rates(rate_ref, place, quads):
    rate = rate_ref[pl.ds(place * quads, quads), :]
    return rate.reshape(quads, 1, rate.shape[1])


def halves(blocks, rows):
    blocks = [b.astype(F32) for b in blocks]
    return [b[:, :rows] for b in blocks], [b[:, rows:] for b in blocks]


def plane_kernel(length, rate_ref, *refs):
    *msgs, sums_ref, out_ref, acc = refs
    place, _ = places()
    quads, rows, lanes = msgs[0].shape
    rows, flat = rows // 2, quads * rows
    modes = lanes // 8
    heads, tails = halves(in_order([m[...] for m in msgs], place), rows)
    rate = own_rates(rate_ref, place, quads)
    nothing = jnp.zeros_like(heads[0])
    before, _, head, tail = scan_blocks(heads, tails, (nothing, nothing), rate, float(length))
    both = jnp.concatenate([head, tail], axis=1)
    out_ref[:flat] = both.astype(BF16).reshape(flat, lanes)
    acc[...] = sums_ref[...]
    spread(pair_terms(before, tails, rate), place, acc, modes)
    out_ref[flat:] = split_pair(acc[...], lanes // 2)


def line_kernel(length, rate_ref, after_ref, *refs):
    count = len(refs) - 2 * PLANE - 1
    msgs, lines = refs[:PLANE], refs[PLANE : PLANE + count]
    outs, acc = refs[PLANE + count : -1], refs[-1]
    place, level = places()
    quads, rows, lanes = msgs[0].shape
    shape = (quads, rows, lanes)
    rows, flat = rows // 2, quads * rows
    modes = lanes // 8
    rate = own_rates(rate_ref, place, quads)
    heads, tails = halves(
        in_order([r[:flat].reshape(shape) for r in lines], level), rows
    )
    nothing = jnp.zeros_like(heads[0])
    before, after, _, _ = scan_blocks(
        heads, tails, (nothing, nothing), rate, float(PLANE * length)
    )
    total = join_pair(lines[0][flat:], lanes // 2)
    for r in lines[1:]:
        total = total + join_pair(r[flat:], lanes // 2)
    acc[...] = total
    spread(pair_terms(before, tails, rate), place, acc, modes)
    sums = split_pair(acc[...], lanes // 2)
    start = [nothing, nothing]
    for i in range(count):
        start[0] = jnp.where(level == i, before[i], start[0])
        start[1] = jnp.where(level == i, after[i], start[1])
    heads, tails = halves(in_order([m[...] for m in msgs], place), rows)
    decay = jnp.exp(-rate * float(length))
    before, after = [start[0]], [start[1]]
    for i in range(PLANE - 1):
        before.append(decay * before[-1] + heads[i])
        after.insert(0, decay * after[0] + tails[PLANE - 1 - i])
    low = lane_iota((quads // 2, 2 * rows, lanes)) < lanes // 2
    packed = []
    for pair in zip(before, after, strict=True):
        found = jnp.concatenate(pair, axis=1)
        found = jnp.where(low, found[: quads // 2], pltpu.roll(found[quads // 2 :], lanes // 2, 2))
        packed.append(found.astype(BF16).reshape(flat // 2, lanes))
    for i, found in enumerate(in_order(packed, place)):
        outs[i][: flat // 2] = found
        outs[i][flat // 2 :] = sums


def outputs_kernel(indices, k_ref, v_ref, g_ref, near_ref, taps_ref, *refs):
    count = len(indices)
    states, refs = refs[:count], refs[count:]
    results, (outs, sems, cs, gs) = refs[-7:-4], refs[-4:]
    place, _ = places()
    _, _, rows, part, length = outs.shape
    modes = taps_ref.shape[2]
    quads = part // 4
    mirror = mirror_of(length)
    spans = [
        pl.ds(pl.multiple_of((place ^ index) * part, part), part) for index in indices
    ]

    def store(which, slot):
        return pltpu.make_async_copy(
            outs.at[which, slot], results[which].at[:, spans[slot], :], sems.at[which, slot]
        )

    def expand(slot):
        index, state_ref = indices[slot], states[slot]
        half = quads // 2
        lane = lane_iota((2 * rows, 8 * modes))
        for quad in range(half):
            state = state_ref[2 * rows * quad : 2 * rows * (quad + 1)]
            locals_ = [4 * (quad + half * (i // 4)) + i % 4 for i in range(8)]
            left = [
                jnp.where((lane >= modes * i) & (lane < modes * (i + 1)), state, 0.0)
                for i in range(8)
            ]
            right = [taps_ref[index, local] for local in locals_]
            every = dot(jnp.concatenate(left, axis=0), jnp.concatenate(right, axis=0), NN)
            every = every.reshape(8, 2 * rows, length)
            for i, local in enumerate(locals_):
                both = every[i] + near_ref[index, local]
                where = pl.ds(local % 8, rows, stride=8)
                cs[slot, local // 8, where, :] = both[:rows]
                gs[slot, local // 8, where, :] = both[rows:]

    def finish(slot):
        def natural(ref):
            pieces = [ref[slot, i].reshape(rows, 8, length) for i in range(part // 8)]
            return jnp.concatenate(pieces, axis=1).astype(BF16)

        own = spans[slot]
        ig = dot(natural(gs).reshape(rows * part, length), mirror, NN)
        outs[0, slot] = product(g_ref[:, own, :], natural(cs))
        store(0, slot).start()
        ig = ig.astype(BF16).reshape(rows, part, length)
        outs[1, slot] = product(ig, v_ref[:, own, :])
        store(1, slot).start()
        outs[2, slot] = product(ig, k_ref[:, own, :])
        store(2, slot).start()

    for slot in range(count + 1):
        if slot < count:
            expand(slot)
        if slot > 0:
            finish(slot - 1)
    for slot in range(count):
        for which in range(3):
            store(which, slot).wait()


def gradients(queries, keys_in, values_in, grad_out, residue, decay_rate):
    chans, length = queries.shape
    groups, modes = residue.shape
    count = lax.axis_size("ctx")
    tp = lax.axis_size("tp")
    depth = count // PLANE
    rows = chans // groups
    part = groups // PLANE
    quads = part // 4
    lanes = 8 * modes

    def cube(x):
        return x.reshape(rows, groups, length)

    query, key, value, grad = cube(queries), cube(keys_in), cube(values_in), cube(grad_out)
    decay, resid = decay_rate.T, residue.T
    vmem = pl.BlockSpec(memory_space=pltpu.VMEM)
    anywhere = pl.BlockSpec(memory_space=pltpu.HBM)

    def shaped(shape, dtype):
        return jax.ShapeDtypeStruct(shape, dtype)

    def call(kernel, in_specs, out_specs, out_shape, scratch, flops, size, aliases=None):
        return pl.pallas_call(
            kernel,
            in_specs=in_specs,
            out_specs=out_specs,
            out_shape=out_shape,
            scratch_shapes=scratch,
            cost_estimate=pl.CostEstimate(flops=flops, bytes_accessed=size, transcendentals=0),
            compiler_params=pltpu.CompilerParams(vmem_limit_bytes=16 * 2**20),
            input_output_aliases=aliases or {},
        )

    def in_hbm(*arrays):
        return [pltpu.with_memory_space_constraint(x, pltpu.HBM) for x in arrays]

    def reducer(slots):
        return [
            pltpu.VMEM((4, slots, rows, part, length), BF16),
            pltpu.SemaphoreType.DMA((4, slots)),
        ] + [pltpu.VMEM((slots, part // 8, rows * 8, length), F32)] * 2

    quarter = (part, 2 * rows, length)
    block = shaped((quads, 2 * rows, lanes), BF16)
    xc, weights, rates, *own = call(
        states_kernel,
        [anywhere] * 5,
        [vmem] * (2 + PLANE),
        [
            shaped((PLANE - 1,) + quarter, BF16),
            shaped((groups, 2, modes, length), BF16),
            shaped((groups // 4, lanes), F32),
        ]
        + [block] * (PLANE - 1),
        [pltpu.VMEM((modes, groups), F32), pltpu.SemaphoreType.DMA] + reducer(PLANE - 1),
        10**9,
        4 * 10**6,
    )(*in_hbm(decay, key, value, grad, query))

    def swap(x, bits):
        return lax.ppermute(x, "ctx", [(i, i ^ bits) for i in range(count)])

    near = [swap(own[i - 1], i) for i in range(1, PLANE)]
    xo, mine, sums = call(
        sums_kernel,
        [anywhere] * 4 + [vmem] * 3,
        [vmem] * 3,
        [shaped(quarter, BF16), block, shaped((2 * modes, lanes), F32)],
        reducer(1) + [pltpu.VMEM((groups, length), F32)],
        10**9,
        4 * 10**6,
    )(*in_hbm(key, value, grad, query), xc, weights, decay)
    near = [mine] + near
    flat = quads * 2 * rows
    plane = call(
        functools.partial(plane_kernel, length),
        [vmem] * (2 + PLANE),
        vmem,
        shaped((flat + 2 * modes, lanes), BF16),
        [pltpu.VMEM((2 * modes, lanes), F32)],
        10**7,
        10**6,
    )(rates, *near, sums)
    line = [plane] + [swap(plane, PLANE * i) for i in range(1, depth)]
    near_part, taps = call(
        local_kernel,
        [vmem] * 5,
        [vmem] * 2,
        [
            shaped((PLANE,) + quarter, F32),
            shaped((PLANE, part, modes, length), BF16),
        ],
        [
            pltpu.VMEM((PLANE, part, length, length), BF16),
            pltpu.VMEM((PLANE, part, length), F32),
            pltpu.VMEM((PLANE, part, 16, length), BF16),
        ],
        10**9,
        4 * 10**6,
    )(xo, xc, decay, resid, plane)
    sent = call(
        functools.partial(line_kernel, length),
        [vmem] * (2 + PLANE + depth),
        [vmem] * PLANE,
        [shaped((flat // 2 + 2 * modes, lanes), BF16)] * PLANE,
        [pltpu.VMEM((2 * modes, lanes), F32)],
        10**7,
        10**6,
    )(rates, taps, *near, *line)
    back = [sent[0]]
    for i in range(1, PLANE):
        back.append(swap(sent[i], i))

    total = sum(
        b[flat // 2 :, : lanes // 2].astype(F32) + b[flat // 2 :, lanes // 2 :].astype(F32)
        for b in back
    )
    bit = 1
    while bit < tp:
        total = total + lax.ppermute(total, "tp", [(i, i ^ bit) for i in range(tp)])
        bit *= 2

    outs = ()
    for indices in ((0,), tuple(range(1, PLANE - 1)), (PLANE - 1,)):
        slots = len(indices)
        outs = call(
            functools.partial(outputs_kernel, indices),
            [vmem] * (5 + slots) + [anywhere] * len(outs),
            [anywhere] * 3,
            [shaped((rows, groups, length), BF16)] * 3,
            [
                pltpu.VMEM((3, slots, rows, part, length), BF16),
                pltpu.SemaphoreType.DMA((3, slots)),
                pltpu.VMEM((slots, part // 8, rows * 8, length), F32),
                pltpu.VMEM((slots, part // 8, rows * 8, length), F32),
            ],
            2 * 10**8 * slots,
            10**6 * slots,
            {5 + slots + i: i for i in range(len(outs))},
        )(key, value, grad, near_part, taps, *(back[i] for i in indices), *outs)
    tokens = count * length
    plain, moment = total[:modes, :groups], total[modes:, :groups]
    return (
        *(x.reshape(chans, length) for x in outs),
        (plain / tokens).T,
        (-(resid * decay) * moment / tokens).T,
    )


def solution(mesh):
    in_specs = (P("tp", "ctx"), P("tp", "ctx"), P("tp", "ctx"), P("tp", "ctx"), P(), P())
    out_specs = (P("tp", "ctx"), P("tp", "ctx"), P("tp", "ctx"), P(), P())
    return jax.shard_map(
        gradients, mesh=mesh, in_specs=in_specs, out_specs=out_specs, check_vma=False
    )
```

```python
import functools

import jax
import jax.numpy as jnp
from jax import lax
from jax.experimental import pallas as pl
from jax.experimental.pallas import tpu as pltpu
from jax.sharding import PartitionSpec as P

F32 = jnp.float32
BF16 = jnp.bfloat16
PLANE = 4
NT = (((1,), (1,)), ((), ()))
NN = (((1,), (0,)), ((), ()))
TN = (((0,), (0,)), ((), ()))


def dot(a, b, dims):
    return lax.dot_general(a, b, dims, preferred_element_type=F32)


def product(a, b):
    return a.astype(BF16) * b.astype(BF16)


def column(table, group):
    return jnp.sum(jnp.where(lane_iota(table.shape) == group, table, 0.0), axis=1, keepdims=True)


def mirror_of(length):
    total = lane_iota((length, length)) + lax.broadcasted_iota(jnp.int32, (length, length), 0)
    return jnp.where(total == length - 1, 1.0, 0.0).astype(BF16)


def places():
    me = lax.axis_index("ctx")
    return lax.rem(me, PLANE), lax.div(me, PLANE)


def lane_iota(shape):
    return lax.broadcasted_iota(jnp.int32, shape, len(shape) - 1)


class Reducer:
    def __init__(self, sources, bufs, sems, w_ref, gs, cs):
        self.sources, self.bufs, self.sems, self.w_ref, self.gs, self.cs = (
            sources, bufs, sems, w_ref, gs, cs
        )
        _, self.rows, self.part, self.length = bufs.shape[1:]
        self.mirror = mirror_of(self.length)

    def copies(self, slot, quarter):
        return [
            pltpu.make_async_copy(
                source.at[:, pl.ds(pl.multiple_of(quarter * self.part, self.part), self.part), :],
                self.bufs.at[which, slot],
                self.sems.at[which, slot],
            )
            for which, source in enumerate(self.sources)
        ]

    def load(self, slot, quarter):
        for copy in self.copies(slot, quarter):
            copy.wait()
        bufs, flat = self.bufs, self.rows * self.part
        x = product(bufs[0, slot], bufs[1, slot]).astype(F32)
        c = product(bufs[2, slot], bufs[3, slot]).reshape(flat, self.length)
        c = dot(c, self.mirror, NN).reshape(x.shape)
        for eight in range(self.part // 8):
            span = slice(8 * eight, 8 * eight + 8)
            self.gs[slot, eight] = x[:, span].reshape(8 * self.rows, self.length)
            self.cs[slot, eight] = c[:, span].reshape(8 * self.rows, self.length)

    def reduce(self, slot, quarter, xc_ref, out_ref):
        modes = self.w_ref.shape[2]
        lane = lane_iota((2 * self.rows, 8 * modes)) % (4 * modes)
        for quad in range(self.part // 4):
            left, right = [], [[], []]
            for side in range(4):
                local = 4 * quad + side
                group = quarter * self.part + local
                where = pl.ds(local % 8, self.rows, stride=8)
                both = jnp.concatenate(
                    [ref[slot, local // 8, where, :] for ref in (self.gs, self.cs)], axis=0
                ).astype(BF16)
                xc_ref[local] = both
                left.append(both)
                right[0].append(self.w_ref[group, 0])
                right[1].append(self.w_ref[group, 1])
            every = dot(
                jnp.concatenate(left, axis=0), jnp.concatenate(right[0] + right[1], axis=0), NT
            )
            every = every.reshape(4, 2 * self.rows, 8 * modes)
            found = every[0]
            for side in range(1, 4):
                found = jnp.where(lane >= side * modes, every[side], found)
            out_ref[quad] = found.astype(BF16)


def states_kernel(dec_hbm, k_hbm, v_hbm, g_hbm, q_hbm, xc_ref, w_ref, rate_ref, *rest):
    outs, rest = rest[: PLANE - 1], rest[PLANE - 1 :]
    dec_ref, dec_sem, bufs, sems, gs, cs = rest
    place, _ = places()
    modes, groups = dec_ref.shape
    work = Reducer((k_hbm, v_hbm, g_hbm, q_hbm), bufs, sems, w_ref, gs, cs)
    length = work.length
    rates_in = pltpu.make_async_copy(dec_hbm, dec_ref, dec_sem)
    rates_in.start()
    for slot in range(PLANE - 1):
        for copy in work.copies(slot, place ^ (slot + 1)):
            copy.start()
    rates_in.wait()
    dec = dec_ref[...]
    behind = float(length) - lane_iota((modes, length)).astype(F32)
    wide = (modes, 8 * modes)
    target = lane_iota(wide) % (4 * modes) - lax.broadcasted_iota(jnp.int32, wide, 0)

    def weights(index, _):
        rates = jnp.zeros(wide, F32)
        for side in range(4):
            group = 4 * index + side
            rate = column(dec, group)
            basis = jnp.exp(-rate * behind)
            w_ref[group, 0] = basis.astype(BF16)
            w_ref[group, 1] = (behind * basis).astype(BF16)
            rates = jnp.where(target == side * modes, rate, rates)
        rate_ref[pl.ds(index, 1), :] = jnp.sum(rates, axis=0, keepdims=True)
        return 0

    lax.fori_loop(0, groups // 4, weights, 0, unroll=4)
    for slot in range(PLANE):
        if slot < PLANE - 1:
            work.load(slot, place ^ (slot + 1))
        if slot > 0:
            work.reduce(slot - 1, place ^ slot, xc_ref.at[slot - 1], outs[slot - 1])


def sums_kernel(k_hbm, v_hbm, g_hbm, q_hbm, xc_ref, w_ref, dec_ref, own_ref, out_ref, sums_ref, *rest):
    bufs, sems, gs, cs, corr_ref = rest
    place, _ = places()
    work = Reducer((k_hbm, v_hbm, g_hbm, q_hbm), bufs, sems, w_ref, gs, cs)
    for copy in work.copies(0, place):
        copy.start()
    _, part, rows, length = xc_ref.shape
    rows = rows // 2
    modes = dec_ref.shape[0]
    paired = (
        lane_iota((length, length)) + lax.broadcasted_iota(jnp.int32, (length, length), 0) < length
    )

    def correlate(ref, base):
        for local in range(part):
            prods = jnp.where(paired, dot(ref[local, :rows], ref[local, rows:], TN), 0.0)
            prods = pltpu.roll(prods, 0, 1, stride=1, stride_axis=0)
            corr_ref[pl.ds(base + local, 1), :] = jnp.sum(prods, axis=0, keepdims=True)

    def others(slot, _):
        correlate(xc_ref.at[slot], part * (place ^ (slot + 1)))
        return 0

    lax.fori_loop(0, PLANE - 1, others, 0)
    work.load(0, place)
    work.reduce(0, place, own_ref, out_ref)
    correlate(own_ref, part * place)
    dec = dec_ref[...]
    lag = float(length - 1) - lane_iota((modes, length)).astype(F32)
    lane = lane_iota((modes, sums_ref.shape[1]))

    def contract(quarter, carry):
        plain, moment = carry
        for local in range(part):
            group = quarter * part + local
            terms = jnp.exp(-column(dec, group) * lag) * corr_ref[pl.ds(group, 1), :]
            plain = jnp.where(lane == group, jnp.sum(terms, axis=1, keepdims=True), plain)
            moment = jnp.where(lane == group, jnp.sum(terms * lag, axis=1, keepdims=True), moment)
        return plain, moment

    zero = jnp.zeros(lane.shape, F32)
    plain, moment = lax.fori_loop(0, PLANE, contract, (zero, zero))
    sums_ref[:modes] = plain
    sums_ref[modes:] = moment


def local_kernel(own_ref, xc_ref, dec_ref, res_ref, after_ref, out_ref, taps_ref, *scratch):
    toep_ref, rows_ref, bands_ref = scratch
    _, part, _, length = xc_ref.shape
    modes = dec_ref.shape[0]
    place, _ = places()
    dec, res = dec_ref[...], res_ref[...]
    ahead = lane_iota((modes, length)).astype(F32)
    step = 16
    lane = lane_iota((step, length))
    row = lax.broadcasted_iota(jnp.int32, (step, length), 0)

    def each(body):
        def run(index, _):
            body(index)
            return 0

        lax.fori_loop(0, PLANE, run, 0)

    @each
    def _(index):
        first_group = (place ^ index) * part
        for local in range(part):
            rate, weight = column(dec, first_group + local), column(res, first_group + local)
            taps = weight * jnp.exp(-rate * ahead)
            taps_ref[index, local] = taps.astype(BF16)
            rows_ref[index, local : local + 1] = jnp.sum(taps, axis=0, keepdims=True)

    @each
    def _(index):
        for local in range(part):
            taps = jnp.broadcast_to(rows_ref[index, local : local + 1], (step, length))
            bands_ref[index, local] = pltpu.roll(taps, 0, 1, stride=1, stride_axis=0).astype(BF16)

    @each
    def _(index):
        for local in range(part):
            band = bands_ref[index, local]
            for first in range(0, length, step):
                toep_ref[index, local, first : first + step] = jnp.where(
                    lane >= row + first, pltpu.roll(band, first, 1), 0.0
                )

    def convolve(index, ref):
        for local in range(part):
            out_ref[index, local] = dot(ref[local], toep_ref[index, local], NN)

    convolve(0, own_ref)

    def others(index, _):
        convolve(index, xc_ref.at[index - 1])
        return 0

    lax.fori_loop(1, PLANE, others, 0)


def split_pair(x, half):
    head = x.astype(BF16).astype(F32)
    tail = (x - head).astype(BF16).astype(F32)
    low = lane_iota(x.shape) < half
    return jnp.where(low, head, pltpu.roll(jnp.where(low, tail, 0.0), half, x.ndim - 1)).astype(BF16)


def join_pair(x, half):
    x = x.astype(F32)
    low = lane_iota(x.shape) < half
    return jnp.where(low, x + pltpu.roll(x, half, x.ndim - 1), 0.0)


def in_order(arrays, place):
    arrays, bit = list(arrays), 1
    while bit < len(arrays):
        swap = (place & bit) != 0
        new = list(arrays)
        for i in range(len(arrays)):
            new[i] = jnp.where(swap, arrays[i ^ bit], arrays[i])
        arrays, bit = new, 2 * bit
    return arrays


def advance(state, decay, gap):
    half = state.shape[2] // 2
    shifted = pltpu.roll(state, half, 2)
    return decay * (state + jnp.where(lane_iota(state.shape) >= half, gap * shifted, 0.0))


def scan_blocks(heads, tails, start, rate, gap):
    decay = jnp.exp(-rate * gap)
    state, before = start[0], []
    for head in heads:
        before.append(state)
        state = advance(state, decay, gap) + head
    other, after = start[1], []
    for tail in tails[::-1]:
        after.insert(0, other)
        other = advance(other, decay, gap) + tail
    return before, after, state, other


def pair_terms(before, tails, rate):
    half = rate.shape[2] // 2
    plain, moment = 0.0, 0.0
    for state, tail in zip(before, tails, strict=True):
        plain = plain + state * tail
        moment = moment + state * pltpu.roll(tail, half, 2)
    plain, moment = jnp.sum(plain, axis=1), jnp.sum(moment, axis=1)
    moment = moment + pltpu.roll(moment, half, 1) - pltpu.roll(plain, half, 1)
    return jnp.where(lane_iota(plain.shape) < half, plain, moment) * jnp.exp(rate[:, 0])


def spread(terms, place, acc, modes):
    quads, lanes = terms.shape
    parts = []
    for _ in range(3):
        parts.append(terms.astype(BF16))
        terms = terms - parts[-1].astype(F32)
    parts = jnp.concatenate([x.astype(F32) for x in parts], axis=0)
    shape = (3 * quads, 4 * lanes)
    lane = lane_iota(shape)
    row = lax.broadcasted_iota(jnp.int32, shape, 0) % quads
    group = lane % lanes - 4 * quads * place
    chosen = jnp.where(group == 4 * row + lane // lanes, 1.0, 0.0)
    turned = dot(parts.astype(BF16), chosen.astype(BF16), TN)
    for side in range(4):
        span = slice(side * lanes, (side + 1) * lanes)
        acc[:modes] += turned[side * modes : (side + 1) * modes, span]
        acc[modes:] += turned[(4 + side) * modes : (5 + side) * modes, span]


def own_rates(rate_ref, place, quads):
    rate = rate_ref[pl.ds(place * quads, quads), :]
    return rate.reshape(quads, 1, rate.shape[1])


def halves(blocks, rows):
    blocks = [b.astype(F32) for b in blocks]
    return [b[:, :rows] for b in blocks], [b[:, rows:] for b in blocks]


def plane_kernel(length, rate_ref, *refs):
    *msgs, sums_ref, out_ref, acc = refs
    place, _ = places()
    quads, rows, lanes = msgs[0].shape
    rows, flat = rows // 2, quads * rows
    modes = lanes // 8
    heads, tails = halves(in_order([m[...] for m in msgs], place), rows)
    rate = own_rates(rate_ref, place, quads)
    nothing = jnp.zeros_like(heads[0])
    before, _, head, tail = scan_blocks(heads, tails, (nothing, nothing), rate, float(length))
    both = jnp.concatenate([head, tail], axis=1)
    out_ref[:flat] = both.astype(BF16).reshape(flat, lanes)
    acc[...] = sums_ref[...]
    spread(pair_terms(before, tails, rate), place, acc, modes)
    out_ref[flat:] = split_pair(acc[...], lanes // 2)


def line_kernel(length, rate_ref, after_ref, *refs):
    count = len(refs) - 2 * PLANE - 1
    msgs, lines = refs[:PLANE], refs[PLANE : PLANE + count]
    outs, acc = refs[PLANE + count : -1], refs[-1]
    place, level = places()
    quads, rows, lanes = msgs[0].shape
    shape = (quads, rows, lanes)
    rows, flat = rows // 2, quads * rows
    modes = lanes // 8
    rate = own_rates(rate_ref, place, quads)
    heads, tails = halves(
        in_order([r[:flat].reshape(shape) for r in lines], level), rows
    )
    nothing = jnp.zeros_like(heads[0])
    before, after, _, _ = scan_blocks(
        heads, tails, (nothing, nothing), rate, float(PLANE * length)
    )
    total = join_pair(lines[0][flat:], lanes // 2)
    for r in lines[1:]:
        total = total + join_pair(r[flat:], lanes // 2)
    acc[...] = total
    spread(pair_terms(before, tails, rate), place, acc, modes)
    sums = split_pair(acc[...], lanes // 2)
    start = [nothing, nothing]
    for i in range(count):
        start[0] = jnp.where(level == i, before[i], start[0])
        start[1] = jnp.where(level == i, after[i], start[1])
    heads, tails = halves(in_order([m[...] for m in msgs], place), rows)
    decay = jnp.exp(-rate * float(length))
    before, after = [start[0]], [start[1]]
    for i in range(PLANE - 1):
        before.append(decay * before[-1] + heads[i])
        after.insert(0, decay * after[0] + tails[PLANE - 1 - i])
    low = lane_iota((quads // 2, 2 * rows, lanes)) < lanes // 2
    packed = []
    for pair in zip(before, after, strict=True):
        found = jnp.concatenate(pair, axis=1)
        found = jnp.where(low, found[: quads // 2], pltpu.roll(found[quads // 2 :], lanes // 2, 2))
        packed.append(found.astype(BF16).reshape(flat // 2, lanes))
    for i, found in enumerate(in_order(packed, place)):
        outs[i][: flat // 2] = found
        outs[i][flat // 2 :] = sums


def outputs_kernel(indices, k_ref, v_ref, g_ref, near_ref, taps_ref, *refs):
    count = len(indices)
    states, refs = refs[:count], refs[count:]
    results, (outs, sems, cs, gs) = refs[-7:-4], refs[-4:]
    place, _ = places()
    _, _, rows, part, length = outs.shape
    modes = taps_ref.shape[2]
    quads = part // 4
    mirror = mirror_of(length)
    spans = [
        pl.ds(pl.multiple_of((place ^ index) * part, part), part) for index in indices
    ]

    def store(which, slot):
        return pltpu.make_async_copy(
            outs.at[which, slot], results[which].at[:, spans[slot], :], sems.at[which, slot]
        )

    def expand(slot):
        index, state_ref = indices[slot], states[slot]
        half = quads // 2
        lane = lane_iota((2 * rows, 8 * modes))
        for quad in range(half):
            state = state_ref[2 * rows * quad : 2 * rows * (quad + 1)]
            locals_ = [4 * (quad + half * (i // 4)) + i % 4 for i in range(8)]
            left = [
                jnp.where((lane >= modes * i) & (lane < modes * (i + 1)), state, 0.0)
                for i in range(8)
            ]
            right = [taps_ref[index, local] for local in locals_]
            every = dot(jnp.concatenate(left, axis=0), jnp.concatenate(right, axis=0), NN)
            every = every.reshape(8, 2 * rows, length)
            for i, local in enumerate(locals_):
                both = every[i] + near_ref[index, local]
                where = pl.ds(local % 8, rows, stride=8)
                cs[slot, local // 8, where, :] = both[:rows]
                gs[slot, local // 8, where, :] = both[rows:]

    def finish(slot):
        def natural(ref):
            pieces = [ref[slot, i].reshape(rows, 8, length) for i in range(part // 8)]
            return jnp.concatenate(pieces, axis=1).astype(BF16)

        own = spans[slot]
        ig = dot(natural(gs).reshape(rows * part, length), mirror, NN)
        outs[0, slot] = product(g_ref[:, own, :], natural(cs))
        store(0, slot).start()
        ig = ig.astype(BF16).reshape(rows, part, length)
        outs[1, slot] = product(ig, v_ref[:, own, :])
        store(1, slot).start()
        outs[2, slot] = product(ig, k_ref[:, own, :])
        store(2, slot).start()

    for slot in range(count + 1):
        if slot < count:
            expand(slot)
        if slot > 0:
            finish(slot - 1)
    for slot in range(count):
        for which in range(3):
            store(which, slot).wait()


def gradients(queries, keys_in, values_in, grad_out, residue, decay_rate):
    chans, length = queries.shape
    groups, modes = residue.shape
    count = lax.axis_size("ctx")
    tp = lax.axis_size("tp")
    depth = count // PLANE
    rows = chans // groups
    part = groups // PLANE
    quads = part // 4
    lanes = 8 * modes

    def cube(x):
        return x.reshape(rows, groups, length)

    query, key, value, grad = cube(queries), cube(keys_in), cube(values_in), cube(grad_out)
    decay, resid = decay_rate.T, residue.T
    vmem = pl.BlockSpec(memory_space=pltpu.VMEM)
    anywhere = pl.BlockSpec(memory_space=pltpu.HBM)

    def shaped(shape, dtype):
        return jax.ShapeDtypeStruct(shape, dtype)

    def call(kernel, in_specs, out_specs, out_shape, scratch, flops, size, aliases=None):
        return pl.pallas_call(
            kernel,
            in_specs=in_specs,
            out_specs=out_specs,
            out_shape=out_shape,
            scratch_shapes=scratch,
            cost_estimate=pl.CostEstimate(flops=flops, bytes_accessed=size, transcendentals=0),
            compiler_params=pltpu.CompilerParams(vmem_limit_bytes=16 * 2**20),
            input_output_aliases=aliases or {},
        )

    def in_hbm(*arrays):
        return [pltpu.with_memory_space_constraint(x, pltpu.HBM) for x in arrays]

    def reducer(slots):
        return [
            pltpu.VMEM((4, slots, rows, part, length), BF16),
            pltpu.SemaphoreType.DMA((4, slots)),
        ] + [pltpu.VMEM((slots, part // 8, rows * 8, length), F32)] * 2

    quarter = (part, 2 * rows, length)
    block = shaped((quads, 2 * rows, lanes), BF16)
    xc, weights, rates, *own = call(
        states_kernel,
        [anywhere] * 5,
        [vmem] * (2 + PLANE),
        [
            shaped((PLANE - 1,) + quarter, BF16),
            shaped((groups, 2, modes, length), BF16),
            shaped((groups // 4, lanes), F32),
        ]
        + [block] * (PLANE - 1),
        [pltpu.VMEM((modes, groups), F32), pltpu.SemaphoreType.DMA] + reducer(PLANE - 1),
        10**9,
        4 * 10**6,
    )(*in_hbm(decay, key, value, grad, query))

    def swap(x, bits):
        return lax.ppermute(x, "ctx", [(i, i ^ bits) for i in range(count)])

    near = []
    for i in range(1, PLANE):
        near.append(swap(own[i - 1], i))
    xo, mine, sums = call(
        sums_kernel,
        [anywhere] * 4 + [vmem] * 3,
        [vmem] * 3,
        [shaped(quarter, BF16), block, shaped((2 * modes, lanes), F32)],
        reducer(1) + [pltpu.VMEM((groups, length), F32)],
        10**9,
        4 * 10**6,
    )(*in_hbm(key, value, grad, query), xc, weights, decay)
    near = [mine] + near
    flat = quads * 2 * rows
    plane = call(
        functools.partial(plane_kernel, length),
        [vmem] * (2 + PLANE),
        vmem,
        shaped((flat + 2 * modes, lanes), BF16),
        [pltpu.VMEM((2 * modes, lanes), F32)],
        10**7,
        10**6,
    )(rates, *near, sums)
    line = [plane] + [swap(plane, PLANE * i) for i in range(1, depth)]
    near_part, taps = call(
        local_kernel,
        [vmem] * 5,
        [vmem] * 2,
        [
            shaped((PLANE,) + quarter, F32),
            shaped((PLANE, part, modes, length), BF16),
        ],
        [
            pltpu.VMEM((PLANE, part, length, length), BF16),
            pltpu.VMEM((PLANE, part, length), F32),
            pltpu.VMEM((PLANE, part, 16, length), BF16),
        ],
        10**9,
        4 * 10**6,
    )(xo, xc, decay, resid, plane)
    sent = call(
        functools.partial(line_kernel, length),
        [vmem] * (2 + PLANE + depth),
        [vmem] * PLANE,
        [shaped((flat // 2 + 2 * modes, lanes), BF16)] * PLANE,
        [pltpu.VMEM((2 * modes, lanes), F32)],
        10**7,
        10**6,
    )(rates, taps, *near, *line)
    back = [sent[0]]
    for i in range(1, PLANE):
        back.append(swap(sent[i], i))

    total = sum(
        b[flat // 2 :, : lanes // 2].astype(F32) + b[flat // 2 :, lanes // 2 :].astype(F32)
        for b in back
    )
    bit = 1
    while bit < tp:
        total = total + lax.ppermute(total, "tp", [(i, i ^ bit) for i in range(tp)])
        bit *= 2

    outs = ()
    for indices in ((0,), (PLANE - 1, 1), (2,)):
        slots = len(indices)
        outs = call(
            functools.partial(outputs_kernel, indices),
            [vmem] * (5 + slots) + [anywhere] * len(outs),
            [anywhere] * 3,
            [shaped((rows, groups, length), BF16)] * 3,
            [
                pltpu.VMEM((3, slots, rows, part, length), BF16),
                pltpu.SemaphoreType.DMA((3, slots)),
                pltpu.VMEM((slots, part // 8, rows * 8, length), F32),
                pltpu.VMEM((slots, part // 8, rows * 8, length), F32),
            ],
            2 * 10**8 * slots,
            10**6 * slots,
            {5 + slots + i: i for i in range(len(outs))},
        )(key, value, grad, near_part, taps, *(back[i] for i in indices), *outs)
    tokens = count * length
    plain, moment = total[:modes, :groups], total[modes:, :groups]
    return (
        *(x.reshape(chans, length) for x in outs),
        (plain / tokens).T,
        (-(resid * decay) * moment / tokens).T,
    )


def solution(mesh):
    in_specs = (P("tp", "ctx"), P("tp", "ctx"), P("tp", "ctx"), P("tp", "ctx"), P(), P())
    out_specs = (P("tp", "ctx"), P("tp", "ctx"), P("tp", "ctx"), P(), P())
    return jax.shard_map(
        gradients, mesh=mesh, in_specs=in_specs, out_specs=out_specs, check_vma=False
    )
```

```python
import functools

import jax
import jax.numpy as jnp
from jax import lax
from jax.experimental import pallas as pl
from jax.experimental.pallas import tpu as pltpu
from jax.sharding import PartitionSpec as P

F32 = jnp.float32
BF16 = jnp.bfloat16
PLANE = 4
NT = (((1,), (1,)), ((), ()))
NN = (((1,), (0,)), ((), ()))
TN = (((0,), (0,)), ((), ()))


def dot(a, b, dims):
    return lax.dot_general(a, b, dims, preferred_element_type=F32)


def product(a, b):
    return a.astype(BF16) * b.astype(BF16)


def column(table, group):
    return jnp.sum(jnp.where(lane_iota(table.shape) == group, table, 0.0), axis=1, keepdims=True)


def mirror_of(length):
    total = lane_iota((length, length)) + lax.broadcasted_iota(jnp.int32, (length, length), 0)
    return jnp.where(total == length - 1, 1.0, 0.0).astype(BF16)


def places():
    me = lax.axis_index("ctx")
    return lax.rem(me, PLANE), lax.div(me, PLANE)


def lane_iota(shape):
    return lax.broadcasted_iota(jnp.int32, shape, len(shape) - 1)


class Reducer:
    def __init__(self, sources, bufs, sems, w_ref, gs, cs):
        self.sources, self.bufs, self.sems, self.w_ref, self.gs, self.cs = (
            sources, bufs, sems, w_ref, gs, cs
        )
        _, self.rows, self.part, self.length = bufs.shape[1:]
        self.mirror = mirror_of(self.length)

    def copies(self, slot, quarter):
        return [
            pltpu.make_async_copy(
                source.at[:, pl.ds(pl.multiple_of(quarter * self.part, self.part), self.part), :],
                self.bufs.at[which, slot],
                self.sems.at[which, slot],
            )
            for which, source in enumerate(self.sources)
        ]

    def load(self, slot, quarter):
        for copy in self.copies(slot, quarter):
            copy.wait()
        bufs, flat = self.bufs, self.rows * self.part
        x = product(bufs[0, slot], bufs[1, slot]).astype(F32)
        c = product(bufs[2, slot], bufs[3, slot]).reshape(flat, self.length)
        c = dot(c, self.mirror, NN).reshape(x.shape)
        for eight in range(self.part // 8):
            span = slice(8 * eight, 8 * eight + 8)
            self.gs[slot, eight] = x[:, span].reshape(8 * self.rows, self.length)
            self.cs[slot, eight] = c[:, span].reshape(8 * self.rows, self.length)

    def reduce(self, slot, quarter, xc_ref, out_ref):
        modes = self.w_ref.shape[2]
        lane = lane_iota((2 * self.rows, 8 * modes)) % (4 * modes)
        for quad in range(self.part // 4):
            left, right = [], [[], []]
            for side in range(4):
                local = 4 * quad + side
                group = quarter * self.part + local
                where = pl.ds(local % 8, self.rows, stride=8)
                both = jnp.concatenate(
                    [ref[slot, local // 8, where, :] for ref in (self.gs, self.cs)], axis=0
                ).astype(BF16)
                xc_ref[local] = both
                left.append(both)
                right[0].append(self.w_ref[group, 0])
                right[1].append(self.w_ref[group, 1])
            every = dot(
                jnp.concatenate(left, axis=0), jnp.concatenate(right[0] + right[1], axis=0), NT
            )
            every = every.reshape(4, 2 * self.rows, 8 * modes)
            found = every[0]
            for side in range(1, 4):
                found = jnp.where(lane >= side * modes, every[side], found)
            out_ref[quad] = found.astype(BF16)


def states_kernel(dec_hbm, k_hbm, v_hbm, g_hbm, q_hbm, xc_ref, w_ref, rate_ref, *rest):
    outs, rest = rest[: PLANE - 1], rest[PLANE - 1 :]
    dec_ref, dec_sem, bufs, sems, gs, cs = rest
    place, _ = places()
    modes, groups = dec_ref.shape
    work = Reducer((k_hbm, v_hbm, g_hbm, q_hbm), bufs, sems, w_ref, gs, cs)
    length = work.length
    rates_in = pltpu.make_async_copy(dec_hbm, dec_ref, dec_sem)
    rates_in.start()
    for slot in range(PLANE - 1):
        for copy in work.copies(slot, place ^ (slot + 1)):
            copy.start()
    rates_in.wait()
    dec = dec_ref[...]
    behind = float(length) - lane_iota((modes, length)).astype(F32)
    wide = (modes, 8 * modes)
    target = lane_iota(wide) % (4 * modes) - lax.broadcasted_iota(jnp.int32, wide, 0)

    def weights(index, _):
        rates = jnp.zeros(wide, F32)
        for side in range(4):
            group = 4 * index + side
            rate = column(dec, group)
            basis = jnp.exp(-rate * behind)
            w_ref[group, 0] = basis.astype(BF16)
            w_ref[group, 1] = (behind * basis).astype(BF16)
            rates = jnp.where(target == side * modes, rate, rates)
        rate_ref[pl.ds(index, 1), :] = jnp.sum(rates, axis=0, keepdims=True)
        return 0

    lax.fori_loop(0, groups // 4, weights, 0, unroll=4)
    for slot in range(PLANE):
        if slot < PLANE - 1:
            work.load(slot, place ^ (slot + 1))
        if slot > 0:
            work.reduce(slot - 1, place ^ slot, xc_ref.at[slot - 1], outs[slot - 1])


def sums_kernel(k_hbm, v_hbm, g_hbm, q_hbm, xc_ref, w_ref, dec_ref, own_ref, out_ref, sums_ref, *rest):
    bufs, sems, gs, cs, prods_ref = rest
    place, _ = places()
    work = Reducer((k_hbm, v_hbm, g_hbm, q_hbm), bufs, sems, w_ref, gs, cs)
    for copy in work.copies(0, place):
        copy.start()
    _, part, rows, length = xc_ref.shape
    rows = rows // 2
    modes = dec_ref.shape[0]
    paired = (
        lane_iota((length, length)) + lax.broadcasted_iota(jnp.int32, (length, length), 0) < length
    )

    def multiply(index, ref):
        for local in range(part):
            prods = dot(ref[local, :rows], ref[local, rows:], TN)
            prods_ref[index, local] = jnp.where(paired, prods, 0.0).astype(BF16)

    def others(index, _):
        multiply(index, xc_ref.at[index - 1])
        return 0

    lax.fori_loop(1, PLANE, others, 0)
    work.load(0, place)
    work.reduce(0, place, own_ref, out_ref)
    multiply(0, own_ref)
    dec = dec_ref[...]
    middle = float(length // 2) - lane_iota((modes, length)).astype(F32)
    lane = lane_iota((modes, sums_ref.shape[1]))

    def contract(index, carry):
        plain, moment = carry
        for local in range(part):
            group = (place ^ index) * part + local
            rate = column(dec, group)
            basis = jnp.exp(-rate * middle)
            left = jnp.concatenate([basis, middle * basis], axis=0).astype(BF16)
            both = dot(left, prods_ref[index, local], NN)
            basis = basis * jnp.exp(rate)
            first = jnp.sum(basis * both[:modes], axis=1, keepdims=True)
            second = basis * ((middle - 1.0) * both[:modes] + both[modes:])
            plain = jnp.where(lane == group, first, plain)
            moment = jnp.where(lane == group, jnp.sum(second, axis=1, keepdims=True), moment)
        return plain, moment

    zero = jnp.zeros(lane.shape, F32)
    plain, moment = lax.fori_loop(0, PLANE, contract, (zero, zero))
    sums_ref[:modes] = plain
    sums_ref[modes:] = moment


def local_kernel(own_ref, xc_ref, dec_ref, res_ref, after_ref, out_ref, taps_ref, *scratch):
    toep_ref, rows_ref, bands_ref = scratch
    _, part, _, length = xc_ref.shape
    modes = dec_ref.shape[0]
    place, _ = places()
    dec, res = dec_ref[...], res_ref[...]
    ahead = lane_iota((modes, length)).astype(F32)
    step = 16
    lane = lane_iota((step, length))
    row = lax.broadcasted_iota(jnp.int32, (step, length), 0)

    def each(body):
        def run(index, _):
            body(index)
            return 0

        lax.fori_loop(0, PLANE, run, 0)

    @each
    def _(index):
        first_group = (place ^ index) * part
        for local in range(part):
            rate, weight = column(dec, first_group + local), column(res, first_group + local)
            taps = weight * jnp.exp(-rate * ahead)
            taps_ref[index, local] = taps.astype(BF16)
            rows_ref[index, local : local + 1] = jnp.sum(taps, axis=0, keepdims=True)

    @each
    def _(index):
        for local in range(part):
            taps = jnp.broadcast_to(rows_ref[index, local : local + 1], (step, length))
            bands_ref[index, local] = pltpu.roll(taps, 0, 1, stride=1, stride_axis=0).astype(BF16)

    @each
    def _(index):
        for local in range(part):
            band = bands_ref[index, local]
            for first in range(0, length, step):
                toep_ref[index, local, first : first + step] = jnp.where(
                    lane >= row + first, pltpu.roll(band, first, 1), 0.0
                )

    def convolve(index, ref):
        for local in range(part):
            out_ref[index, local] = dot(ref[local], toep_ref[index, local], NN)

    convolve(0, own_ref)

    def others(index, _):
        convolve(index, xc_ref.at[index - 1])
        return 0

    lax.fori_loop(1, PLANE, others, 0)


def split_pair(x, half):
    head = x.astype(BF16).astype(F32)
    tail = (x - head).astype(BF16).astype(F32)
    low = lane_iota(x.shape) < half
    return jnp.where(low, head, pltpu.roll(jnp.where(low, tail, 0.0), half, x.ndim - 1)).astype(BF16)


def join_pair(x, half):
    x = x.astype(F32)
    low = lane_iota(x.shape) < half
    return jnp.where(low, x + pltpu.roll(x, half, x.ndim - 1), 0.0)


def in_order(arrays, place):
    arrays, bit = list(arrays), 1
    while bit < len(arrays):
        swap = (place & bit) != 0
        new = list(arrays)
        for i in range(len(arrays)):
            new[i] = jnp.where(swap, arrays[i ^ bit], arrays[i])
        arrays, bit = new, 2 * bit
    return arrays


def advance(state, decay, gap):
    half = state.shape[2] // 2
    shifted = pltpu.roll(state, half, 2)
    return decay * (state + jnp.where(lane_iota(state.shape) >= half, gap * shifted, 0.0))


def scan_blocks(heads, tails, start, rate, gap):
    decay = jnp.exp(-rate * gap)
    state, before = start[0], []
    for head in heads:
        before.append(state)
        state = advance(state, decay, gap) + head
    other, after = start[1], []
    for tail in tails[::-1]:
        after.insert(0, other)
        other = advance(other, decay, gap) + tail
    return before, after, state, other


def pair_terms(before, tails, rate):
    half = rate.shape[2] // 2
    plain, moment = 0.0, 0.0
    for state, tail in zip(before, tails, strict=True):
        plain = plain + state * tail
        moment = moment + state * pltpu.roll(tail, half, 2)
    plain, moment = jnp.sum(plain, axis=1), jnp.sum(moment, axis=1)
    moment = moment + pltpu.roll(moment, half, 1) - pltpu.roll(plain, half, 1)
    return jnp.where(lane_iota(plain.shape) < half, plain, moment) * jnp.exp(rate[:, 0])


def spread(terms, place, acc, modes):
    quads, lanes = terms.shape
    parts = []
    for _ in range(3):
        parts.append(terms.astype(BF16))
        terms = terms - parts[-1].astype(F32)
    parts = jnp.concatenate([x.astype(F32) for x in parts], axis=0)
    shape = (3 * quads, 4 * lanes)
    lane = lane_iota(shape)
    row = lax.broadcasted_iota(jnp.int32, shape, 0) % quads
    group = lane % lanes - 4 * quads * place
    chosen = jnp.where(group == 4 * row + lane // lanes, 1.0, 0.0)
    turned = dot(parts.astype(BF16), chosen.astype(BF16), TN)
    for side in range(4):
        span = slice(side * lanes, (side + 1) * lanes)
        acc[:modes] += turned[side * modes : (side + 1) * modes, span]
        acc[modes:] += turned[(4 + side) * modes : (5 + side) * modes, span]


def own_rates(rate_ref, place, quads):
    rate = rate_ref[pl.ds(place * quads, quads), :]
    return rate.reshape(quads, 1, rate.shape[1])


def halves(blocks, rows):
    blocks = [b.astype(F32) for b in blocks]
    return [b[:, :rows] for b in blocks], [b[:, rows:] for b in blocks]


def plane_kernel(length, rate_ref, *refs):
    *msgs, sums_ref, out_ref, acc = refs
    place, _ = places()
    quads, rows, lanes = msgs[0].shape
    rows, flat = rows // 2, quads * rows
    modes = lanes // 8
    heads, tails = halves(in_order([m[...] for m in msgs], place), rows)
    rate = own_rates(rate_ref, place, quads)
    nothing = jnp.zeros_like(heads[0])
    before, _, head, tail = scan_blocks(heads, tails, (nothing, nothing), rate, float(length))
    both = jnp.concatenate([head, tail], axis=1)
    out_ref[:flat] = both.astype(BF16).reshape(flat, lanes)
    acc[...] = sums_ref[...]
    spread(pair_terms(before, tails, rate), place, acc, modes)
    out_ref[flat:] = split_pair(acc[...], lanes // 2)


def line_kernel(length, rate_ref, after_ref, *refs):
    count = len(refs) - 2 * PLANE - 1
    msgs, lines = refs[:PLANE], refs[PLANE : PLANE + count]
    outs, acc = refs[PLANE + count : -1], refs[-1]
    place, level = places()
    quads, rows, lanes = msgs[0].shape
    shape = (quads, rows, lanes)
    rows, flat = rows // 2, quads * rows
    modes = lanes // 8
    rate = own_rates(rate_ref, place, quads)
    heads, tails = halves(
        in_order([r[:flat].reshape(shape) for r in lines], level), rows
    )
    nothing = jnp.zeros_like(heads[0])
    before, after, _, _ = scan_blocks(
        heads, tails, (nothing, nothing), rate, float(PLANE * length)
    )
    total = join_pair(lines[0][flat:], lanes // 2)
    for r in lines[1:]:
        total = total + join_pair(r[flat:], lanes // 2)
    acc[...] = total
    spread(pair_terms(before, tails, rate), place, acc, modes)
    sums = split_pair(acc[...], lanes // 2)
    start = [nothing, nothing]
    for i in range(count):
        start[0] = jnp.where(level == i, before[i], start[0])
        start[1] = jnp.where(level == i, after[i], start[1])
    heads, tails = halves(in_order([m[...] for m in msgs], place), rows)
    decay = jnp.exp(-rate * float(length))
    before, after = [start[0]], [start[1]]
    for i in range(PLANE - 1):
        before.append(decay * before[-1] + heads[i])
        after.insert(0, decay * after[0] + tails[PLANE - 1 - i])
    low = lane_iota((quads // 2, 2 * rows, lanes)) < lanes // 2
    packed = []
    for pair in zip(before, after, strict=True):
        found = jnp.concatenate(pair, axis=1)
        found = jnp.where(low, found[: quads // 2], pltpu.roll(found[quads // 2 :], lanes // 2, 2))
        packed.append(found.astype(BF16).reshape(flat // 2, lanes))
    for i, found in enumerate(in_order(packed, place)):
        outs[i][: flat // 2] = found
        outs[i][flat // 2 :] = sums


def outputs_kernel(indices, k_ref, v_ref, g_ref, near_ref, taps_ref, *refs):
    count = len(indices)
    states, refs = refs[:count], refs[count:]
    results, (outs, sems, cs, gs) = refs[-7:-4], refs[-4:]
    place, _ = places()
    _, _, rows, part, length = outs.shape
    modes = taps_ref.shape[2]
    quads = part // 4
    mirror = mirror_of(length)
    spans = [
        pl.ds(pl.multiple_of((place ^ index) * part, part), part) for index in indices
    ]

    def store(which, slot):
        return pltpu.make_async_copy(
            outs.at[which, slot], results[which].at[:, spans[slot], :], sems.at[which, slot]
        )

    def expand(slot):
        index, state_ref = indices[slot], states[slot]
        half = quads // 2
        lane = lane_iota((2 * rows, 8 * modes))
        for quad in range(half):
            state = state_ref[2 * rows * quad : 2 * rows * (quad + 1)]
            locals_ = [4 * (quad + half * (i // 4)) + i % 4 for i in range(8)]
            left = [
                jnp.where((lane >= modes * i) & (lane < modes * (i + 1)), state, 0.0)
                for i in range(8)
            ]
            right = [taps_ref[index, local] for local in locals_]
            every = dot(jnp.concatenate(left, axis=0), jnp.concatenate(right, axis=0), NN)
            every = every.reshape(8, 2 * rows, length)
            for i, local in enumerate(locals_):
                both = every[i] + near_ref[index, local]
                where = pl.ds(local % 8, rows, stride=8)
                cs[slot, local // 8, where, :] = both[:rows]
                gs[slot, local // 8, where, :] = both[rows:]

    def finish(slot):
        def natural(ref):
            pieces = [ref[slot, i].reshape(rows, 8, length) for i in range(part // 8)]
            return jnp.concatenate(pieces, axis=1).astype(BF16)

        own = spans[slot]
        ig = dot(natural(gs).reshape(rows * part, length), mirror, NN)
        outs[0, slot] = product(g_ref[:, own, :], natural(cs))
        store(0, slot).start()
        ig = ig.astype(BF16).reshape(rows, part, length)
        outs[1, slot] = product(ig, v_ref[:, own, :])
        store(1, slot).start()
        outs[2, slot] = product(ig, k_ref[:, own, :])
        store(2, slot).start()

    for slot in range(count + 1):
        if slot < count:
            expand(slot)
        if slot > 0:
            finish(slot - 1)
    for slot in range(count):
        for which in range(3):
            store(which, slot).wait()


def gradients(queries, keys_in, values_in, grad_out, residue, decay_rate):
    chans, length = queries.shape
    groups, modes = residue.shape
    count = lax.axis_size("ctx")
    tp = lax.axis_size("tp")
    depth = count // PLANE
    rows = chans // groups
    part = groups // PLANE
    quads = part // 4
    lanes = 8 * modes

    def cube(x):
        return x.reshape(rows, groups, length)

    query, key, value, grad = cube(queries), cube(keys_in), cube(values_in), cube(grad_out)
    decay, resid = decay_rate.T, residue.T
    vmem = pl.BlockSpec(memory_space=pltpu.VMEM)
    anywhere = pl.BlockSpec(memory_space=pltpu.HBM)

    def shaped(shape, dtype):
        return jax.ShapeDtypeStruct(shape, dtype)

    def call(kernel, in_specs, out_specs, out_shape, scratch, flops, size, aliases=None):
        return pl.pallas_call(
            kernel,
            in_specs=in_specs,
            out_specs=out_specs,
            out_shape=out_shape,
            scratch_shapes=scratch,
            cost_estimate=pl.CostEstimate(flops=flops, bytes_accessed=size, transcendentals=0),
            compiler_params=pltpu.CompilerParams(vmem_limit_bytes=16 * 2**20),
            input_output_aliases=aliases or {},
        )

    def in_hbm(*arrays):
        return [pltpu.with_memory_space_constraint(x, pltpu.HBM) for x in arrays]

    def reducer(slots):
        return [
            pltpu.VMEM((4, slots, rows, part, length), BF16),
            pltpu.SemaphoreType.DMA((4, slots)),
        ] + [pltpu.VMEM((slots, part // 8, rows * 8, length), F32)] * 2

    quarter = (part, 2 * rows, length)
    block = shaped((quads, 2 * rows, lanes), BF16)
    xc, weights, rates, *own = call(
        states_kernel,
        [anywhere] * 5,
        [vmem] * (2 + PLANE),
        [
            shaped((PLANE - 1,) + quarter, BF16),
            shaped((groups, 2, modes, length), BF16),
            shaped((groups // 4, lanes), F32),
        ]
        + [block] * (PLANE - 1),
        [pltpu.VMEM((modes, groups), F32), pltpu.SemaphoreType.DMA] + reducer(PLANE - 1),
        10**9,
        4 * 10**6,
    )(*in_hbm(decay, key, value, grad, query))

    def swap(x, bits):
        return lax.ppermute(x, "ctx", [(i, i ^ bits) for i in range(count)])

    near = []
    for i in range(1, PLANE):
        near.append(swap(own[i - 1], i))
    xo, mine, sums = call(
        sums_kernel,
        [anywhere] * 4 + [vmem] * 3,
        [vmem] * 3,
        [shaped(quarter, BF16), block, shaped((2 * modes, lanes), F32)],
        reducer(1) + [pltpu.VMEM((PLANE, part, length, length), BF16)],
        10**9,
        4 * 10**6,
    )(*in_hbm(key, value, grad, query), xc, weights, decay)
    near = [mine] + near
    flat = quads * 2 * rows
    plane = call(
        functools.partial(plane_kernel, length),
        [vmem] * (2 + PLANE),
        vmem,
        shaped((flat + 2 * modes, lanes), BF16),
        [pltpu.VMEM((2 * modes, lanes), F32)],
        10**7,
        10**6,
    )(rates, *near, sums)
    line = [plane] + [swap(plane, PLANE * i) for i in range(1, depth)]
    near_part, taps = call(
        local_kernel,
        [vmem] * 5,
        [vmem] * 2,
        [
            shaped((PLANE,) + quarter, F32),
            shaped((PLANE, part, modes, length), BF16),
        ],
        [
            pltpu.VMEM((PLANE, part, length, length), BF16),
            pltpu.VMEM((PLANE, part, length), F32),
            pltpu.VMEM((PLANE, part, 16, length), BF16),
        ],
        10**9,
        4 * 10**6,
    )(xo, xc, decay, resid, plane)
    sent = call(
        functools.partial(line_kernel, length),
        [vmem] * (2 + PLANE + depth),
        [vmem] * PLANE,
        [shaped((flat // 2 + 2 * modes, lanes), BF16)] * PLANE,
        [pltpu.VMEM((2 * modes, lanes), F32)],
        10**7,
        10**6,
    )(rates, taps, *near, *line)
    back = [sent[0]]
    for i in range(1, PLANE):
        back.append(swap(sent[i], i))

    total = sum(
        b[flat // 2 :, : lanes // 2].astype(F32) + b[flat // 2 :, lanes // 2 :].astype(F32)
        for b in back
    )
    bit = 1
    while bit < tp:
        total = total + lax.ppermute(total, "tp", [(i, i ^ bit) for i in range(tp)])
        bit *= 2

    outs = ()
    for indices in ((0,), (PLANE - 1,), tuple(range(1, PLANE - 1))):
        slots = len(indices)
        outs = call(
            functools.partial(outputs_kernel, indices),
            [vmem] * (5 + slots) + [anywhere] * len(outs),
            [anywhere] * 3,
            [shaped((rows, groups, length), BF16)] * 3,
            [
                pltpu.VMEM((3, slots, rows, part, length), BF16),
                pltpu.SemaphoreType.DMA((3, slots)),
                pltpu.VMEM((slots, part // 8, rows * 8, length), F32),
                pltpu.VMEM((slots, part // 8, rows * 8, length), F32),
            ],
            2 * 10**8 * slots,
            10**6 * slots,
            {5 + slots + i: i for i in range(len(outs))},
        )(key, value, grad, near_part, taps, *(back[i] for i in indices), *outs)
    tokens = count * length
    plain, moment = total[:modes, :groups], total[modes:, :groups]
    return (
        *(x.reshape(chans, length) for x in outs),
        (plain / tokens).T,
        (-(resid * decay) * moment / tokens).T,
    )


def solution(mesh):
    in_specs = (P("tp", "ctx"), P("tp", "ctx"), P("tp", "ctx"), P("tp", "ctx"), P(), P())
    out_specs = (P("tp", "ctx"), P("tp", "ctx"), P("tp", "ctx"), P(), P())
    return jax.shard_map(
        gradients, mesh=mesh, in_specs=in_specs, out_specs=out_specs, check_vma=False
    )
```

```python
import functools

import jax
import jax.numpy as jnp
from jax import lax
from jax.experimental import pallas as pl
from jax.experimental.pallas import tpu as pltpu
from jax.sharding import PartitionSpec as P

F32 = jnp.float32
BF16 = jnp.bfloat16
PLANE = 4
NT = (((1,), (1,)), ((), ()))
NN = (((1,), (0,)), ((), ()))
TN = (((0,), (0,)), ((), ()))


def dot(a, b, dims):
    return lax.dot_general(a, b, dims, preferred_element_type=F32)


def product(a, b):
    return a.astype(BF16) * b.astype(BF16)


def column(table, group):
    return jnp.sum(jnp.where(lane_iota(table.shape) == group, table, 0.0), axis=1, keepdims=True)


def mirror_of(length):
    total = lane_iota((length, length)) + lax.broadcasted_iota(jnp.int32, (length, length), 0)
    return jnp.where(total == length - 1, 1.0, 0.0).astype(BF16)


def places():
    me = lax.axis_index("ctx")
    return lax.rem(me, PLANE), lax.div(me, PLANE)


def lane_iota(shape):
    return lax.broadcasted_iota(jnp.int32, shape, len(shape) - 1)


class Reducer:
    def __init__(self, sources, bufs, sems, w_ref, gs, cs):
        self.sources, self.bufs, self.sems, self.w_ref, self.gs, self.cs = (
            sources, bufs, sems, w_ref, gs, cs
        )
        _, self.rows, self.part, self.length = bufs.shape[1:]
        self.mirror = mirror_of(self.length)

    def copies(self, slot, quarter):
        return [
            pltpu.make_async_copy(
                source.at[:, pl.ds(pl.multiple_of(quarter * self.part, self.part), self.part), :],
                self.bufs.at[which, slot],
                self.sems.at[which, slot],
            )
            for which, source in enumerate(self.sources)
        ]

    def load(self, slot, quarter):
        for copy in self.copies(slot, quarter):
            copy.wait()
        bufs, flat = self.bufs, self.rows * self.part
        x = product(bufs[0, slot], bufs[1, slot]).astype(F32)
        c = product(bufs[2, slot], bufs[3, slot]).reshape(flat, self.length)
        c = dot(c, self.mirror, NN).reshape(x.shape)
        for eight in range(self.part // 8):
            span = slice(8 * eight, 8 * eight + 8)
            self.gs[slot, eight] = x[:, span].reshape(8 * self.rows, self.length)
            self.cs[slot, eight] = c[:, span].reshape(8 * self.rows, self.length)

    def reduce(self, slot, quarter, xc_ref, out_ref):
        modes = self.w_ref.shape[2]
        lane = lane_iota((2 * self.rows, 8 * modes)) % (4 * modes)
        for quad in range(self.part // 4):
            left, right = [], [[], []]
            for side in range(4):
                local = 4 * quad + side
                group = quarter * self.part + local
                where = pl.ds(local % 8, self.rows, stride=8)
                both = jnp.concatenate(
                    [ref[slot, local // 8, where, :] for ref in (self.gs, self.cs)], axis=0
                ).astype(BF16)
                xc_ref[local] = both
                left.append(both)
                right[0].append(self.w_ref[group, 0])
                right[1].append(self.w_ref[group, 1])
            every = dot(
                jnp.concatenate(left, axis=0), jnp.concatenate(right[0] + right[1], axis=0), NT
            )
            every = every.reshape(4, 2 * self.rows, 8 * modes)
            found = every[0]
            for side in range(1, 4):
                found = jnp.where(lane >= side * modes, every[side], found)
            out_ref[quad] = found.astype(BF16)


def states_kernel(dec_hbm, k_hbm, v_hbm, g_hbm, q_hbm, xc_ref, w_ref, rate_ref, *rest):
    outs, rest = rest[: PLANE - 1], rest[PLANE - 1 :]
    dec_ref, dec_sem, bufs, sems, gs, cs = rest
    place, _ = places()
    modes, groups = dec_ref.shape
    work = Reducer((k_hbm, v_hbm, g_hbm, q_hbm), bufs, sems, w_ref, gs, cs)
    length = work.length
    rates_in = pltpu.make_async_copy(dec_hbm, dec_ref, dec_sem)
    rates_in.start()
    for slot in range(PLANE - 1):
        for copy in work.copies(slot, place ^ (slot + 1)):
            copy.start()
    rates_in.wait()
    dec = dec_ref[...]
    behind = float(length) - lane_iota((modes, length)).astype(F32)
    wide = (modes, 8 * modes)
    target = lane_iota(wide) % (4 * modes) - lax.broadcasted_iota(jnp.int32, wide, 0)

    def weights(index, _):
        rates = jnp.zeros(wide, F32)
        for side in range(4):
            group = 4 * index + side
            rate = column(dec, group)
            basis = jnp.exp(-rate * behind)
            w_ref[group, 0] = basis.astype(BF16)
            w_ref[group, 1] = (behind * basis).astype(BF16)
            rates = jnp.where(target == side * modes, rate, rates)
        rate_ref[pl.ds(index, 1), :] = jnp.sum(rates, axis=0, keepdims=True)
        return 0

    lax.fori_loop(0, groups // 4, weights, 0, unroll=4)
    for slot in range(PLANE):
        if slot < PLANE - 1:
            work.load(slot, place ^ (slot + 1))
        if slot > 0:
            work.reduce(slot - 1, place ^ slot, xc_ref.at[slot - 1], outs[slot - 1])


def sums_kernel(k_hbm, v_hbm, g_hbm, q_hbm, xc_ref, w_ref, dec_ref, own_ref, out_ref, sums_ref, *rest):
    bufs, sems, gs, cs, prods_ref, left_ref, basis_ref = rest
    place, _ = places()
    work = Reducer((k_hbm, v_hbm, g_hbm, q_hbm), bufs, sems, w_ref, gs, cs)
    for copy in work.copies(0, place):
        copy.start()
    _, part, rows, length = xc_ref.shape
    rows = rows // 2
    modes = dec_ref.shape[0]
    paired = (
        lane_iota((length, length)) + lax.broadcasted_iota(jnp.int32, (length, length), 0) < length
    )

    def multiply(index, ref):
        for local in range(part):
            prods = dot(ref[local, :rows], ref[local, rows:], TN)
            prods_ref[index, local] = jnp.where(paired, prods, 0.0).astype(BF16)

    multiply(1, xc_ref.at[0])
    work.load(0, place)
    multiply(2, xc_ref.at[1])
    work.reduce(0, place, own_ref, out_ref)
    multiply(3, xc_ref.at[2])
    multiply(0, own_ref)
    dec = dec_ref[...]
    middle = float(length // 2) - lane_iota((modes, length)).astype(F32)
    lane = lane_iota((modes, sums_ref.shape[1]))

    def tables(index, _):
        for local in range(part):
            rate = column(dec, (place ^ index) * part + local)
            basis = jnp.exp(-rate * middle)
            left_ref[index, local] = jnp.concatenate([basis, middle * basis], axis=0).astype(BF16)
            basis_ref[index, local] = basis * jnp.exp(rate)
        return 0

    lax.fori_loop(0, PLANE, tables, 0, unroll=2)

    def contract(index, carry):
        plain, moment = carry
        for local in range(part):
            group = (place ^ index) * part + local
            both = dot(left_ref[index, local], prods_ref[index, local], NN)
            basis = basis_ref[index, local]
            first = jnp.sum(basis * both[:modes], axis=1, keepdims=True)
            second = basis * ((middle - 1.0) * both[:modes] + both[modes:])
            plain = jnp.where(lane == group, first, plain)
            moment = jnp.where(lane == group, jnp.sum(second, axis=1, keepdims=True), moment)
        return plain, moment

    zero = jnp.zeros(lane.shape, F32)
    plain, moment = lax.fori_loop(0, PLANE, contract, (zero, zero), unroll=True)
    sums_ref[:modes] = plain
    sums_ref[modes:] = moment


def local_kernel(own_ref, xc_ref, dec_ref, res_ref, after_ref, out_ref, taps_ref, *scratch):
    toep_ref, rows_ref, bands_ref = scratch
    _, part, _, length = xc_ref.shape
    modes = dec_ref.shape[0]
    place, _ = places()
    dec, res = dec_ref[...], res_ref[...]
    ahead = lane_iota((modes, length)).astype(F32)
    step = 16
    lane = lane_iota((step, length))
    row = lax.broadcasted_iota(jnp.int32, (step, length), 0)

    def each(body):
        def run(index, _):
            body(index)
            return 0

        lax.fori_loop(0, PLANE, run, 0)

    @each
    def _(index):
        first_group = (place ^ index) * part
        for local in range(part):
            rate, weight = column(dec, first_group + local), column(res, first_group + local)
            taps = weight * jnp.exp(-rate * ahead)
            taps_ref[index, local] = taps.astype(BF16)
            rows_ref[index, local : local + 1] = jnp.sum(taps, axis=0, keepdims=True)

    @each
    def _(index):
        for local in range(part):
            taps = jnp.broadcast_to(rows_ref[index, local : local + 1], (step, length))
            bands_ref[index, local] = pltpu.roll(taps, 0, 1, stride=1, stride_axis=0).astype(BF16)

    @each
    def _(index):
        for local in range(part):
            band = bands_ref[index, local]
            for first in range(0, length, step):
                toep_ref[index, local, first : first + step] = jnp.where(
                    lane >= row + first, pltpu.roll(band, first, 1), 0.0
                )

    def convolve(index, ref):
        for local in range(part):
            out_ref[index, local] = dot(ref[local], toep_ref[index, local], NN)

    convolve(0, own_ref)

    def others(index, _):
        convolve(index, xc_ref.at[index - 1])
        return 0

    lax.fori_loop(1, PLANE, others, 0)


def split_pair(x, half):
    head = x.astype(BF16).astype(F32)
    tail = (x - head).astype(BF16).astype(F32)
    low = lane_iota(x.shape) < half
    return jnp.where(low, head, pltpu.roll(jnp.where(low, tail, 0.0), half, x.ndim - 1)).astype(BF16)


def join_pair(x, half):
    x = x.astype(F32)
    low = lane_iota(x.shape) < half
    return jnp.where(low, x + pltpu.roll(x, half, x.ndim - 1), 0.0)


def in_order(arrays, place):
    arrays, bit = list(arrays), 1
    while bit < len(arrays):
        swap = (place & bit) != 0
        new = list(arrays)
        for i in range(len(arrays)):
            new[i] = jnp.where(swap, arrays[i ^ bit], arrays[i])
        arrays, bit = new, 2 * bit
    return arrays


def advance(state, decay, gap):
    half = state.shape[2] // 2
    shifted = pltpu.roll(state, half, 2)
    return decay * (state + jnp.where(lane_iota(state.shape) >= half, gap * shifted, 0.0))


def scan_blocks(heads, tails, start, rate, gap):
    decay = jnp.exp(-rate * gap)
    state, before = start[0], []
    for head in heads:
        before.append(state)
        state = advance(state, decay, gap) + head
    other, after = start[1], []
    for tail in tails[::-1]:
        after.insert(0, other)
        other = advance(other, decay, gap) + tail
    return before, after, state, other


def pair_terms(before, tails, rate):
    half = rate.shape[2] // 2
    plain, moment = 0.0, 0.0
    for state, tail in zip(before, tails, strict=True):
        plain = plain + state * tail
        moment = moment + state * pltpu.roll(tail, half, 2)
    plain, moment = jnp.sum(plain, axis=1), jnp.sum(moment, axis=1)
    moment = moment + pltpu.roll(moment, half, 1) - pltpu.roll(plain, half, 1)
    return jnp.where(lane_iota(plain.shape) < half, plain, moment) * jnp.exp(rate[:, 0])


def spread(terms, place, acc, modes):
    quads, lanes = terms.shape
    parts = []
    for _ in range(3):
        parts.append(terms.astype(BF16))
        terms = terms - parts[-1].astype(F32)
    parts = jnp.concatenate([x.astype(F32) for x in parts], axis=0)
    shape = (3 * quads, 4 * lanes)
    lane = lane_iota(shape)
    row = lax.broadcasted_iota(jnp.int32, shape, 0) % quads
    group = lane % lanes - 4 * quads * place
    chosen = jnp.where(group == 4 * row + lane // lanes, 1.0, 0.0)
    turned = dot(parts.astype(BF16), chosen.astype(BF16), TN)
    for side in range(4):
        span = slice(side * lanes, (side + 1) * lanes)
        acc[:modes] += turned[side * modes : (side + 1) * modes, span]
        acc[modes:] += turned[(4 + side) * modes : (5 + side) * modes, span]


def own_rates(rate_ref, place, quads):
    rate = rate_ref[pl.ds(place * quads, quads), :]
    return rate.reshape(quads, 1, rate.shape[1])


def halves(blocks, rows):
    blocks = [b.astype(F32) for b in blocks]
    return [b[:, :rows] for b in blocks], [b[:, rows:] for b in blocks]


def plane_kernel(length, rate_ref, *refs):
    *msgs, sums_ref, out_ref, acc = refs
    place, _ = places()
    quads, rows, lanes = msgs[0].shape
    rows, flat = rows // 2, quads * rows
    modes = lanes // 8
    heads, tails = halves(in_order([m[...] for m in msgs], place), rows)
    rate = own_rates(rate_ref, place, quads)
    nothing = jnp.zeros_like(heads[0])
    before, _, head, tail = scan_blocks(heads, tails, (nothing, nothing), rate, float(length))
    both = jnp.concatenate([head, tail], axis=1)
    out_ref[:flat] = both.astype(BF16).reshape(flat, lanes)
    acc[...] = sums_ref[...]
    spread(pair_terms(before, tails, rate), place, acc, modes)
    out_ref[flat:] = split_pair(acc[...], lanes // 2)


def line_kernel(length, rate_ref, after_ref, *refs):
    count = len(refs) - 2 * PLANE - 1
    msgs, lines = refs[:PLANE], refs[PLANE : PLANE + count]
    outs, acc = refs[PLANE + count : -1], refs[-1]
    place, level = places()
    quads, rows, lanes = msgs[0].shape
    shape = (quads, rows, lanes)
    rows, flat = rows // 2, quads * rows
    modes = lanes // 8
    rate = own_rates(rate_ref, place, quads)
    heads, tails = halves(
        in_order([r[:flat].reshape(shape) for r in lines], level), rows
    )
    nothing = jnp.zeros_like(heads[0])
    before, after, _, _ = scan_blocks(
        heads, tails, (nothing, nothing), rate, float(PLANE * length)
    )
    total = join_pair(lines[0][flat:], lanes // 2)
    for r in lines[1:]:
        total = total + join_pair(r[flat:], lanes // 2)
    acc[...] = total
    spread(pair_terms(before, tails, rate), place, acc, modes)
    sums = split_pair(acc[...], lanes // 2)
    start = [nothing, nothing]
    for i in range(count):
        start[0] = jnp.where(level == i, before[i], start[0])
        start[1] = jnp.where(level == i, after[i], start[1])
    heads, tails = halves(in_order([m[...] for m in msgs], place), rows)
    decay = jnp.exp(-rate * float(length))
    before, after = [start[0]], [start[1]]
    for i in range(PLANE - 1):
        before.append(decay * before[-1] + heads[i])
        after.insert(0, decay * after[0] + tails[PLANE - 1 - i])
    low = lane_iota((quads // 2, 2 * rows, lanes)) < lanes // 2
    packed = []
    for pair in zip(before, after, strict=True):
        found = jnp.concatenate(pair, axis=1)
        found = jnp.where(low, found[: quads // 2], pltpu.roll(found[quads // 2 :], lanes // 2, 2))
        packed.append(found.astype(BF16).reshape(flat // 2, lanes))
    for i, found in enumerate(in_order(packed, place)):
        outs[i][: flat // 2] = found
        outs[i][flat // 2 :] = sums


def outputs_kernel(indices, k_ref, v_ref, g_ref, near_ref, taps_ref, *refs):
    count = len(indices)
    states, refs = refs[:count], refs[count:]
    results, (outs, sems, cs, gs) = refs[-7:-4], refs[-4:]
    place, _ = places()
    _, _, rows, part, length = outs.shape
    modes = taps_ref.shape[2]
    quads = part // 4
    mirror = mirror_of(length)
    spans = [
        pl.ds(pl.multiple_of((place ^ index) * part, part), part) for index in indices
    ]

    def store(which, slot):
        return pltpu.make_async_copy(
            outs.at[which, slot], results[which].at[:, spans[slot], :], sems.at[which, slot]
        )

    def expand(slot):
        index, state_ref = indices[slot], states[slot]
        half = quads // 2
        lane = lane_iota((2 * rows, 8 * modes))
        for quad in range(half):
            state = state_ref[2 * rows * quad : 2 * rows * (quad + 1)]
            locals_ = [4 * (quad + half * (i // 4)) + i % 4 for i in range(8)]
            left = [
                jnp.where((lane >= modes * i) & (lane < modes * (i + 1)), state, 0.0)
                for i in range(8)
            ]
            right = [taps_ref[index, local] for local in locals_]
            every = dot(jnp.concatenate(left, axis=0), jnp.concatenate(right, axis=0), NN)
            every = every.reshape(8, 2 * rows, length)
            for i, local in enumerate(locals_):
                both = every[i] + near_ref[index, local]
                where = pl.ds(local % 8, rows, stride=8)
                cs[slot, local // 8, where, :] = both[:rows]
                gs[slot, local // 8, where, :] = both[rows:]

    def finish(slot):
        def natural(ref):
            pieces = [ref[slot, i].reshape(rows, 8, length) for i in range(part // 8)]
            return jnp.concatenate(pieces, axis=1).astype(BF16)

        own = spans[slot]
        ig = dot(natural(gs).reshape(rows * part, length), mirror, NN)
        outs[0, slot] = product(g_ref[:, own, :], natural(cs))
        store(0, slot).start()
        ig = ig.astype(BF16).reshape(rows, part, length)
        outs[1, slot] = product(ig, v_ref[:, own, :])
        store(1, slot).start()
        outs[2, slot] = product(ig, k_ref[:, own, :])
        store(2, slot).start()

    for slot in range(count + 1):
        if slot < count:
            expand(slot)
        if slot > 0:
            finish(slot - 1)
    for slot in range(count):
        for which in range(3):
            store(which, slot).wait()


def gradients(queries, keys_in, values_in, grad_out, residue, decay_rate):
    chans, length = queries.shape
    groups, modes = residue.shape
    count = lax.axis_size("ctx")
    tp = lax.axis_size("tp")
    depth = count // PLANE
    rows = chans // groups
    part = groups // PLANE
    quads = part // 4
    lanes = 8 * modes

    def cube(x):
        return x.reshape(rows, groups, length)

    query, key, value, grad = cube(queries), cube(keys_in), cube(values_in), cube(grad_out)
    decay, resid = decay_rate.T, residue.T
    vmem = pl.BlockSpec(memory_space=pltpu.VMEM)
    anywhere = pl.BlockSpec(memory_space=pltpu.HBM)

    def shaped(shape, dtype):
        return jax.ShapeDtypeStruct(shape, dtype)

    def call(kernel, in_specs, out_specs, out_shape, scratch, flops, size, aliases=None):
        return pl.pallas_call(
            kernel,
            in_specs=in_specs,
            out_specs=out_specs,
            out_shape=out_shape,
            scratch_shapes=scratch,
            cost_estimate=pl.CostEstimate(flops=flops, bytes_accessed=size, transcendentals=0),
            compiler_params=pltpu.CompilerParams(vmem_limit_bytes=16 * 2**20),
            input_output_aliases=aliases or {},
        )

    def in_hbm(*arrays):
        return [pltpu.with_memory_space_constraint(x, pltpu.HBM) for x in arrays]

    def reducer(slots):
        return [
            pltpu.VMEM((4, slots, rows, part, length), BF16),
            pltpu.SemaphoreType.DMA((4, slots)),
        ] + [pltpu.VMEM((slots, part // 8, rows * 8, length), F32)] * 2

    quarter = (part, 2 * rows, length)
    block = shaped((quads, 2 * rows, lanes), BF16)
    xc, weights, rates, *own = call(
        states_kernel,
        [anywhere] * 5,
        [vmem] * (2 + PLANE),
        [
            shaped((PLANE - 1,) + quarter, BF16),
            shaped((groups, 2, modes, length), BF16),
            shaped((groups // 4, lanes), F32),
        ]
        + [block] * (PLANE - 1),
        [pltpu.VMEM((modes, groups), F32), pltpu.SemaphoreType.DMA] + reducer(PLANE - 1),
        10**9,
        4 * 10**6,
    )(*in_hbm(decay, key, value, grad, query))

    def swap(x, bits):
        return lax.ppermute(x, "ctx", [(i, i ^ bits) for i in range(count)])

    near = []
    for i in range(1, PLANE):
        near.append(swap(own[i - 1], i))
    xo, mine, sums = call(
        sums_kernel,
        [anywhere] * 4 + [vmem] * 3,
        [vmem] * 3,
        [shaped(quarter, BF16), block, shaped((2 * modes, lanes), F32)],
        reducer(1)
        + [
            pltpu.VMEM((PLANE, part, length, length), BF16),
            pltpu.VMEM((PLANE, part, 2 * modes, length), BF16),
            pltpu.VMEM((PLANE, part, modes, length), F32),
        ],
        10**9,
        4 * 10**6,
    )(*in_hbm(key, value, grad, query), xc, weights, decay)
    near = [mine] + near
    flat = quads * 2 * rows
    plane = call(
        functools.partial(plane_kernel, length),
        [vmem] * (2 + PLANE),
        vmem,
        shaped((flat + 2 * modes, lanes), BF16),
        [pltpu.VMEM((2 * modes, lanes), F32)],
        10**7,
        10**6,
    )(rates, *near, sums)
    line = [plane] + [swap(plane, PLANE * i) for i in range(1, depth)]
    near_part, taps = call(
        local_kernel,
        [vmem] * 5,
        [vmem] * 2,
        [
            shaped((PLANE,) + quarter, F32),
            shaped((PLANE, part, modes, length), BF16),
        ],
        [
            pltpu.VMEM((PLANE, part, length, length), BF16),
            pltpu.VMEM((PLANE, part, length), F32),
            pltpu.VMEM((PLANE, part, 16, length), BF16),
        ],
        10**9,
        4 * 10**6,
    )(xo, xc, decay, resid, plane)
    sent = call(
        functools.partial(line_kernel, length),
        [vmem] * (2 + PLANE + depth),
        [vmem] * PLANE,
        [shaped((flat // 2 + 2 * modes, lanes), BF16)] * PLANE,
        [pltpu.VMEM((2 * modes, lanes), F32)],
        10**7,
        10**6,
    )(rates, taps, *near, *line)
    back = [sent[0]]
    for i in range(1, PLANE):
        back.append(swap(sent[i], i))

    total = sum(
        b[flat // 2 :, : lanes // 2].astype(F32) + b[flat // 2 :, lanes // 2 :].astype(F32)
        for b in back
    )
    bit = 1
    while bit < tp:
        total = total + lax.ppermute(total, "tp", [(i, i ^ bit) for i in range(tp)])
        bit *= 2

    outs = ()
    for indices in ((0,), (PLANE - 1,), tuple(range(1, PLANE - 1))):
        slots = len(indices)
        outs = call(
            functools.partial(outputs_kernel, indices),
            [vmem] * (5 + slots) + [anywhere] * len(outs),
            [anywhere] * 3,
            [shaped((rows, groups, length), BF16)] * 3,
            [
                pltpu.VMEM((3, slots, rows, part, length), BF16),
                pltpu.SemaphoreType.DMA((3, slots)),
                pltpu.VMEM((slots, part // 8, rows * 8, length), F32),
                pltpu.VMEM((slots, part // 8, rows * 8, length), F32),
            ],
            2 * 10**8 * slots,
            10**6 * slots,
            {5 + slots + i: i for i in range(len(outs))},
        )(key, value, grad, near_part, taps, *(back[i] for i in indices), *outs)
    tokens = count * length
    plain, moment = total[:modes, :groups], total[modes:, :groups]
    return (
        *(x.reshape(chans, length) for x in outs),
        (plain / tokens).T,
        (-(resid * decay) * moment / tokens).T,
    )


def solution(mesh):
    in_specs = (P("tp", "ctx"), P("tp", "ctx"), P("tp", "ctx"), P("tp", "ctx"), P(), P())
    out_specs = (P("tp", "ctx"), P("tp", "ctx"), P("tp", "ctx"), P(), P())
    return jax.shard_map(
        gradients, mesh=mesh, in_specs=in_specs, out_specs=out_specs, check_vma=False
    )
```

```python
import functools

import jax
import jax.numpy as jnp
from jax import lax
from jax.experimental import pallas as pl
from jax.experimental.pallas import tpu as pltpu
from jax.sharding import PartitionSpec as P

F32 = jnp.float32
BF16 = jnp.bfloat16
PLANE = 4
NT = (((1,), (1,)), ((), ()))
NN = (((1,), (0,)), ((), ()))
TN = (((0,), (0,)), ((), ()))


def dot(a, b, dims):
    return lax.dot_general(a, b, dims, preferred_element_type=F32)


def product(a, b):
    return a.astype(BF16) * b.astype(BF16)


def column(table, group):
    return jnp.sum(jnp.where(lane_iota(table.shape) == group, table, 0.0), axis=1, keepdims=True)


def mirror_of(length):
    total = lane_iota((length, length)) + lax.broadcasted_iota(jnp.int32, (length, length), 0)
    return jnp.where(total == length - 1, 1.0, 0.0).astype(BF16)


def places():
    me = lax.axis_index("ctx")
    return lax.rem(me, PLANE), lax.div(me, PLANE)


def lane_iota(shape):
    return lax.broadcasted_iota(jnp.int32, shape, len(shape) - 1)


class Reducer:
    def __init__(self, sources, bufs, sems, w_ref, gs, cs):
        self.sources, self.bufs, self.sems, self.w_ref, self.gs, self.cs = (
            sources, bufs, sems, w_ref, gs, cs
        )
        _, self.rows, self.part, self.length = bufs.shape[1:]
        self.mirror = mirror_of(self.length)

    def copies(self, slot, quarter):
        return [
            pltpu.make_async_copy(
                source.at[:, pl.ds(pl.multiple_of(quarter * self.part, self.part), self.part), :],
                self.bufs.at[which, slot],
                self.sems.at[which, slot],
            )
            for which, source in enumerate(self.sources)
        ]

    def load(self, slot, quarter):
        for copy in self.copies(slot, quarter):
            copy.wait()
        bufs, flat = self.bufs, self.rows * self.part
        x = product(bufs[0, slot], bufs[1, slot]).astype(F32)
        c = product(bufs[2, slot], bufs[3, slot]).reshape(flat, self.length)
        c = dot(c, self.mirror, NN).reshape(x.shape)
        for eight in range(self.part // 8):
            span = slice(8 * eight, 8 * eight + 8)
            self.gs[slot, eight] = x[:, span].reshape(8 * self.rows, self.length)
            self.cs[slot, eight] = c[:, span].reshape(8 * self.rows, self.length)

    def reduce(self, slot, quarter, xc_ref, out_ref):
        modes = self.w_ref.shape[2]
        lane = lane_iota((2 * self.rows, 8 * modes)) % (4 * modes)
        for quad in range(self.part // 4):
            left, right = [], [[], []]
            for side in range(4):
                local = 4 * quad + side
                group = quarter * self.part + local
                where = pl.ds(local % 8, self.rows, stride=8)
                both = jnp.concatenate(
                    [ref[slot, local // 8, where, :] for ref in (self.gs, self.cs)], axis=0
                ).astype(BF16)
                xc_ref[local] = both
                left.append(both)
                right[0].append(self.w_ref[group, 0])
                right[1].append(self.w_ref[group, 1])
            every = dot(
                jnp.concatenate(left, axis=0), jnp.concatenate(right[0] + right[1], axis=0), NT
            )
            every = every.reshape(4, 2 * self.rows, 8 * modes)
            found = every[0]
            for side in range(1, 4):
                found = jnp.where(lane >= side * modes, every[side], found)
            out_ref[quad] = found.astype(BF16)


def states_kernel(dec_hbm, k_hbm, v_hbm, g_hbm, q_hbm, xc_ref, w_ref, rate_ref, *rest):
    outs, rest = rest[: PLANE - 1], rest[PLANE - 1 :]
    dec_ref, dec_sem, bufs, sems, gs, cs = rest
    place, _ = places()
    modes, groups = dec_ref.shape
    work = Reducer((k_hbm, v_hbm, g_hbm, q_hbm), bufs, sems, w_ref, gs, cs)
    length = work.length
    rates_in = pltpu.make_async_copy(dec_hbm, dec_ref, dec_sem)
    rates_in.start()
    for slot in range(PLANE - 1):
        for copy in work.copies(slot, place ^ (slot + 1)):
            copy.start()
    rates_in.wait()
    dec = dec_ref[...]
    behind = float(length) - lane_iota((modes, length)).astype(F32)
    wide = (modes, 8 * modes)
    target = lane_iota(wide) % (4 * modes) - lax.broadcasted_iota(jnp.int32, wide, 0)

    def weights(index, _):
        rates = jnp.zeros(wide, F32)
        for side in range(4):
            group = 4 * index + side
            rate = column(dec, group)
            basis = jnp.exp(-rate * behind)
            w_ref[group, 0] = basis.astype(BF16)
            w_ref[group, 1] = (behind * basis).astype(BF16)
            rates = jnp.where(target == side * modes, rate, rates)
        rate_ref[pl.ds(index, 1), :] = jnp.sum(rates, axis=0, keepdims=True)
        return 0

    lax.fori_loop(0, groups // 4, weights, 0, unroll=4)
    for slot in range(PLANE):
        if slot < PLANE - 1:
            work.load(slot, place ^ (slot + 1))
        if slot > 0:
            work.reduce(slot - 1, place ^ slot, xc_ref.at[slot - 1], outs[slot - 1])


def sums_kernel(k_hbm, v_hbm, g_hbm, q_hbm, xc_ref, w_ref, dec_ref, own_ref, out_ref, sums_ref, *rest):
    bufs, sems, gs, cs, prods_ref, left_ref, basis_ref = rest
    place, _ = places()
    work = Reducer((k_hbm, v_hbm, g_hbm, q_hbm), bufs, sems, w_ref, gs, cs)
    for copy in work.copies(0, place):
        copy.start()
    _, part, rows, length = xc_ref.shape
    rows = rows // 2
    modes = dec_ref.shape[0]
    paired = (
        lane_iota((length, length)) + lax.broadcasted_iota(jnp.int32, (length, length), 0) < length
    )

    def multiply(index, ref):
        for local in range(part):
            prods = dot(ref[local, :rows], ref[local, rows:], TN)
            prods_ref[index, local] = jnp.where(paired, prods, 0.0).astype(BF16)

    multiply(1, xc_ref.at[0])
    work.load(0, place)
    multiply(2, xc_ref.at[1])
    work.reduce(0, place, own_ref, out_ref)
    multiply(3, xc_ref.at[2])
    multiply(0, own_ref)
    dec = dec_ref[...]
    middle = float(length // 2) - lane_iota((modes, length)).astype(F32)
    lane = lane_iota((modes, sums_ref.shape[1]))

    def tables(index, _):
        for local in range(part):
            rate = column(dec, (place ^ index) * part + local)
            basis = jnp.exp(-rate * middle)
            left_ref[index, local] = jnp.concatenate([basis, middle * basis], axis=0).astype(BF16)
            basis_ref[index, local] = basis * jnp.exp(rate)
        return 0

    lax.fori_loop(0, PLANE, tables, 0, unroll=2)

    def contract(index, carry):
        plain, moment = carry
        for local in range(part):
            group = (place ^ index) * part + local
            both = dot(left_ref[index, local], prods_ref[index, local], NN)
            basis = basis_ref[index, local]
            first = jnp.sum(basis * both[:modes], axis=1, keepdims=True)
            second = basis * ((middle - 1.0) * both[:modes] + both[modes:])
            plain = jnp.where(lane == group, first, plain)
            moment = jnp.where(lane == group, jnp.sum(second, axis=1, keepdims=True), moment)
        return plain, moment

    zero = jnp.zeros(lane.shape, F32)
    plain, moment = lax.fori_loop(0, PLANE, contract, (zero, zero), unroll=True)
    sums_ref[:modes] = plain
    sums_ref[modes:] = moment


def local_kernel(own_ref, xc_ref, dec_ref, res_ref, after_ref, out_ref, taps_ref, *scratch):
    toep_ref, rows_ref, bands_ref = scratch
    _, part, _, length = xc_ref.shape
    modes = dec_ref.shape[0]
    place, _ = places()
    dec, res = dec_ref[...], res_ref[...]
    ahead = lane_iota((modes, length)).astype(F32)
    step = 16
    lane = lane_iota((step, length))
    row = lax.broadcasted_iota(jnp.int32, (step, length), 0)

    def each(body):
        def run(index, _):
            body(index)
            return 0

        lax.fori_loop(0, PLANE, run, 0)

    @each
    def _(index):
        first_group = (place ^ index) * part
        for local in range(part):
            rate, weight = column(dec, first_group + local), column(res, first_group + local)
            taps = weight * jnp.exp(-rate * ahead)
            taps_ref[index, local] = taps.astype(BF16)
            rows_ref[index, local : local + 1] = jnp.sum(taps, axis=0, keepdims=True)

    @each
    def _(index):
        for local in range(part):
            taps = jnp.broadcast_to(rows_ref[index, local : local + 1], (step, length))
            bands_ref[index, local] = pltpu.roll(taps, 0, 1, stride=1, stride_axis=0).astype(BF16)

    @each
    def _(index):
        for local in range(part):
            band = bands_ref[index, local]
            for first in range(0, length, step):
                toep_ref[index, local, first : first + step] = jnp.where(
                    lane >= row + first, pltpu.roll(band, first, 1), 0.0
                )

    def convolve(index, ref):
        for local in range(part):
            out_ref[index, local] = dot(ref[local], toep_ref[index, local], NN)

    convolve(0, own_ref)

    def others(index, _):
        convolve(index, xc_ref.at[index - 1])
        return 0

    lax.fori_loop(1, PLANE, others, 0)


def split_pair(x, half):
    head = x.astype(BF16).astype(F32)
    tail = (x - head).astype(BF16).astype(F32)
    low = lane_iota(x.shape) < half
    return jnp.where(low, head, pltpu.roll(jnp.where(low, tail, 0.0), half, x.ndim - 1)).astype(BF16)


def join_pair(x, half):
    x = x.astype(F32)
    low = lane_iota(x.shape) < half
    return jnp.where(low, x + pltpu.roll(x, half, x.ndim - 1), 0.0)


def in_order(arrays, place):
    arrays, bit = list(arrays), 1
    while bit < len(arrays):
        swap = (place & bit) != 0
        new = list(arrays)
        for i in range(len(arrays)):
            new[i] = jnp.where(swap, arrays[i ^ bit], arrays[i])
        arrays, bit = new, 2 * bit
    return arrays


def scan_blocks(heads, tails, rate, gap):
    half = rate.shape[2] // 2
    decay = jnp.exp(-rate * gap)
    lift = jnp.where(lane_iota(rate.shape) >= half, gap * decay, 0.0)

    def run(blocks):
        state, reached = None, []
        for block in blocks:
            reached.append(state)
            if state is not None:
                block = decay * state + lift * pltpu.roll(state, half, 2) + block
            state = block
        return reached, state

    before, head = run(heads)
    after, tail = run(tails[::-1])
    return before, after[::-1], head, tail


def pair_sums(before, tails):
    half = tails[0].shape[2] // 2
    plain, moment = 0.0, 0.0
    for state, tail in zip(before[1:], tails[1:], strict=True):
        plain = plain + state * tail
        moment = moment + state * pltpu.roll(tail, half, 2)
    return jnp.sum(plain, axis=1), jnp.sum(moment, axis=1)


def pair_terms(sums, rate):
    half = rate.shape[1] // 2
    plain, moment = (jnp.concatenate(x, axis=0) for x in zip(*sums, strict=True))
    moment = moment + pltpu.roll(moment, half, 1) - pltpu.roll(plain, half, 1)
    return jnp.where(lane_iota(plain.shape) < half, plain, moment) * jnp.exp(rate)


def spread(terms, place, acc, modes):
    quads, lanes = terms.shape
    parts = []
    for _ in range(3):
        parts.append(terms.astype(BF16))
        terms = terms - parts[-1].astype(F32)
    parts = jnp.concatenate([x.astype(F32) for x in parts], axis=0)
    shape = (3 * quads, 4 * lanes)
    lane = lane_iota(shape)
    row = lax.broadcasted_iota(jnp.int32, shape, 0) % quads
    group = lane % lanes - 4 * quads * place
    chosen = jnp.where(group == 4 * row + lane // lanes, 1.0, 0.0)
    turned = dot(parts.astype(BF16), chosen.astype(BF16), TN)
    for side in range(4):
        span = slice(side * lanes, (side + 1) * lanes)
        acc[:modes] += turned[side * modes : (side + 1) * modes, span]
        acc[modes:] += turned[(4 + side) * modes : (5 + side) * modes, span]


def own_rates(rate_ref, place, quads):
    return rate_ref[pl.ds(place * quads, quads), :]


def halves(blocks, rows):
    blocks = [b.astype(F32) for b in blocks]
    return [b[:, :rows] for b in blocks], [b[:, rows:] for b in blocks]


def plane_kernel(length, rate_ref, *refs):
    *msgs, sums_ref, out_ref, acc = refs
    place, _ = places()
    quads, rows, lanes = msgs[0].shape
    flat = quads * rows
    modes = lanes // 8
    rate = own_rates(rate_ref, place, quads)
    sums = []
    for quad in range(quads):
        one = slice(quad, quad + 1)
        heads, tails = halves(in_order([m[one] for m in msgs], place), rows // 2)
        before, _, head, tail = scan_blocks(heads, tails, rate[one, None], float(length))
        both = jnp.concatenate([head, tail], axis=1).astype(BF16)
        out_ref[quad * rows : (quad + 1) * rows] = both[0]
        sums.append(pair_sums(before, tails))
    acc[...] = sums_ref[...]
    spread(pair_terms(sums, rate), place, acc, modes)
    out_ref[flat:] = split_pair(acc[...], lanes // 2)


def line_kernel(length, rate_ref, after_ref, *refs):
    count = len(refs) - 2 * PLANE - 1
    msgs, lines = refs[:PLANE], refs[PLANE : PLANE + count]
    outs, acc = refs[PLANE + count : -1], refs[-1]
    place, level = places()
    quads, rows, lanes = msgs[0].shape
    flat = quads * rows
    modes = lanes // 8
    rate = own_rates(rate_ref, place, quads)
    sums, found = [], []
    for quad in range(quads):
        one = slice(quad, quad + 1)
        part = slice(quad * rows, (quad + 1) * rows)
        heads, tails = halves(in_order([r[part][None] for r in lines], level), rows // 2)
        before, after, _, _ = scan_blocks(heads, tails, rate[one, None], float(PLANE * length))
        sums.append(pair_sums(before, tails))
        start = [jnp.zeros_like(heads[0]), jnp.zeros_like(heads[0])]
        for i in range(1, count):
            start[0] = jnp.where(level == i, before[i], start[0])
            start[1] = jnp.where(level == i - 1, after[i - 1], start[1])
        heads, tails = halves(in_order([m[one] for m in msgs], place), rows // 2)
        decay = jnp.exp(-rate[one, None] * float(length))
        before, after = [start[0]], [start[1]]
        for i in range(PLANE - 1):
            before.append(decay * before[-1] + heads[i])
            after.insert(0, decay * after[0] + tails[PLANE - 1 - i])
        found.append(
            [jnp.concatenate(pair, axis=1)[0] for pair in zip(before, after, strict=True)]
        )
    low = lane_iota((rows, lanes)) < lanes // 2
    for quad in range(quads // 2):
        packed = [
            jnp.where(low, x, pltpu.roll(y, lanes // 2, 1)).astype(BF16)
            for x, y in zip(found[quad], found[quad + quads // 2], strict=True)
        ]
        for i, x in enumerate(in_order(packed, place)):
            outs[i][quad * rows : (quad + 1) * rows] = x
    total = join_pair(lines[0][flat:], lanes // 2)
    for r in lines[1:]:
        total = total + join_pair(r[flat:], lanes // 2)
    acc[...] = total
    spread(pair_terms(sums, rate), place, acc, modes)
    total = split_pair(acc[...], lanes // 2)
    for i in range(PLANE):
        outs[i][flat // 2 :] = total


def outputs_kernel(indices, k_ref, v_ref, g_ref, near_ref, taps_ref, *refs):
    count = len(indices)
    states, refs = refs[:count], refs[count:]
    results, (outs, sems, cs, gs) = refs[-7:-4], refs[-4:]
    place, _ = places()
    _, _, rows, part, length = outs.shape
    modes = taps_ref.shape[2]
    quads = part // 4
    mirror = mirror_of(length)
    spans = [
        pl.ds(pl.multiple_of((place ^ index) * part, part), part) for index in indices
    ]

    def store(which, slot):
        return pltpu.make_async_copy(
            outs.at[which, slot], results[which].at[:, spans[slot], :], sems.at[which, slot]
        )

    def expand(slot):
        index, state_ref = indices[slot], states[slot]
        half = quads // 2
        lane = lane_iota((2 * rows, 8 * modes))
        for quad in range(half):
            state = state_ref[2 * rows * quad : 2 * rows * (quad + 1)]
            locals_ = [4 * (quad + half * (i // 4)) + i % 4 for i in range(8)]
            left = [
                jnp.where((lane >= modes * i) & (lane < modes * (i + 1)), state, 0.0)
                for i in range(8)
            ]
            right = [taps_ref[index, local] for local in locals_]
            every = dot(jnp.concatenate(left, axis=0), jnp.concatenate(right, axis=0), NN)
            every = every.reshape(8, 2 * rows, length)
            for i, local in enumerate(locals_):
                both = every[i] + near_ref[index, local]
                where = pl.ds(local % 8, rows, stride=8)
                cs[slot, local // 8, where, :] = both[:rows]
                gs[slot, local // 8, where, :] = both[rows:]

    def finish(slot):
        def natural(ref):
            pieces = [ref[slot, i].reshape(rows, 8, length) for i in range(part // 8)]
            return jnp.concatenate(pieces, axis=1).astype(BF16)

        own = spans[slot]
        ig = dot(natural(gs).reshape(rows * part, length), mirror, NN)
        outs[0, slot] = product(g_ref[:, own, :], natural(cs))
        store(0, slot).start()
        ig = ig.astype(BF16).reshape(rows, part, length)
        outs[1, slot] = product(ig, v_ref[:, own, :])
        store(1, slot).start()
        outs[2, slot] = product(ig, k_ref[:, own, :])
        store(2, slot).start()

    for slot in range(count + 1):
        if slot < count:
            expand(slot)
        if slot > 0:
            finish(slot - 1)
    for slot in range(count):
        for which in range(3):
            store(which, slot).wait()


def gradients(queries, keys_in, values_in, grad_out, residue, decay_rate):
    chans, length = queries.shape
    groups, modes = residue.shape
    count = lax.axis_size("ctx")
    tp = lax.axis_size("tp")
    depth = count // PLANE
    rows = chans // groups
    part = groups // PLANE
    quads = part // 4
    lanes = 8 * modes

    def cube(x):
        return x.reshape(rows, groups, length)

    query, key, value, grad = cube(queries), cube(keys_in), cube(values_in), cube(grad_out)
    decay, resid = decay_rate.T, residue.T
    vmem = pl.BlockSpec(memory_space=pltpu.VMEM)
    anywhere = pl.BlockSpec(memory_space=pltpu.HBM)

    def shaped(shape, dtype):
        return jax.ShapeDtypeStruct(shape, dtype)

    def call(kernel, in_specs, out_specs, out_shape, scratch, flops, size, aliases=None):
        return pl.pallas_call(
            kernel,
            in_specs=in_specs,
            out_specs=out_specs,
            out_shape=out_shape,
            scratch_shapes=scratch,
            cost_estimate=pl.CostEstimate(flops=flops, bytes_accessed=size, transcendentals=0),
            compiler_params=pltpu.CompilerParams(vmem_limit_bytes=16 * 2**20),
            input_output_aliases=aliases or {},
        )

    def in_hbm(*arrays):
        return [pltpu.with_memory_space_constraint(x, pltpu.HBM) for x in arrays]

    def reducer(slots):
        return [
            pltpu.VMEM((4, slots, rows, part, length), BF16),
            pltpu.SemaphoreType.DMA((4, slots)),
        ] + [pltpu.VMEM((slots, part // 8, rows * 8, length), F32)] * 2

    quarter = (part, 2 * rows, length)
    block = shaped((quads, 2 * rows, lanes), BF16)
    xc, weights, rates, *own = call(
        states_kernel,
        [anywhere] * 5,
        [vmem] * (2 + PLANE),
        [
            shaped((PLANE - 1,) + quarter, BF16),
            shaped((groups, 2, modes, length), BF16),
            shaped((groups // 4, lanes), F32),
        ]
        + [block] * (PLANE - 1),
        [pltpu.VMEM((modes, groups), F32), pltpu.SemaphoreType.DMA] + reducer(PLANE - 1),
        10**9,
        4 * 10**6,
    )(*in_hbm(decay, key, value, grad, query))

    def swap(x, bits):
        return lax.ppermute(x, "ctx", [(i, i ^ bits) for i in range(count)])

    near = []
    for i in range(1, PLANE):
        near.append(swap(own[i - 1], i))
    xo, mine, sums = call(
        sums_kernel,
        [anywhere] * 4 + [vmem] * 3,
        [vmem] * 3,
        [shaped(quarter, BF16), block, shaped((2 * modes, lanes), F32)],
        reducer(1)
        + [
            pltpu.VMEM((PLANE, part, length, length), BF16),
            pltpu.VMEM((PLANE, part, 2 * modes, length), BF16),
            pltpu.VMEM((PLANE, part, modes, length), F32),
        ],
        10**9,
        4 * 10**6,
    )(*in_hbm(key, value, grad, query), xc, weights, decay)
    near = [mine] + near
    flat = quads * 2 * rows
    plane = call(
        functools.partial(plane_kernel, length),
        [vmem] * (2 + PLANE),
        vmem,
        shaped((flat + 2 * modes, lanes), BF16),
        [pltpu.VMEM((2 * modes, lanes), F32)],
        10**7,
        10**6,
    )(rates, *near, sums)
    line = [plane] + [swap(plane, PLANE * i) for i in range(1, depth)]
    near_part, taps = call(
        local_kernel,
        [vmem] * 5,
        [vmem] * 2,
        [
            shaped((PLANE,) + quarter, F32),
            shaped((PLANE, part, modes, length), BF16),
        ],
        [
            pltpu.VMEM((PLANE, part, length, length), BF16),
            pltpu.VMEM((PLANE, part, length), F32),
            pltpu.VMEM((PLANE, part, 16, length), BF16),
        ],
        10**9,
        4 * 10**6,
    )(xo, xc, decay, resid, plane)
    sent = call(
        functools.partial(line_kernel, length),
        [vmem] * (2 + PLANE + depth),
        [vmem] * PLANE,
        [shaped((flat // 2 + 2 * modes, lanes), BF16)] * PLANE,
        [pltpu.VMEM((2 * modes, lanes), F32)],
        10**7,
        10**6,
    )(rates, taps, *near, *line)
    back = [sent[0]]
    for i in range(1, PLANE):
        back.append(swap(sent[i], i))

    total = sum(
        b[flat // 2 :, : lanes // 2].astype(F32) + b[flat // 2 :, lanes // 2 :].astype(F32)
        for b in back
    )
    bit = 1
    while bit < tp:
        total = total + lax.ppermute(total, "tp", [(i, i ^ bit) for i in range(tp)])
        bit *= 2

    outs = ()
    for indices in ((0,), (PLANE - 1,), tuple(range(1, PLANE - 1))):
        slots = len(indices)
        outs = call(
            functools.partial(outputs_kernel, indices),
            [vmem] * (5 + slots) + [anywhere] * len(outs),
            [anywhere] * 3,
            [shaped((rows, groups, length), BF16)] * 3,
            [
                pltpu.VMEM((3, slots, rows, part, length), BF16),
                pltpu.SemaphoreType.DMA((3, slots)),
                pltpu.VMEM((slots, part // 8, rows * 8, length), F32),
                pltpu.VMEM((slots, part // 8, rows * 8, length), F32),
            ],
            2 * 10**8 * slots,
            10**6 * slots,
            {5 + slots + i: i for i in range(len(outs))},
        )(key, value, grad, near_part, taps, *(back[i] for i in indices), *outs)
    tokens = count * length
    plain, moment = total[:modes, :groups], total[modes:, :groups]
    return (
        *(x.reshape(chans, length) for x in outs),
        (plain / tokens).T,
        (-(resid * decay) * moment / tokens).T,
    )


def solution(mesh):
    in_specs = (P("tp", "ctx"), P("tp", "ctx"), P("tp", "ctx"), P("tp", "ctx"), P(), P())
    out_specs = (P("tp", "ctx"), P("tp", "ctx"), P("tp", "ctx"), P(), P())
    return jax.shard_map(
        gradients, mesh=mesh, in_specs=in_specs, out_specs=out_specs, check_vma=False
    )
```

```python
import functools

import jax
import jax.numpy as jnp
from jax import lax
from jax.experimental import pallas as pl
from jax.experimental.pallas import tpu as pltpu
from jax.sharding import PartitionSpec as P

F32 = jnp.float32
BF16 = jnp.bfloat16
PLANE = 4
NT = (((1,), (1,)), ((), ()))
NN = (((1,), (0,)), ((), ()))
TN = (((0,), (0,)), ((), ()))


def dot(a, b, dims):
    return lax.dot_general(a, b, dims, preferred_element_type=F32)


def product(a, b):
    return a.astype(BF16) * b.astype(BF16)


def column(table, group):
    return jnp.sum(jnp.where(lane_iota(table.shape) == group, table, 0.0), axis=1, keepdims=True)


def mirror_of(length):
    total = lane_iota((length, length)) + lax.broadcasted_iota(jnp.int32, (length, length), 0)
    return jnp.where(total == length - 1, 1.0, 0.0).astype(BF16)


def places():
    me = lax.axis_index("ctx")
    return lax.rem(me, PLANE), lax.div(me, PLANE)


def lane_iota(shape):
    return lax.broadcasted_iota(jnp.int32, shape, len(shape) - 1)


class Reducer:
    def __init__(self, sources, bufs, sems, w_ref, gs, cs):
        self.sources, self.bufs, self.sems, self.w_ref, self.gs, self.cs = (
            sources, bufs, sems, w_ref, gs, cs
        )
        _, self.rows, self.part, self.length = bufs.shape[1:]
        self.mirror = mirror_of(self.length)

    def copies(self, slot, quarter):
        return [
            pltpu.make_async_copy(
                source.at[:, pl.ds(pl.multiple_of(quarter * self.part, self.part), self.part), :],
                self.bufs.at[which, slot],
                self.sems.at[which, slot],
            )
            for which, source in enumerate(self.sources)
        ]

    def load(self, slot, quarter):
        for copy in self.copies(slot, quarter):
            copy.wait()
        bufs, flat = self.bufs, self.rows * self.part
        x = product(bufs[0, slot], bufs[1, slot]).astype(F32)
        c = product(bufs[2, slot], bufs[3, slot]).reshape(flat, self.length)
        c = dot(c, self.mirror, NN).reshape(x.shape)
        for eight in range(self.part // 8):
            span = slice(8 * eight, 8 * eight + 8)
            self.gs[slot, eight] = x[:, span].reshape(8 * self.rows, self.length)
            self.cs[slot, eight] = c[:, span].reshape(8 * self.rows, self.length)

    def reduce(self, slot, quarter, xc_ref, out_ref):
        modes = self.w_ref.shape[2]
        lane = lane_iota((2 * self.rows, 8 * modes)) % (4 * modes)
        for quad in range(self.part // 4):
            left, right = [], [[], []]
            for side in range(4):
                local = 4 * quad + side
                group = quarter * self.part + local
                where = pl.ds(local % 8, self.rows, stride=8)
                both = jnp.concatenate(
                    [ref[slot, local // 8, where, :] for ref in (self.gs, self.cs)], axis=0
                ).astype(BF16)
                xc_ref[local] = both
                left.append(both)
                right[0].append(self.w_ref[group, 0])
                right[1].append(self.w_ref[group, 1])
            every = dot(
                jnp.concatenate(left, axis=0), jnp.concatenate(right[0] + right[1], axis=0), NT
            )
            every = every.reshape(4, 2 * self.rows, 8 * modes)
            found = every[0]
            for side in range(1, 4):
                found = jnp.where(lane >= side * modes, every[side], found)
            out_ref[quad] = found.astype(BF16)


def states_kernel(dec_hbm, k_hbm, v_hbm, g_hbm, q_hbm, xc_ref, w_ref, rate_ref, *rest):
    outs, rest = rest[: PLANE - 1], rest[PLANE - 1 :]
    dec_ref, dec_sem, bufs, sems, gs, cs = rest
    place, _ = places()
    modes, groups = dec_ref.shape
    work = Reducer((k_hbm, v_hbm, g_hbm, q_hbm), bufs, sems, w_ref, gs, cs)
    length = work.length
    rates_in = pltpu.make_async_copy(dec_hbm, dec_ref, dec_sem)
    rates_in.start()
    for slot in range(PLANE - 1):
        for copy in work.copies(slot, place ^ (slot + 1)):
            copy.start()
    rates_in.wait()
    dec = dec_ref[...]
    behind = float(length) - lane_iota((modes, length)).astype(F32)
    wide = (modes, 8 * modes)
    target = lane_iota(wide) % (4 * modes) - lax.broadcasted_iota(jnp.int32, wide, 0)

    def weights(index, _):
        rates = jnp.zeros(wide, F32)
        for side in range(4):
            group = 4 * index + side
            rate = column(dec, group)
            basis = jnp.exp(-rate * behind)
            w_ref[group, 0] = basis.astype(BF16)
            w_ref[group, 1] = (behind * basis).astype(BF16)
            rates = jnp.where(target == side * modes, rate, rates)
        rate_ref[pl.ds(index, 1), :] = jnp.sum(rates, axis=0, keepdims=True)
        return 0

    lax.fori_loop(0, groups // 4, weights, 0, unroll=4)
    for slot in range(PLANE):
        if slot < PLANE - 1:
            work.load(slot, place ^ (slot + 1))
        if slot > 0:
            work.reduce(slot - 1, place ^ slot, xc_ref.at[slot - 1], outs[slot - 1])


def sums_kernel(k_hbm, v_hbm, g_hbm, q_hbm, xc_ref, w_ref, dec_ref, own_ref, out_ref, sums_ref, *rest):
    bufs, sems, gs, cs, prods_ref, left_ref, basis_ref = rest
    place, _ = places()
    work = Reducer((k_hbm, v_hbm, g_hbm, q_hbm), bufs, sems, w_ref, gs, cs)
    for copy in work.copies(0, place):
        copy.start()
    _, part, rows, length = xc_ref.shape
    rows = rows // 2
    modes = dec_ref.shape[0]
    paired = (
        lane_iota((length, length)) + lax.broadcasted_iota(jnp.int32, (length, length), 0) < length
    )

    def multiply(index, ref):
        for local in range(part):
            prods = dot(ref[local, :rows], ref[local, rows:], TN)
            prods_ref[index, local] = jnp.where(paired, prods, 0.0).astype(BF16)

    multiply(1, xc_ref.at[0])
    work.load(0, place)
    multiply(2, xc_ref.at[1])
    work.reduce(0, place, own_ref, out_ref)
    multiply(3, xc_ref.at[2])
    multiply(0, own_ref)
    dec = dec_ref[...]
    middle = float(length // 2) - lane_iota((modes, length)).astype(F32)
    lane = lane_iota((modes, sums_ref.shape[1]))

    def tables(index, _):
        for local in range(part):
            rate = column(dec, (place ^ index) * part + local)
            basis = jnp.exp(-rate * middle)
            left_ref[index, local] = jnp.concatenate([basis, middle * basis], axis=0).astype(BF16)
            basis_ref[index, local] = basis * jnp.exp(rate)
        return 0

    lax.fori_loop(0, PLANE, tables, 0, unroll=2)

    def contract(index, carry):
        plain, moment = carry
        for local in range(part):
            group = (place ^ index) * part + local
            both = dot(left_ref[index, local], prods_ref[index, local], NN)
            basis = basis_ref[index, local]
            first = jnp.sum(basis * both[:modes], axis=1, keepdims=True)
            second = basis * ((middle - 1.0) * both[:modes] + both[modes:])
            plain = jnp.where(lane == group, first, plain)
            moment = jnp.where(lane == group, jnp.sum(second, axis=1, keepdims=True), moment)
        return plain, moment

    zero = jnp.zeros(lane.shape, F32)
    plain, moment = lax.fori_loop(0, PLANE, contract, (zero, zero), unroll=True)
    sums_ref[:modes] = plain
    sums_ref[modes:] = moment


def local_kernel(own_ref, xc_ref, dec_ref, res_ref, after_ref, out_ref, taps_ref, *scratch):
    toep_ref, rows_ref, bands_ref = scratch
    _, part, _, length = xc_ref.shape
    modes = dec_ref.shape[0]
    place, _ = places()
    dec, res = dec_ref[...], res_ref[...]
    ahead = lane_iota((modes, length)).astype(F32)
    step = 16
    lane = lane_iota((step, length))
    row = lax.broadcasted_iota(jnp.int32, (step, length), 0)

    def each(body):
        def run(index, _):
            body(index)
            return 0

        lax.fori_loop(0, PLANE, run, 0)

    @each
    def _(index):
        first_group = (place ^ index) * part
        for local in range(part):
            rate, weight = column(dec, first_group + local), column(res, first_group + local)
            taps = weight * jnp.exp(-rate * ahead)
            taps_ref[index, local] = taps.astype(BF16)
            rows_ref[index, local : local + 1] = jnp.sum(taps, axis=0, keepdims=True)

    @each
    def _(index):
        for local in range(part):
            taps = jnp.broadcast_to(rows_ref[index, local : local + 1], (step, length))
            bands_ref[index, local] = pltpu.roll(taps, 0, 1, stride=1, stride_axis=0).astype(BF16)

    @each
    def _(index):
        for local in range(part):
            band = bands_ref[index, local]
            for first in range(0, length, step):
                toep_ref[index, local, first : first + step] = jnp.where(
                    lane >= row + first, pltpu.roll(band, first, 1), 0.0
                )

    def convolve(index, ref):
        for local in range(part):
            out_ref[index, local] = dot(ref[local], toep_ref[index, local], NN)

    convolve(0, own_ref)

    def others(index, _):
        convolve(index, xc_ref.at[index - 1])
        return 0

    lax.fori_loop(1, PLANE, others, 0)


def pack_sums(x, half):
    rows = x.shape[0] // 2
    low = lane_iota((rows, x.shape[1])) < half
    return jnp.where(low, x[:rows], pltpu.roll(x[rows:], half, 1)).astype(BF16)


def unpack_sums(x, half):
    x = x.astype(F32)
    low = lane_iota(x.shape) < half
    both = jnp.concatenate([x, pltpu.roll(x, half, 1)], axis=0)
    return jnp.where(jnp.concatenate([low, low], axis=0), both, 0.0)


def in_order(arrays, place):
    arrays, bit = list(arrays), 1
    while bit < len(arrays):
        swap = (place & bit) != 0
        new = list(arrays)
        for i in range(len(arrays)):
            new[i] = jnp.where(swap, arrays[i ^ bit], arrays[i])
        arrays, bit = new, 2 * bit
    return arrays


def scan_blocks(heads, tails, rate, gap):
    half = rate.shape[2] // 2
    decay = jnp.exp(-rate * gap)
    lift = jnp.where(lane_iota(rate.shape) >= half, gap * decay, 0.0)

    def run(blocks):
        state, reached = None, []
        for block in blocks:
            reached.append(state)
            if state is not None:
                block = decay * state + lift * pltpu.roll(state, half, 2) + block
            state = block
        return reached, state

    before, head = run(heads)
    after, tail = run(tails[::-1])
    return before, after[::-1], head, tail


def pair_sums(before, tails):
    half = tails[0].shape[2] // 2
    plain, moment = 0.0, 0.0
    for state, tail in zip(before[1:], tails[1:], strict=True):
        plain = plain + state * tail
        moment = moment + state * pltpu.roll(tail, half, 2)
    return jnp.sum(plain, axis=1), jnp.sum(moment, axis=1)


def pair_terms(sums, rate):
    half = rate.shape[1] // 2
    plain, moment = (jnp.concatenate(x, axis=0) for x in zip(*sums, strict=True))
    moment = moment + pltpu.roll(moment, half, 1) - pltpu.roll(plain, half, 1)
    return jnp.where(lane_iota(plain.shape) < half, plain, moment) * jnp.exp(rate)


def spread(terms, place, acc, modes):
    quads, lanes = terms.shape
    parts = []
    for _ in range(3):
        parts.append(terms.astype(BF16))
        terms = terms - parts[-1].astype(F32)
    parts = jnp.concatenate([x.astype(F32) for x in parts], axis=0)
    shape = (3 * quads, 4 * lanes)
    lane = lane_iota(shape)
    row = lax.broadcasted_iota(jnp.int32, shape, 0) % quads
    group = lane % lanes - 4 * quads * place
    chosen = jnp.where(group == 4 * row + lane // lanes, 1.0, 0.0)
    turned = dot(parts.astype(BF16), chosen.astype(BF16), TN)
    for side in range(4):
        span = slice(side * lanes, (side + 1) * lanes)
        acc[:modes] += turned[side * modes : (side + 1) * modes, span]
        acc[modes:] += turned[(4 + side) * modes : (5 + side) * modes, span]


def own_rates(rate_ref, place, quads):
    return rate_ref[pl.ds(place * quads, quads), :]


def halves(blocks, rows):
    blocks = [b.astype(F32) for b in blocks]
    return [b[:, :rows] for b in blocks], [b[:, rows:] for b in blocks]


def plane_kernel(length, rate_ref, *refs):
    *msgs, sums_ref, out_ref, acc = refs
    place, _ = places()
    quads, rows, lanes = msgs[0].shape
    flat = quads * rows
    modes = lanes // 8
    rate = own_rates(rate_ref, place, quads)
    sums = []
    for quad in range(quads):
        one = slice(quad, quad + 1)
        heads, tails = halves(in_order([m[one] for m in msgs], place), rows // 2)
        before, _, head, tail = scan_blocks(heads, tails, rate[one, None], float(length))
        both = jnp.concatenate([head, tail], axis=1).astype(BF16)
        out_ref[quad * rows : (quad + 1) * rows] = both[0]
        sums.append(pair_sums(before, tails))
    acc[...] = sums_ref[...]
    spread(pair_terms(sums, rate), place, acc, modes)
    out_ref[flat:] = pack_sums(acc[...], lanes // 2)


def line_kernel(length, rate_ref, after_ref, *refs):
    count = len(refs) - 2 * PLANE - 1
    msgs, lines = refs[:PLANE], refs[PLANE : PLANE + count]
    outs, acc = refs[PLANE + count : -1], refs[-1]
    place, level = places()
    quads, rows, lanes = msgs[0].shape
    flat = quads * rows
    modes = lanes // 8
    rate = own_rates(rate_ref, place, quads)
    sums, found = [], []
    for quad in range(quads):
        one = slice(quad, quad + 1)
        part = slice(quad * rows, (quad + 1) * rows)
        heads, tails = halves(in_order([r[part][None] for r in lines], level), rows // 2)
        before, after, _, _ = scan_blocks(heads, tails, rate[one, None], float(PLANE * length))
        sums.append(pair_sums(before, tails))
        start = [jnp.zeros_like(heads[0]), jnp.zeros_like(heads[0])]
        for i in range(1, count):
            start[0] = jnp.where(level == i, before[i], start[0])
            start[1] = jnp.where(level == i - 1, after[i - 1], start[1])
        heads, tails = halves(in_order([m[one] for m in msgs], place), rows // 2)
        decay = jnp.exp(-rate[one, None] * float(length))
        before, after = [start[0]], [start[1]]
        for i in range(PLANE - 1):
            before.append(decay * before[-1] + heads[i])
            after.insert(0, decay * after[0] + tails[PLANE - 1 - i])
        found.append(
            [jnp.concatenate(pair, axis=1)[0] for pair in zip(before, after, strict=True)]
        )
    low = lane_iota((rows, lanes)) < lanes // 2
    for quad in range(quads // 2):
        packed = [
            jnp.where(low, x, pltpu.roll(y, lanes // 2, 1)).astype(BF16)
            for x, y in zip(found[quad], found[quad + quads // 2], strict=True)
        ]
        for i, x in enumerate(in_order(packed, place)):
            outs[i][quad * rows : (quad + 1) * rows] = x
    total = unpack_sums(lines[0][flat:], lanes // 2)
    for r in lines[1:]:
        total = total + unpack_sums(r[flat:], lanes // 2)
    acc[...] = total
    spread(pair_terms(sums, rate), place, acc, modes)
    total = pack_sums(acc[...], lanes // 2)
    for i in range(PLANE):
        outs[i][flat // 2 :] = total


def outputs_kernel(indices, k_ref, v_ref, g_ref, near_ref, taps_ref, *refs):
    count = len(indices)
    states, refs = refs[:count], refs[count:]
    results, (outs, sems, cs, gs) = refs[-7:-4], refs[-4:]
    place, _ = places()
    _, _, rows, part, length = outs.shape
    modes = taps_ref.shape[2]
    quads = part // 4
    mirror = mirror_of(length)
    spans = [
        pl.ds(pl.multiple_of((place ^ index) * part, part), part) for index in indices
    ]

    def store(which, slot):
        return pltpu.make_async_copy(
            outs.at[which, slot], results[which].at[:, spans[slot], :], sems.at[which, slot]
        )

    def expand(slot):
        index, state_ref = indices[slot], states[slot]
        half = quads // 2
        lane = lane_iota((2 * rows, 8 * modes))
        for quad in range(half):
            state = state_ref[2 * rows * quad : 2 * rows * (quad + 1)]
            locals_ = [4 * (quad + half * (i // 4)) + i % 4 for i in range(8)]
            left = [
                jnp.where((lane >= modes * i) & (lane < modes * (i + 1)), state, 0.0)
                for i in range(8)
            ]
            right = [taps_ref[index, local] for local in locals_]
            every = dot(jnp.concatenate(left, axis=0), jnp.concatenate(right, axis=0), NN)
            every = every.reshape(8, 2 * rows, length)
            for i, local in enumerate(locals_):
                both = every[i] + near_ref[index, local]
                where = pl.ds(local % 8, rows, stride=8)
                cs[slot, local // 8, where, :] = both[:rows]
                gs[slot, local // 8, where, :] = both[rows:]

    def finish(slot):
        def natural(ref):
            pieces = [ref[slot, i].reshape(rows, 8, length) for i in range(part // 8)]
            return jnp.concatenate(pieces, axis=1).astype(BF16)

        own = spans[slot]
        ig = dot(natural(gs).reshape(rows * part, length), mirror, NN)
        outs[0, slot] = product(g_ref[:, own, :], natural(cs))
        store(0, slot).start()
        ig = ig.astype(BF16).reshape(rows, part, length)
        outs[1, slot] = product(ig, v_ref[:, own, :])
        store(1, slot).start()
        outs[2, slot] = product(ig, k_ref[:, own, :])
        store(2, slot).start()

    for slot in range(count + 1):
        if slot < count:
            expand(slot)
        if slot > 0:
            finish(slot - 1)
    for slot in range(count):
        for which in range(3):
            store(which, slot).wait()


def gradients(queries, keys_in, values_in, grad_out, residue, decay_rate):
    chans, length = queries.shape
    groups, modes = residue.shape
    count = lax.axis_size("ctx")
    tp = lax.axis_size("tp")
    depth = count // PLANE
    rows = chans // groups
    part = groups // PLANE
    quads = part // 4
    lanes = 8 * modes

    def cube(x):
        return x.reshape(rows, groups, length)

    query, key, value, grad = cube(queries), cube(keys_in), cube(values_in), cube(grad_out)
    decay, resid = decay_rate.T, residue.T
    vmem = pl.BlockSpec(memory_space=pltpu.VMEM)
    anywhere = pl.BlockSpec(memory_space=pltpu.HBM)

    def shaped(shape, dtype):
        return jax.ShapeDtypeStruct(shape, dtype)

    def call(kernel, in_specs, out_specs, out_shape, scratch, flops, size, aliases=None):
        return pl.pallas_call(
            kernel,
            in_specs=in_specs,
            out_specs=out_specs,
            out_shape=out_shape,
            scratch_shapes=scratch,
            cost_estimate=pl.CostEstimate(flops=flops, bytes_accessed=size, transcendentals=0),
            compiler_params=pltpu.CompilerParams(vmem_limit_bytes=16 * 2**20),
            input_output_aliases=aliases or {},
        )

    def in_hbm(*arrays):
        return [pltpu.with_memory_space_constraint(x, pltpu.HBM) for x in arrays]

    def reducer(slots):
        return [
            pltpu.VMEM((4, slots, rows, part, length), BF16),
            pltpu.SemaphoreType.DMA((4, slots)),
        ] + [pltpu.VMEM((slots, part // 8, rows * 8, length), F32)] * 2

    quarter = (part, 2 * rows, length)
    block = shaped((quads, 2 * rows, lanes), BF16)
    xc, weights, rates, *own = call(
        states_kernel,
        [anywhere] * 5,
        [vmem] * (2 + PLANE),
        [
            shaped((PLANE - 1,) + quarter, BF16),
            shaped((groups, 2, modes, length), BF16),
            shaped((groups // 4, lanes), F32),
        ]
        + [block] * (PLANE - 1),
        [pltpu.VMEM((modes, groups), F32), pltpu.SemaphoreType.DMA] + reducer(PLANE - 1),
        10**9,
        4 * 10**6,
    )(*in_hbm(decay, key, value, grad, query))

    def swap(x, bits):
        return lax.ppermute(x, "ctx", [(i, i ^ bits) for i in range(count)])

    near = []
    for i in range(1, PLANE):
        near.append(swap(own[i - 1], i))
    xo, mine, sums = call(
        sums_kernel,
        [anywhere] * 4 + [vmem] * 3,
        [vmem] * 3,
        [shaped(quarter, BF16), block, shaped((2 * modes, lanes), F32)],
        reducer(1)
        + [
            pltpu.VMEM((PLANE, part, length, length), BF16),
            pltpu.VMEM((PLANE, part, 2 * modes, length), BF16),
            pltpu.VMEM((PLANE, part, modes, length), F32),
        ],
        10**9,
        4 * 10**6,
    )(*in_hbm(key, value, grad, query), xc, weights, decay)
    near = [mine] + near
    flat = quads * 2 * rows
    plane = call(
        functools.partial(plane_kernel, length),
        [vmem] * (2 + PLANE),
        vmem,
        shaped((flat + modes, lanes), BF16),
        [pltpu.VMEM((2 * modes, lanes), F32)],
        10**7,
        10**6,
    )(rates, *near, sums)
    line = [plane]
    for i in range(1, depth):
        line.append(swap(plane, PLANE * i))
    near_part, taps = call(
        local_kernel,
        [vmem] * 5,
        [vmem] * 2,
        [
            shaped((PLANE,) + quarter, F32),
            shaped((PLANE, part, modes, length), BF16),
        ],
        [
            pltpu.VMEM((PLANE, part, length, length), BF16),
            pltpu.VMEM((PLANE, part, length), F32),
            pltpu.VMEM((PLANE, part, 16, length), BF16),
        ],
        10**9,
        4 * 10**6,
    )(xo, xc, decay, resid, plane)
    sent = call(
        functools.partial(line_kernel, length),
        [vmem] * (2 + PLANE + depth),
        [vmem] * PLANE,
        [shaped((flat // 2 + modes, lanes), BF16)] * PLANE,
        [pltpu.VMEM((2 * modes, lanes), F32)],
        10**7,
        10**6,
    )(rates, taps, *near, *line)
    back = [sent[0]]
    for i in range(1, PLANE):
        back.append(swap(sent[i], i))

    total = sum(b[flat // 2 :].astype(F32) for b in back)
    bit = 1
    while bit < tp:
        total = total + lax.ppermute(total, "tp", [(i, i ^ bit) for i in range(tp)])
        bit *= 2

    outs = ()
    for indices in ((0,), (PLANE - 1,), tuple(range(1, PLANE - 1))):
        slots = len(indices)
        outs = call(
            functools.partial(outputs_kernel, indices),
            [vmem] * (5 + slots) + [anywhere] * len(outs),
            [anywhere] * 3,
            [shaped((rows, groups, length), BF16)] * 3,
            [
                pltpu.VMEM((3, slots, rows, part, length), BF16),
                pltpu.SemaphoreType.DMA((3, slots)),
                pltpu.VMEM((slots, part // 8, rows * 8, length), F32),
                pltpu.VMEM((slots, part // 8, rows * 8, length), F32),
            ],
            2 * 10**8 * slots,
            10**6 * slots,
            {5 + slots + i: i for i in range(len(outs))},
        )(key, value, grad, near_part, taps, *(back[i] for i in indices), *outs)
    tokens = count * length
    plain, moment = total[:, :groups], total[:, lanes // 2 : lanes // 2 + groups]
    return (
        *(x.reshape(chans, length) for x in outs),
        (plain / tokens).T,
        (-(resid * decay) * moment / tokens).T,
    )


def solution(mesh):
    in_specs = (P("tp", "ctx"), P("tp", "ctx"), P("tp", "ctx"), P("tp", "ctx"), P(), P())
    out_specs = (P("tp", "ctx"), P("tp", "ctx"), P("tp", "ctx"), P(), P())
    return jax.shard_map(
        gradients, mesh=mesh, in_specs=in_specs, out_specs=out_specs, check_vma=False
    )
```
